32 devices in a mesh: fsdp: 2 (over core), ctx: 4 (over y, x), tp: 4 (over z).
Axes of the slice: x: 2, y: 2, z: 4, core: 2. Of those that a mesh axis runs over, the one named last changes fastest.
Arguments:
- layer_input: float32 [4, 1024, 512], P('fsdp', 'ctx'), may hold values from -6 to 6
- timesteps: int32 [4], P('fsdp'), may hold values from 0 to 999
- segment_ids: int32 [4, 1024], P('fsdp'), may hold values from 0 to 15, never falling along the last dimension, each value on 1 to 512 neighbouring positions
- time_table: float32 [1000, 512], replicated, may hold values from -3 to 3
- ln1_gain: float32 [512], replicated, may hold values from 0.5 to 1.5
- ln1_bias: float32 [512], replicated, may hold values from -1.5 to 1.5
- w_qkv: float32 [3, 512, 512], P(None, 'fsdp', 'tp'), may hold values from -0.25 to 0.25
- b_qv: float32 [2, 512], P(None, 'tp'), may hold values from -1.5 to 1.5
- w_out_t: float32 [512, 512], P('fsdp', 'tp'), may hold values from -1 to 1
- b_out: float32 [512], replicated, may hold values from -1.5 to 1.5
- ln2_gain: float32 [512], replicated, may hold values from 0.5 to 1.5
- ln2_bias: float32 [512], replicated, may hold values from -1.5 to 1.5
- w_up: float32 [512, 2048], P('fsdp', 'tp'), may hold values from -0.25 to 0.25
- b_up: float32 [2048], P('tp'), may hold values from -1.5 to 1.5
- w_down_t: float32 [512, 2048], P('fsdp', 'tp'), may hold values from -0.125 to 0.125
- b_down: float32 [512], replicated, may hold values from -1.5 to 1.5
- out_grad: float32 [4, 1024, 512], P('fsdp', 'ctx'), may hold values from -6 to 6
Outputs:
- output: float32 [4, 1024, 512], P('fsdp', 'ctx')
- grad_input: float32 [4, 1024, 512], P('fsdp', 'ctx')
- grad_table: float32 [1000, 512], replicated
- grad_ln1_gain: float32 [512], replicated
- grad_ln1_bias: float32 [512], replicated
- grad_w_qkv: float32 [3, 512, 512], P(None, 'fsdp', 'tp')
- grad_b_qv: float32 [2, 512], P(None, 'tp')
- grad_w_out_t: float32 [512, 512], P('fsdp', 'tp')
- grad_b_out: float32 [512], replicated
- grad_ln2_gain: float32 [512], replicated
- grad_ln2_bias: float32 [512], replicated
- grad_w_up: float32 [512, 2048], P('fsdp', 'tp')
- grad_b_up: float32 [2048], P('tp')
- grad_w_down_t: float32 [512, 2048], P('fsdp', 'tp')
- grad_b_down: float32 [512], replicated
The draws below stay inside these ranges and needn't reach their ends.
Inputs may be any that keep to these rules, and one draw needn't show every extreme that they name: `segment_ids`: in each sequence the ids never fall; each document has 1 to 512 characters and one has exactly 512.
All inputs are finite; a program needn't handle non-finite values.
Results may differ from the reference program's by a relative error of at most 0.011.
Values may be sent and summed in bfloat16 or wider, within the bound.
No kernel may reach another device: no remote copies, remote signals or barrier semaphores. Data moves between devices by JAX's collectives and lax.ppermute only.
A program may use at most 64 MiB of HBM per device.

```python
import math
import jax
import jax.numpy as jnp
import numpy as np
from jax import lax

D = 512
HEADS = 8
HEAD_DIM = 64
FF = 2048
STEPS = 1000
LEN = 1024
DOCS = 16
SEG_MOST = 512
SEQS = 4


def place_ends(values, own_key, least, top_value):
    dims = values.shape
    spot = [jax.random.randint(jax.random.fold_in(own_key, axis), (), 0, dims[axis]) for axis in range(len(dims))]
    values = values.at[tuple(spot)].set(least)
    longest = dims.index(max(dims))
    spot[longest] = (spot[longest] + 1) % dims[longest]
    return values.at[tuple(spot)].set(top_value)


def level_of(key, dims, pieces, low, largest):
    def one(axis_at, blocks):
        heights = jax.random.uniform(jax.random.fold_in(jax.random.fold_in(key, 6), axis_at), (blocks,), jnp.float32, low / len(pieces), largest / len(pieces))
        return jnp.repeat(jnp.exp(heights), dims[axis_at] // blocks).reshape((-1,) + (1,) * (len(dims) - axis_at - 1))

    factor_of = one(*pieces[0])
    for cut in pieces[1:]:
        factor_of = factor_of * one(*cut)
    return factor_of


def split_up(amount, total, most, lean):
    weights = [(1 << 20) // math.isqrt(rank ** lean) + 1 for rank in range(2, amount + 1)]
    surplus, given = total - most - (amount - 1), [1] * (amount - 1)
    while surplus > 0:
        free = [i for i in range(amount - 1) if given[i] < most]
        mass, budget = sum([weights[i] for i in free]), surplus
        for i in free:
            extra = min(most - given[i], max(1, budget * weights[i] // mass), surplus)
            given[i] = given[i] + extra
            surplus = surplus - extra
    return np.array([most] + given)


def ragged_sizes(key, count, total, most, skew):
    if count == 2:
        one = jax.random.randint(key, (), max(1, total - most), min(most, total - 1) + 1)
        return jnp.stack([one, total - one])
    sizes = jnp.asarray(split_up(count, total, most, skew), jnp.int32)
    couples = (count - 1) // 2
    donor, receiver = sizes[1:1 + 2 * couples:2], sizes[2:2 + 2 * couples:2]
    margin = jnp.minimum(donor - 1, most - receiver)
    shifted = jax.random.randint(jax.random.fold_in(key, 1), (couples,), 0, 1 << 20) % (margin + 1)
    sizes = sizes.at[1:1 + 2 * couples:2].set(donor - shifted).at[2:2 + 2 * couples:2].set(receiver + shifted)
    return sizes[jax.random.permutation(jax.random.fold_in(key, 2), count)]


def gaussian(key, shape, width, limit, pieces=(), dtype=jnp.bfloat16):
    array = jax.random.normal(key, shape, jnp.float32) * width
    if len(pieces) > 0:
        array = level_of(key, shape, pieces, -0.22, 0.18) * array
    return jnp.clip(array, min=-limit, max=limit).astype(dtype)


def setup_inputs(seed: int = 0) -> dict:
    streams_of = jax.random.split(jax.random.key(seed), 18)
    return {
        "layer_input": gaussian(streams_of[0], (SEQS, LEN, D), 1.0, 6.0, ((0, 2), (1, 4)), jnp.float32),
        "timesteps": place_ends(jax.random.randint(streams_of[1], (SEQS,), 0, STEPS), jax.random.fold_in(streams_of[1], 1), 0, STEPS - 1).astype(jnp.int32),
        "segment_ids": jax.vmap(lambda own: jnp.searchsorted(jnp.cumsum(ragged_sizes(own, DOCS, LEN, SEG_MOST, 2)), jnp.arange(LEN), side="right"))(jax.random.split(streams_of[2], SEQS)).reshape((SEQS, LEN)).astype(jnp.int32),
        "time_table": gaussian(streams_of[3], (STEPS, D), 0.5, 3.0, (), jnp.float32),
        "ln1_gain": jnp.clip(1.0 + 0.1 * jax.random.normal(streams_of[4], (D,), jnp.float32), 0.5, 1.5),
        "ln1_bias": gaussian(streams_of[5], (D,), 0.3, 1.5, (), jnp.float32),
        "w_qkv": gaussian(streams_of[6], (3, D, D), D ** -0.5, 0.25, ((1, 2), (2, 4)), jnp.float32),
        "b_qv": gaussian(streams_of[7], (2, D), 0.3, 1.5, ((1, 4),), jnp.float32),
        "w_out_t": gaussian(streams_of[8], (D, D), (D // 16) ** -0.5, 1.0, ((0, 2), (1, 4)), jnp.float32),
        "b_out": gaussian(streams_of[9], (D,), 0.3, 1.5, (), jnp.float32),
        "ln2_gain": jnp.clip(1.0 + 0.1 * jax.random.normal(streams_of[10], (D,), jnp.float32), 0.5, 1.5),
        "ln2_bias": gaussian(streams_of[11], (D,), 0.3, 1.5, (), jnp.float32),
        "w_up": gaussian(streams_of[12], (D, FF), D ** -0.5, 0.25, ((0, 2), (1, 4)), jnp.float32),
        "b_up": gaussian(streams_of[13], (FF,), 0.3, 1.5, ((0, 4),), jnp.float32),
        "w_down_t": gaussian(streams_of[14], (D, FF), FF ** -0.5, 0.125, ((0, 2), (1, 4)), jnp.float32),
        "b_down": gaussian(streams_of[15], (D,), 0.3, 1.5, (), jnp.float32),
        "out_grad": gaussian(streams_of[16], (SEQS, LEN, D), 1.0, 6.0, ((0, 2), (1, 4)), jnp.float32),
    }


EPSILON = 1e-05
NEGATIVE = -1e+30
PRECISE = lax.Precision.HIGHEST

@jax.custom_vjp
def low(v):
    return lax.optimization_barrier(v.astype(jnp.bfloat16)).astype(jnp.float32)

@jax.custom_vjp
def low_back(v):
    return v

def low_keep(v):
    return (low(v), None)

def low_pass(kept, grad):
    return (grad,)

def back_keep(v):
    return (v, None)

def back_low(kept, grad):
    return (low(grad),)
low.defvjp(low_keep, low_pass)
low_back.defvjp(back_keep, back_low)

def layer_norm(values, norm_gain, norm_bias):
    centre = values - lax.optimization_barrier(jnp.mean(values, axis=-1, keepdims=True))
    spread = lax.optimization_barrier(jnp.mean(centre * centre, axis=-1, keepdims=True))
    return centre * lax.rsqrt(spread + EPSILON) * norm_gain + norm_bias

def attend(block):
    queries, keys_all, values_all, doc_ids = block
    length = queries.shape[0]
    query_heads = queries.reshape(length, HEADS, HEAD_DIM)
    key_heads = keys_all.reshape(length, HEADS, HEAD_DIM)
    value_heads = values_all.reshape(length, HEADS, HEAD_DIM)
    raw_scores = low_back(jnp.einsum('qhd,khd->hqk', query_heads, key_heads, precision=PRECISE))
    same_doc = doc_ids[:, None] == doc_ids[None, :]
    scores = jnp.where(same_doc[None], raw_scores * HEAD_DIM ** (-0.5), NEGATIVE)
    weights = low(jax.nn.softmax(scores, axis=-1))
    mixed = jnp.einsum('hqk,khd->qhd', weights, value_heads, precision=PRECISE)
    return mixed.reshape(length, HEADS * HEAD_DIM)

def reference(layer_input, timesteps, segment_ids, time_table, ln1_gain, ln1_bias, w_qkv, b_qv, w_out_t, b_out, ln2_gain, ln2_bias, w_up, b_up, w_down_t, b_down, out_grad):

    def forward(inputs, table, gain_one, bias_one, qkv_master, qkv_bias, out_master, out_bias, gain_two, bias_two, up_master, up_bias, down_master, down_bias):
        seq_total = inputs.shape[0]
        embedded = table[timesteps]
        stream = (inputs + embedded[:, None, :]).reshape(seq_total * LEN, D)
        normed = low(layer_norm(stream, gain_one, bias_one))
        qkv_low = low(qkv_master)
        queries = low(low_back(jnp.dot(normed, qkv_low[0], precision=PRECISE)) + qkv_bias[0])
        keys_proj = low(low_back(jnp.dot(normed, qkv_low[1], precision=PRECISE)))
        values_proj = low(low_back(jnp.dot(normed, qkv_low[2], precision=PRECISE)) + qkv_bias[1])
        mixed = lax.map(jax.checkpoint(attend), (queries.reshape(seq_total, LEN, D), keys_proj.reshape(seq_total, LEN, D), values_proj.reshape(seq_total, LEN, D), segment_ids))
        mixed = low(low_back(mixed.reshape(seq_total * LEN, D)))
        resid = stream + low_back(jnp.dot(mixed, low(out_master).T, precision=PRECISE)) + out_bias
        normed_two = low(layer_norm(resid, gain_two, bias_two))
        pre_act = low_back(jnp.dot(normed_two, low(up_master), precision=PRECISE)) + up_bias
        activ = low(jax.nn.gelu(pre_act))
        result = resid + low_back(jnp.dot(activ, low(down_master).T, precision=PRECISE)) + down_bias
        return result.reshape(seq_total, LEN, D)
    output, pull = jax.vjp(forward, layer_input, time_table, ln1_gain, ln1_bias, w_qkv, b_qv, w_out_t, b_out, ln2_gain, ln2_bias, w_up, b_up, w_down_t, b_down)
    grad_input, grad_table, grad_ln1_gain, grad_ln1_bias, grad_w_qkv, grad_b_qv, grad_w_out_t, grad_b_out, grad_ln2_gain, grad_ln2_bias, grad_w_up, grad_b_up, grad_w_down_t, grad_b_down = pull(out_grad)
    return (output, grad_input, grad_table, grad_ln1_gain, grad_ln1_bias, grad_w_qkv, grad_b_qv, grad_w_out_t, grad_b_out, grad_ln2_gain, grad_ln2_bias, grad_w_up, grad_b_up, grad_w_down_t, grad_b_down)
```

```python
import functools
import jax
import jax.numpy as jnp
from jax import lax
from jax.experimental import pallas as pl
from jax.experimental.pallas import tpu as pltpu
from jax.sharding import PartitionSpec as P

HEAD_DIM = 64
SCALE = HEAD_DIM ** (-0.5)
EPSILON = 1e-05
NEGATIVE = -1e30
F32 = jnp.float32
BF16 = jnp.bfloat16


def xor_pairs(size, bits):
    return [(i, i ^ bits) for i in range(size)]


def dot_nn(left, right):
    return lax.dot_general(left, right, (((1,), (0,)), ((), ())), preferred_element_type=F32)


def dot_nt(left, right):
    return lax.dot_general(left, right, (((1,), (1,)), ((), ())), preferred_element_type=F32)


def dot_tn(left, right):
    return lax.dot_general(left, right, (((0,), (0,)), ((), ())), preferred_element_type=F32)


def norm_parts(values):
    centre = values - jnp.mean(values, axis=-1, keepdims=True)
    spread = jnp.mean(centre * centre, axis=-1, keepdims=True)
    inverse = lax.rsqrt(spread + EPSILON)
    return centre * inverse, inverse


def norm_back(grad, hat, inverse, gain):
    scaled = grad * gain
    mean_one = jnp.mean(scaled, axis=-1, keepdims=True)
    mean_two = jnp.mean(scaled * hat, axis=-1, keepdims=True)
    return inverse * (scaled - mean_one - hat * mean_two)


def mask_biases(where_ref, seg_ref, span):
    chunk = where_ref[0]
    count = seg_ref.shape[1] // span

    def ids_of(step):
        start = pl.multiple_of((chunk ^ step) * span, span)
        return seg_ref[:, pl.ds(start, span)]

    own = jnp.broadcast_to(ids_of(0), (span, span)).T
    return [
        jnp.where(own == jnp.broadcast_to(ids_of(step), (span, span)), 0.0, NEGATIVE)
        for step in range(count)
    ]


def lane_mask(shape, head):
    lanes = lax.broadcasted_iota(jnp.int32, shape, 1)
    return (lanes // HEAD_DIM) == head


def attend_forward_kernel(where_ref, seg_ref, q_ref, kv0, kv1, kv2, kv3, mixed_ref, lse_ref):
    span, width = q_ref.shape
    biases = mask_biases(where_ref, seg_ref, span)
    kvs = (kv0, kv1, kv2, kv3)
    query = q_ref[...]
    mixed, lse = None, None
    for head in range(width // HEAD_DIM):
        mine = lane_mask((span, width), head)
        masked = jnp.where(mine, query, jnp.zeros_like(query))
        scores = [
            dot_nt(masked, kv[:, :width]) * SCALE + bias for kv, bias in zip(kvs, biases)
        ]
        top = functools.reduce(
            jnp.maximum, [jnp.max(block, axis=-1, keepdims=True) for block in scores]
        )
        grown = [jnp.exp(block - top) for block in scores]
        total = functools.reduce(
            jnp.add, [jnp.sum(block, axis=-1, keepdims=True) for block in grown]
        )
        share = 1.0 / total
        out = functools.reduce(
            jnp.add,
            [dot_nn((block * share).astype(BF16), kv[:, width:]) for block, kv in zip(grown, kvs)],
        )
        log_total = jnp.broadcast_to(top + jnp.log(total), (span, width))
        mixed = out if head == 0 else jnp.where(mine, out, mixed)
        lse = log_total if head == 0 else jnp.where(mine, log_total, lse)
    mixed_ref[...] = mixed.astype(BF16)
    lse_ref[...] = lse


def attend_backward_kernel(
    where_ref, seg_ref, q_ref, g_ref, lse_ref, kv0, kv1, kv2, kv3,
    dq_ref, own_ref, out1, out2, out3,
):
    span, width = q_ref.shape
    biases = mask_biases(where_ref, seg_ref, span)
    kvs = (kv0, kv1, kv2, kv3)
    outs = (own_ref, out1, out2, out3)
    query, grad = q_ref[...], g_ref[...]
    dq, dks, dvs = None, [None] * 4, [None] * 4
    for head in range(width // HEAD_DIM):
        mine = lane_mask((span, width), head)
        masked_q = jnp.where(mine, query, jnp.zeros_like(query))
        masked_g = jnp.where(mine, grad, jnp.zeros_like(grad))
        lse = lse_ref[:, head * HEAD_DIM : head * HEAD_DIM + 1]
        probs = [
            jnp.exp(dot_nt(masked_q, kv[:, :width]) * SCALE + bias - lse)
            for kv, bias in zip(kvs, biases)
        ]
        grads = [dot_nt(masked_g, kv[:, width:]) for kv in kvs]
        inner = functools.reduce(
            jnp.add,
            [jnp.sum(p * g, axis=-1, keepdims=True) for p, g in zip(probs, grads)],
        )
        raws = [(p * (g - inner) * SCALE).astype(BF16) for p, g in zip(probs, grads)]
        head_dq = functools.reduce(
            jnp.add, [dot_nn(raw, kv[:, :width]) for raw, kv in zip(raws, kvs)]
        )
        dq = head_dq if head == 0 else jnp.where(mine, head_dq, dq)
        for step in range(4):
            head_dk = dot_tn(raws[step], query)
            head_dv = dot_tn(probs[step].astype(BF16), grad)
            dks[step] = head_dk if head == 0 else jnp.where(mine, head_dk, dks[step])
            dvs[step] = head_dv if head == 0 else jnp.where(mine, head_dv, dvs[step])
    dq_ref[...] = dq
    for step in range(4):
        outs[step][:, :width] = dks[step].astype(outs[step].dtype)
        outs[step][:, width:] = dvs[step].astype(outs[step].dtype)


def vmem_specs(count):
    return [pl.BlockSpec(memory_space=pltpu.VMEM)] * count


def attend_forward(where, seg, query, kvs):
    span, width = query.shape
    return pl.pallas_call(
        attend_forward_kernel,
        out_shape=(
            jax.ShapeDtypeStruct((span, width), BF16),
            jax.ShapeDtypeStruct((span, width), F32),
        ),
        in_specs=[pl.BlockSpec(memory_space=pltpu.SMEM)] + vmem_specs(6),
        out_specs=tuple(vmem_specs(2)),
        compiler_params=pltpu.CompilerParams(vmem_limit_bytes=40 << 20),
        cost_estimate=pl.CostEstimate(
            flops=4 * 2 * 4 * span * span * width, bytes_accessed=2 << 20, transcendentals=8 * span * span
        ),
    )(where, seg, query, *kvs)


def attend_backward(where, seg, query, grad, lse, kvs):
    span, width = query.shape
    return pl.pallas_call(
        attend_backward_kernel,
        out_shape=(
            jax.ShapeDtypeStruct((span, width), F32),
            jax.ShapeDtypeStruct((span, 2 * width), F32),
        )
        + (jax.ShapeDtypeStruct((span, 2 * width), BF16),) * 3,
        in_specs=[pl.BlockSpec(memory_space=pltpu.SMEM)] + vmem_specs(8),
        out_specs=tuple(vmem_specs(5)),
        compiler_params=pltpu.CompilerParams(vmem_limit_bytes=40 << 20),
        cost_estimate=pl.CostEstimate(
            flops=10 * 2 * 4 * span * span * width, bytes_accessed=3 << 20, transcendentals=8 * span * span
        ),
    )(where, seg, query, grad, lse, *kvs)


def swap(values, axis, size, bits):
    return lax.ppermute(values, axis, xor_pairs(size, bits))


def gather_rows(part, parts, place):
    if parts != 2:
        return lax.all_gather(part, "fsdp", axis=0, tiled=True)
    other = swap(part, "fsdp", 2, 1)
    return jnp.where(
        place == 0, jnp.concatenate([part, other]), jnp.concatenate([other, part])
    )


def scatter_rows(whole, parts, place):
    if parts != 2:
        return lax.psum_scatter(whole, "fsdp", scatter_dimension=0, tiled=True)
    rows = whole.shape[0] // 2
    given = lax.dynamic_slice_in_dim(whole, (1 - place) * rows, rows, 0).astype(BF16)
    kept = lax.dynamic_slice_in_dim(whole, place * rows, rows, 0)
    return kept + swap(given, "fsdp", 2, 1).astype(F32)


def sum_four(values, axis):
    got = [swap(values, axis, 4, bits) for bits in (1, 2, 3)]
    return (values + got[0]) + (got[1] + got[2])


def scatter_four(values, axis, place):
    rows = values.shape[0] // 4

    def quarter(bits):
        return lax.dynamic_slice_in_dim(values, (place ^ bits) * rows, rows, 0)

    got = [swap(quarter(bits).astype(BF16), axis, 4, bits).astype(F32) for bits in (1, 2, 3)]
    return (quarter(0) + got[0]) + (got[1] + got[2])


def gather_four(part, axis, place):
    pieces = [part] + [swap(part, axis, 4, bits) for bits in (1, 2, 3)]
    out = []
    for spot in range(4):
        bits = place ^ spot
        low = jnp.where(bits == 0, pieces[0], pieces[1])
        high = jnp.where(bits == 2, pieces[2], pieces[3])
        out.append(jnp.where(bits < 2, low, high))
    return jnp.concatenate(out)


def per_device(
    layer_input,
    timesteps,
    segment_ids,
    time_table,
    ln1_gain,
    ln1_bias,
    w_qkv,
    b_qv,
    w_out_t,
    b_out,
    ln2_gain,
    ln2_bias,
    w_up,
    b_up,
    w_down_t,
    b_down,
    out_grad,
    *,
    parts,
):
    span, model_width = layer_input.shape[1:]
    step_count = time_table.shape[0]
    cols = w_qkv.shape[2]
    hidden = w_up.shape[1]
    half = span // 2
    core = lax.axis_index("fsdp")
    chunk = lax.axis_index("ctx")
    shard = lax.axis_index("tp")
    pair, bit = shard // 2, shard % 2

    qkv_part = jnp.concatenate([w_qkv[0], w_qkv[1], w_qkv[2]], axis=1).astype(BF16)
    rest_part = jnp.concatenate([w_out_t, w_up, w_down_t], axis=1).astype(BF16)
    bias_part = jnp.concatenate([b_qv[0], b_qv[1], b_up])[None]
    qkv_own = gather_rows(qkv_part, parts, core)
    bias_other = swap(bias_part, "tp", 4, 2)
    qkv_other = gather_rows(swap(qkv_part, "tp", 4, 2), parts, core)
    rest_far = swap(rest_part, "tp", 4, 2)
    rest_both = gather_rows(jnp.concatenate([rest_part, rest_far], axis=1), parts, core)
    rest = cols + 2 * hidden
    out_mat = jnp.concatenate([rest_both[:, :cols], rest_both[:, rest : rest + cols]], axis=1)
    up_mat = jnp.concatenate(
        [rest_both[:, cols : cols + hidden], rest_both[:, rest + cols : rest + cols + hidden]],
        axis=1,
    )
    down_mat = jnp.concatenate(
        [rest_both[:, cols + hidden : rest], rest_both[:, rest + cols + hidden :]], axis=1
    )
    up_bias = jnp.concatenate([b_up, bias_other[0, 2 * cols :]])

    def of_pair(values):
        return lax.dynamic_index_in_dim(values, pair, 0, keepdims=False)

    step_at = of_pair(timesteps)
    embedded = lax.dynamic_slice(time_table, (step_at, 0), (1, model_width))
    stream = of_pair(layer_input) + embedded
    seg = of_pair(segment_ids)[None]
    cotan = of_pair(out_grad)
    where = chunk.astype(jnp.int32).reshape(1)

    hat_one, inverse_one = norm_parts(stream)
    normed = (hat_one * ln1_gain + ln1_bias).astype(BF16)

    def project(weights, q_bias, v_bias):
        raw = dot_nn(normed, weights)
        query = (raw[:, :cols] + q_bias).astype(BF16)
        value = (raw[:, 2 * cols :] + v_bias).astype(BF16)
        return query, jnp.concatenate([raw[:, cols : 2 * cols].astype(BF16), value], axis=1)

    def spread_kv(kv):
        return [kv] + [swap(kv, "ctx", 4, bits) for bits in (1, 2, 3)]

    query_own, kv_own = project(qkv_own, b_qv[0], b_qv[1])
    kvs_own = spread_kv(kv_own)
    query_other, kv_other = project(
        qkv_other, bias_other[0, :cols], bias_other[0, cols : 2 * cols]
    )
    kvs_other = spread_kv(kv_other)
    mixed_own, lse_own = attend_forward(where, seg, query_own, kvs_own)
    mixed_other, lse_other = attend_forward(where, seg, query_other, kvs_other)
    mixed = jnp.concatenate([mixed_own, mixed_other], axis=1)

    attn_terms = dot_nt(mixed, out_mat)
    resid = stream + (attn_terms + swap(attn_terms.astype(BF16), "tp", 4, 1).astype(F32)) + b_out
    hat_two, inverse_two = norm_parts(resid)
    normed_two = (hat_two * ln2_gain + ln2_bias).astype(BF16)
    pre_act = dot_nn(normed_two, up_mat) + up_bias
    activ, gelu_pull = jax.vjp(jax.nn.gelu, pre_act)
    activ_low = activ.astype(BF16)
    cotan_low = cotan.astype(BF16)
    (grad_pre,) = gelu_pull(dot_nn(cotan_low, down_mat))
    grad_pre_low = grad_pre.astype(BF16)
    back_two = dot_nt(grad_pre_low, up_mat)
    ffn_terms = dot_nt(activ_low, down_mat)

    def half_of(values, which):
        return lax.dynamic_slice_in_dim(values, which * half, half, 0)

    def scatter_pair(values):
        got = swap(half_of(values, 1 - bit).astype(BF16), "tp", 4, 1)
        return half_of(values, bit) + got.astype(F32)

    norm_grad = scatter_pair(back_two)
    hat_half, inverse_half = half_of(hat_two, bit), half_of(inverse_two, bit)
    cotan_half = half_of(cotan, bit)
    grad_resid = cotan_half + norm_back(norm_grad, hat_half, inverse_half, ln2_gain)
    resid_low = grad_resid.astype(BF16)
    resid_far = swap(resid_low, "tp", 4, 1)
    resid_all = jnp.where(
        bit == 0,
        jnp.concatenate([resid_low, resid_far]),
        jnp.concatenate([resid_far, resid_low]),
    )
    grad_mixed = dot_nn(resid_all, out_mat).astype(BF16)

    out_half = half_of(resid, bit) + scatter_pair(ffn_terms) + b_down
    output = gather_four(out_half.astype(BF16), "tp", shard).astype(F32)

    def reduce_weights(terms):
        mine = scatter_rows(terms, parts, core)
        quarter = scatter_four(mine, "ctx", chunk)
        width = quarter.shape[1] // 2
        summed = quarter[:, :width] + swap(quarter[:, width:].astype(BF16), "tp", 4, 2).astype(F32)
        return gather_four(summed.astype(BF16), "ctx", chunk).astype(F32)

    grad_up = dot_tn(normed_two, grad_pre_low)
    grad_down = dot_tn(cotan_low, activ_low)
    grad_out = dot_tn(resid_all, mixed)
    rest_terms = jnp.concatenate(
        [
            grad_out[:, :cols],
            grad_up[:, :hidden],
            grad_down[:, :hidden],
            grad_out[:, cols:],
            grad_up[:, hidden:],
            grad_down[:, hidden:],
        ],
        axis=1,
    )
    rest_owned = reduce_weights(rest_terms)

    def attend_pull(query, grad, lse, kvs):
        dq, kept, *given = attend_backward(where, seg, query, grad, lse, kvs)
        got = [swap(piece, "ctx", 4, bits + 1).astype(F32) for bits, piece in enumerate(given)]
        grad_kv = (kept + got[0]) + (got[1] + got[2])
        sums = jnp.stack([jnp.sum(dq, axis=0), jnp.sum(grad_kv[:, cols:], axis=0)])
        return jnp.concatenate([dq, grad_kv], axis=1).astype(BF16), sums

    pulled_own, qv_own = attend_pull(query_own, grad_mixed[:, :cols], lse_own, kvs_own)
    pulled_other, qv_other = attend_pull(query_other, grad_mixed[:, cols:], lse_other, kvs_other)

    back_one = dot_nt(pulled_own, qkv_own) + dot_nt(pulled_other, qkv_other)
    gain_one = jnp.sum(back_one * hat_one, axis=0)
    bias_one = jnp.sum(back_one, axis=0)
    stream_terms = norm_back(back_one, hat_one, inverse_one, ln1_gain)
    sequence_sum = jnp.sum(stream_terms, axis=0) + jnp.sum(grad_resid, axis=0)
    input_half = grad_resid + scatter_pair(stream_terms)
    grad_input = gather_four(input_half.astype(BF16), "tp", shard).astype(F32)

    qkv_terms = jnp.concatenate(
        [dot_tn(normed, pulled_own), dot_tn(normed, pulled_other)], axis=1
    )
    qkv_owned = reduce_weights(qkv_terms)

    seqs = 2 * parts
    place = 2 * core + pair
    rows = lambda *values: jnp.stack(values)
    fixed = rows(
        gain_one,
        bias_one,
        jnp.sum(norm_grad * hat_half, axis=0),
        jnp.sum(norm_grad, axis=0),
        jnp.sum(grad_resid, axis=0),
        jnp.sum(cotan_half, axis=0),
    )
    seq_hot = (jnp.arange(seqs) == place).astype(F32)
    seq_rows = seq_hot[:, None] * sequence_sum[None]
    first = jnp.logical_and(chunk == 0, bit == 0).astype(F32)
    step_row = jnp.pad(seq_hot * step_at.astype(F32) * first, (0, model_width - seqs))[None]
    four = jnp.arange(4)[:, None]
    near, far = (four == shard).astype(F32), (four == shard ^ 2).astype(F32)
    up_sum = jnp.sum(grad_pre, axis=0)
    up_rows = near * up_sum[None, :hidden] + far * up_sum[None, hidden:]
    qv_rows = (near[None] * qv_own[:, None] + far[None] * qv_other[:, None]).reshape(
        2, 4 * cols
    )
    small = jnp.concatenate([fixed, seq_rows, step_row, up_rows, qv_rows])
    small = small + swap(small, "fsdp", 2, 1) if parts == 2 else lax.psum(small, "fsdp")
    small = sum_four(sum_four(small, "ctx"), "tp")
    seq_sums = small[6 : 6 + seqs]
    steps = small[6 + seqs, :seqs].astype(jnp.int32)
    hot = (jnp.arange(step_count, dtype=jnp.int32)[:, None] == steps[None]).astype(F32)
    grad_table = jnp.dot(hot, seq_sums, precision=lax.Precision.HIGHEST)
    up_at, qv_at = 7 + seqs, 11 + seqs
    grad_b_up = lax.dynamic_index_in_dim(small[up_at : up_at + 4], shard, 0, keepdims=False)
    grad_b_qv = lax.dynamic_slice_in_dim(small[qv_at : qv_at + 2], shard * cols, cols, 1)

    shape = layer_input.shape
    return (
        output.reshape(shape),
        grad_input.reshape(shape),
        grad_table,
        small[0],
        small[1],
        jnp.stack([qkv_owned[:, i * cols : (i + 1) * cols] for i in range(3)]),
        grad_b_qv,
        rest_owned[:, :cols],
        small[4],
        small[2],
        small[3],
        rest_owned[:, cols : cols + hidden],
        grad_b_up,
        rest_owned[:, cols + hidden :],
        small[5],
    )


def solution(mesh):
    placed = (
        P("fsdp", "ctx", None),
        P("fsdp"),
        P("fsdp", None),
        P(),
        P(),
        P(),
        P(None, "fsdp", "tp"),
        P(None, "tp"),
        P("fsdp", "tp"),
        P(),
        P(),
        P(),
        P("fsdp", "tp"),
        P("tp"),
        P("fsdp", "tp"),
        P(),
        P("fsdp", "ctx", None),
    )
    return jax.shard_map(
        functools.partial(per_device, parts=mesh.shape["fsdp"]),
        mesh=mesh,
        in_specs=placed,
        out_specs=(
            P("fsdp", "ctx", None),
            P("fsdp", "ctx", None),
            P(),
            P(),
            P(),
            P(None, "fsdp", "tp"),
            P(None, "tp"),
            P("fsdp", "tp"),
            P(),
            P(),
            P(),
            P("fsdp", "tp"),
            P("tp"),
            P("fsdp", "tp"),
            P(),
        ),
        check_vma=False,
    )
```

```python
import functools
import jax
import jax.numpy as jnp
from jax import lax
from jax.experimental import pallas as pl
from jax.experimental.pallas import tpu as pltpu
from jax.sharding import PartitionSpec as P

HEAD_DIM = 64
SCALE = HEAD_DIM ** (-0.5)
EPSILON = 1e-05
NEGATIVE = -1e30
F32 = jnp.float32
BF16 = jnp.bfloat16
BIAS_ROWS = 16
CUBE = 0.044715
ROOT = 0.7978845608028654
COST = 20_000_000_000
VMEM = pl.BlockSpec(memory_space=pltpu.VMEM)
SMEM = pl.BlockSpec(memory_space=pltpu.SMEM)


def dot_nn(left, right):
    return lax.dot_general(left, right, (((1,), (0,)), ((), ())), preferred_element_type=F32)


def dot_nt(left, right):
    return lax.dot_general(left, right, (((1,), (1,)), ((), ())), preferred_element_type=F32)


def dot_tn(left, right):
    return lax.dot_general(left, right, (((0,), (0,)), ((), ())), preferred_element_type=F32)


def total(values):
    return functools.reduce(jnp.add, values)


def norm_parts(values):
    centre = values - jnp.mean(values, axis=-1, keepdims=True)
    spread = jnp.mean(centre * centre, axis=-1, keepdims=True)
    inverse = lax.rsqrt(spread + EPSILON)
    return centre * inverse, inverse


def norm_back(grad, hat, inverse, gain):
    scaled = grad * gain
    mean_one = jnp.mean(scaled, axis=-1, keepdims=True)
    mean_two = jnp.mean(scaled * hat, axis=-1, keepdims=True)
    return inverse * (scaled - mean_one - hat * mean_two)


def column_sum(values):
    return jnp.sum(values, axis=0, keepdims=True)


def window(index, size):
    return pl.ds(pl.multiple_of(index * size, size), size)


def halves(spot_ref, size):
    return window(spot_ref[0], size), window(1 - spot_ref[0], size)


def hold(*values):
    return lax.optimization_barrier(values)


class Order:
    def __init__(self, spot):
        self.spot = spot

    def call(self, kernel, outs, operands, *, far=(), scratch=(), limit=12):
        scalars = [SMEM if operand.ndim == 1 else None for operand in operands]
        specs = [
            pl.BlockSpec(memory_space=pltpu.HBM) if i in far else scalars[i] or VMEM
            for i in range(len(operands))
        ]
        operands = [
            pltpu.with_memory_space_constraint(operand, pltpu.HBM) if i in far else operand
            for i, operand in enumerate(operands)
        ]
        results = pl.pallas_call(
            kernel,
            out_shape=tuple(jax.ShapeDtypeStruct(shape, dtype) for shape, dtype in outs),
            in_specs=[SMEM] + specs,
            out_specs=(VMEM,) * len(outs),
            scratch_shapes=list(scratch),
            compiler_params=pltpu.CompilerParams(vmem_limit_bytes=limit << 20),
            cost_estimate=pl.CostEstimate(
                flops=COST, bytes_accessed=1 << 16, transcendentals=0
            ),
        )(self.spot, *operands)
        first, self.spot = hold(results[0], self.spot)
        return [first, *results[1:]]

    def swap(self, values, axis, bits):
        values, self.spot = hold(values, self.spot)
        size = 2 if axis == "fsdp" else 4
        with jax.named_scope("swap_%s_%d" % (axis, bits)):
            return lax.ppermute(values, axis, [(i, i ^ bits) for i in range(size)])

    def swap_three(self, values, axis):
        return [self.swap(values, axis, bits) for bits in (1, 2, 3)]

    def swap_turn(self, values, turn):
        values, self.spot = hold(values, self.spot)
        pairs = [
            (4 * core + i, 4 * core + (i ^ (1 + (core + turn) % 2)))
            for core in range(2)
            for i in range(4)
        ]
        with jax.named_scope("swap_turn_%d" % turn):
            return lax.ppermute(values, ("fsdp", "ctx"), pairs)


def fetch(copies, sems):
    started = [
        pltpu.make_async_copy(source, target, sems.at[i])
        for i, (source, target) in enumerate(copies)
    ]
    for copy in started:
        copy.start()
    for copy in started:
        copy.wait()


def split_three(values):
    high = values.astype(BF16)
    rest = values - high.astype(F32)
    middle = rest.astype(BF16)
    return [high, middle, (rest - middle.astype(F32)).astype(BF16)]


def pack_first_kernel(
    spot_ref, steps_ref, w_hbm, out_hbm, qv_hbm, up_hbm, pack_ref, w_ref, o_ref, qv_ref, up_ref,
    sems,
):
    rows, cols = w_ref.shape[1:]
    fetch([(w_hbm, w_ref), (out_hbm, o_ref), (qv_hbm, qv_ref), (up_hbm, up_ref)], sems)
    for i in range(3):
        pack_ref[:rows, i * cols : (i + 1) * cols] = w_ref[i].astype(BF16)
    pack_ref[:rows, 3 * cols :] = o_ref[...].astype(BF16)
    lanes = lax.broadcasted_iota(jnp.int32, (1, cols), 1)
    steps = jnp.zeros((1, cols), F32)
    for i in range(steps_ref.shape[0]):
        steps = jnp.where(lanes == i, steps_ref[i].astype(F32), steps)
    fill = jnp.zeros((1, cols), F32)
    line = jnp.concatenate([qv_ref[0:1], qv_ref[1:2], steps, fill], axis=1)
    parts = split_three(jnp.concatenate([line, up_ref[...]], axis=0))
    fill = jnp.zeros((BIAS_ROWS - 6, 4 * cols), F32)
    stack = jnp.concatenate([v.astype(F32) for v in parts] + [fill], axis=0)
    pack_ref[rows:, :] = stack.astype(BF16)


def bias_lines(pack_ref, row):
    bits = pack_ref[row : row + BIAS_ROWS, :].astype(F32)
    lines = bits[0:2] + bits[2:4] + bits[4:6]
    return lines[0:1], lines[1:2]


def pack_rest_kernel(
    spot_ref, up_hbm, down_hbm, cotan_hbm, pack_ref, half_ref, cotan_ref, up_ref, down_ref, sems
):
    hidden = up_ref.shape[1]
    pair = spot_ref[2] // 2
    fetch([(up_hbm, up_ref), (down_hbm, down_ref), (cotan_hbm.at[pair], cotan_ref)], sems)
    pack_ref[:, :hidden] = up_ref[...].astype(BF16)
    pack_ref[:, hidden:] = down_ref[...].astype(BF16)
    mine = window(spot_ref[1] % 2, half_ref.shape[0])
    half_ref[:, :hidden] = up_ref[mine, :].astype(BF16)
    half_ref[:, hidden:] = down_ref[mine, :].astype(BF16)


def join_kernel(spot_ref, *refs, place, keep):
    pieces, out_ref = refs[:-1], refs[-1]
    rows = pieces[0].shape[0]
    for bits, piece in enumerate(pieces):
        at = window((spot_ref[place] & keep) ^ bits, rows)
        out_ref[at, :] = piece[...].astype(out_ref.dtype)


def join(order, place, pieces, dtype):
    rows, cols = pieces[0].shape
    kernel = functools.partial(join_kernel, place=place, keep=len(pieces) - 1)
    return order.call(kernel, [((rows * len(pieces), cols), dtype)], pieces)[0]


def stream_kernel(
    spot_ref, steps_ref, x_hbm, table_hbm, seg_hbm, g1, b1, g2, b2, bo, bd,
    stream_ref, normed_ref, seg_ref, lines_ref, x_ref, table_ref, ids_ref, line_ref, sems,
):
    pair = spot_ref[2] // 2
    step = steps_ref[pair]
    block = pl.multiple_of(step // 8 * 8, 8)
    copies = [
        (x_hbm.at[pair], x_ref),
        (table_hbm.at[pl.ds(block, 8), :], table_ref),
        (seg_hbm, ids_ref),
    ]
    vectors = (g1, b1, g2, b2, bo, bd)
    fetch(copies + [(v, line_ref.at[i]) for i, v in enumerate(vectors)], sems)
    for i in range(len(vectors)):
        lines_ref[i : i + 1, :] = line_ref[i]
    seg_ref[...] = ids_ref[pl.ds(pair, 1), :]
    stream = x_ref[...] + table_ref[pl.ds(step % 8, 1), :]
    hat, _ = norm_parts(stream)
    stream_ref[...] = stream
    normed_ref[...] = (hat * line_ref[0] + line_ref[1]).astype(BF16)


def project_kernel(spot_ref, normed_ref, one_ref, two_ref, bias_ref, q_ref, kv_ref, *, row):
    cols = q_ref.shape[1]
    size = normed_ref.shape[1] // 2
    one, two = halves(spot_ref, size)
    raw = dot_nn(normed_ref[:, one], one_ref[:size, : 3 * cols])
    raw = raw + dot_nn(normed_ref[:, two], two_ref[:size, : 3 * cols])
    line, _ = bias_lines(bias_ref, row)
    q_bias, v_bias = line[:, :cols], line[:, cols : 2 * cols]
    q_ref[...] = (raw[:, :cols] + q_bias).astype(BF16)
    kv_ref[:, :cols] = raw[:, cols : 2 * cols].astype(BF16)
    kv_ref[:, cols:] = (raw[:, 2 * cols :] + v_bias).astype(BF16)


def mask_biases(spot_ref, seg_ref, span):
    chunk = spot_ref[1]
    ids = [seg_ref[:, window(chunk ^ step, span)] for step in range(seg_ref.shape[1] // span)]
    own = jnp.broadcast_to(ids[0], (span, span)).T
    return [
        jnp.where(own == jnp.broadcast_to(step_ids, (span, span)), 0.0, NEGATIVE)
        for step_ids in ids
    ]


def lane_mask(shape, head):
    return (lax.broadcasted_iota(jnp.int32, shape, 1) // HEAD_DIM) == head


def attend_forward(spot_ref, seg_ref, q_ref, kvs, mixed_ref, lse_ref):
    span, width = q_ref.shape
    biases = mask_biases(spot_ref, seg_ref, span)
    query = q_ref[...]
    mixed, lse = None, None
    for head in range(width // HEAD_DIM):
        mine = lane_mask((span, width), head)
        masked = jnp.where(mine, query, jnp.zeros_like(query))
        scores = [dot_nt(masked, kv[:, :width]) * SCALE + bias for kv, bias in zip(kvs, biases)]
        top = functools.reduce(
            jnp.maximum, [jnp.max(block, axis=-1, keepdims=True) for block in scores]
        )
        grown = [jnp.exp(block - top) for block in scores]
        mass = total([jnp.sum(block, axis=-1, keepdims=True) for block in grown])
        share = 1.0 / mass
        out = total(
            [dot_nn((block * share).astype(BF16), kv[:, width:]) for block, kv in zip(grown, kvs)]
        )
        log_mass = jnp.broadcast_to(top + jnp.log(mass), (span, width))
        mixed = out if head == 0 else jnp.where(mine, out, mixed)
        lse = log_mass if head == 0 else jnp.where(mine, log_mass, lse)
    mixed_ref[...] = mixed.astype(BF16)
    lse_ref[...] = lse


def attend_one_kernel(spot_ref, seg_ref, q_ref, kv0, kv1, kv2, kv3, mixed_ref, lse_ref):
    attend_forward(spot_ref, seg_ref, q_ref, (kv0, kv1, kv2, kv3), mixed_ref, lse_ref)


def attend_two_kernel(
    spot_ref, seg_ref, q_ref, kv0, kv1, kv2, kv3, near_ref, one_n, two_n, one_f, two_f,
    mixed_ref, lse_ref, terms_ref, given_ref,
):
    attend_forward(spot_ref, seg_ref, q_ref, (kv0, kv1, kv2, kv3), mixed_ref, lse_ref)
    size, cols = terms_ref.shape[1] // 2, q_ref.shape[1]
    one, two = halves(spot_ref, size)
    near, far = near_ref[...], mixed_ref[...]
    for columns, near_w, far_w in ((one, one_n, one_f), (two, two_n, two_f)):
        terms = dot_nt(near, near_w[:size, 3 * cols :]) + dot_nt(far, far_w[:size, 3 * cols :])
        terms_ref[:, columns] = terms
        given_ref[:, columns] = terms.astype(BF16)


def gelu_parts(x):
    square = x * x
    curve = jnp.tanh(ROOT * (x + CUBE * (x * square)))
    half = 0.5 * (1.0 + curve)
    slope = half + 0.5 * x * (1.0 - curve * curve) * (ROOT * (1.0 + 3.0 * CUBE * square))
    return x * half, slope


def ffn_kernel(
    spot_ref, stream_ref, terms_ref, got_ref, cotan_ref, lines_ref, near_pack, far_pack,
    one_n, two_n, *refs, row,
):
    count = len(refs) - 14
    pieces, refs = refs[:count], refs[count:]
    if count == 2:
        (one_f, two_f), refs = pieces, refs[:-2]
    else:
        (one_f, two_f), refs = refs[-2:], refs[:-2]
        rows = pieces[0].shape[0]
        for target, mine, other in ((one_f, 0, 1), (two_f, 2, 3)):
            target[window(spot_ref[1] % 2, rows), :] = pieces[mine][...]
            target[window(1 - spot_ref[1] % 2, rows), :] = pieces[other][...]
    ffn_body(
        spot_ref, stream_ref, terms_ref, got_ref, cotan_ref, lines_ref, near_pack, far_pack,
        one_n, two_n, one_f, two_f, *refs, row=row,
    )


def ffn_body(
    spot_ref, stream_ref, terms_ref, got_ref, cotan_ref, lines_ref, near_pack, far_pack,
    one_n, two_n, one_f, two_f,
    back_given, back_kept, ffn_given, out_kept, resid_ref, normed_ref, act_ref, pre_ref, low_ref,
    sum_ref, back_all, resid_all, *, row,
):
    span, width = stream_ref.shape
    hidden = one_n.shape[1] // 2
    half = span // 2
    bit = spot_ref[2] % 2
    one, two = halves(spot_ref, width // 2)
    resid = stream_ref[...] + (terms_ref[...] + got_ref[...].astype(F32)) + lines_ref[4:5, :]
    resid_all[...] = resid
    hat, _ = norm_parts(resid)
    normed_ref[...] = (hat * lines_ref[2:3, :] + lines_ref[3:4, :]).astype(BF16)
    low_ref[...] = cotan_ref[...].astype(BF16)
    biases = [bias_lines(pack, row)[1] for pack in (near_pack, far_pack)]
    back_one = back_two = ffn_one = ffn_two = None
    for side, (first, second) in enumerate(((one_n, two_n), (one_f, two_f))):
        bias = biases[side]
        at = slice(side * hidden, (side + 1) * hidden)
        pre = dot_nn(normed_ref[:, one], first[:, :hidden])
        pre = pre + dot_nn(normed_ref[:, two], second[:, :hidden]) + bias
        value, slope = gelu_parts(pre)
        grad = dot_nn(low_ref[:, one], first[:, hidden:])
        grad = (grad + dot_nn(low_ref[:, two], second[:, hidden:])) * slope
        sum_ref[:, at] = column_sum(grad)
        act_ref[:, at] = value.astype(BF16)
        pre_ref[:, at] = grad.astype(BF16)
        act, pre_low = act_ref[:, at], pre_ref[:, at]
        terms = [
            dot_nt(pre_low, first[:, :hidden]),
            dot_nt(pre_low, second[:, :hidden]),
            dot_nt(act, first[:, hidden:]),
            dot_nt(act, second[:, hidden:]),
        ]
        if side == 0:
            back_one, back_two, ffn_one, ffn_two = terms
    back_all[:, one] = back_one + terms[0]
    back_all[:, two] = back_two + terms[1]
    given, kept = window(1 - bit, half), window(bit, half)
    back_given[...] = back_all[given, :].astype(BF16)
    back_kept[...] = back_all[kept, :]
    back_all[:, one] = ffn_one + terms[2]
    back_all[:, two] = ffn_two + terms[3]
    ffn_given[...] = back_all[given, :].astype(BF16)
    resid_ref[...] = resid_all[kept, :]
    out_kept[...] = resid_all[kept, :] + back_all[kept, :] + lines_ref[5:6, :]


def ffn_grads_kernel(spot_ref, normed_ref, low_ref, act_ref, pre_ref, kept_ref, given_ref):
    hidden = act_ref.shape[1] // 2
    one, two = halves(spot_ref, normed_ref.shape[1] // 2)
    for columns, out_ref in ((two, given_ref), (one, kept_ref)):
        normed, low = normed_ref[:, columns], low_ref[:, columns]
        for side in range(2):
            at = slice(side * hidden, (side + 1) * hidden)
            start = 2 * side * hidden
            up = dot_tn(normed, pre_ref[:, at])
            out_ref[:, start : start + hidden] = up.astype(out_ref.dtype)
            down = dot_tn(low, act_ref[:, at])
            out_ref[:, start + hidden : start + 2 * hidden] = down.astype(out_ref.dtype)


def resid_kernel(
    spot_ref, kept_ref, got_ref, resid_ref, cotan_ref, lines_ref, grad_ref, low_ref, rows_ref
):
    half = kept_ref.shape[0]
    bit = spot_ref[2] % 2
    grad = kept_ref[...] + got_ref[...].astype(F32)
    hat, inverse = norm_parts(resid_ref[...])
    cotan = cotan_ref[window(bit, half), :]
    resid_grad = cotan + norm_back(grad, hat, inverse, lines_ref[2:3, :])
    grad_ref[...] = resid_grad
    low_ref[...] = resid_grad.astype(BF16)
    sums = [grad * hat, grad, resid_grad, cotan]
    rows_ref[...] = jnp.concatenate([column_sum(v) for v in sums], axis=0)


def attend_backward(spot_ref, seg_ref, q_ref, grad, lse_ref, kvs, dq_ref, outs, side):
    span, width = q_ref.shape
    biases = mask_biases(spot_ref, seg_ref, span)
    query = q_ref[...]
    dq, dks, dvs = None, [None] * 4, [None] * 4
    for head in range(width // HEAD_DIM):
        mine = lane_mask((span, width), head)
        masked_q = jnp.where(mine, query, jnp.zeros_like(query))
        masked_g = jnp.where(mine, grad, jnp.zeros_like(grad))
        lse = lse_ref[:, head * HEAD_DIM : head * HEAD_DIM + 1]
        probs = [
            jnp.exp(dot_nt(masked_q, kv[:, :width]) * SCALE + bias - lse)
            for kv, bias in zip(kvs, biases)
        ]
        grads = [dot_nt(masked_g, kv[:, width:]) for kv in kvs]
        inner = total([jnp.sum(p * g, axis=-1, keepdims=True) for p, g in zip(probs, grads)])
        raws = [(p * (g - inner) * SCALE).astype(BF16) for p, g in zip(probs, grads)]
        head_dq = total([dot_nn(raw, kv[:, :width]) for raw, kv in zip(raws, kvs)])
        dq = head_dq if head == 0 else jnp.where(mine, head_dq, dq)
        for step in range(4):
            head_dk = dot_tn(raws[step], query)
            head_dv = dot_tn(probs[step].astype(BF16), grad)
            dks[step] = head_dk if head == 0 else jnp.where(mine, head_dk, dks[step])
            dvs[step] = head_dv if head == 0 else jnp.where(mine, head_dv, dvs[step])
    dq_ref[:, side * width : (side + 1) * width] = dq
    at = 2 * side * width
    for step in range(4):
        outs[step][:, at : at + width] = dks[step].astype(outs[step].dtype)
        outs[step][:, at + width : at + 2 * width] = dvs[step].astype(outs[step].dtype)


def pull_kernel(
    spot_ref, seg_ref, q_n, lse_n, n0, n1, n2, n3, q_f, lse_f, f0, f1, f2, f3, mine_ref, got_ref,
    one_n, two_n, one_f, two_f,
    dq_ref, own_ref, out1, out2, out3, low_ref,
):
    half, cols = mine_ref.shape[0], q_n.shape[1]
    size = low_ref.shape[1] // 2
    bit = spot_ref[2] % 2
    low_ref[window(bit, half), :] = mine_ref[...]
    low_ref[window(1 - bit, half), :] = got_ref[...]
    one, two = halves(spot_ref, size)
    outs = (own_ref, out1, out2, out3)
    sides = ((q_n, lse_n, (n0, n1, n2, n3), one_n, two_n), (q_f, lse_f, (f0, f1, f2, f3), one_f, two_f))
    for side, (q_ref, lse_ref, kvs, first, second) in enumerate(sides):
        grad = dot_nn(low_ref[:, one], first[:size, 3 * cols :])
        grad = grad + dot_nn(low_ref[:, two], second[:size, 3 * cols :])
        attend_backward(
            spot_ref, seg_ref, q_ref, grad.astype(BF16), lse_ref, kvs, dq_ref, outs, side
        )


def input_kernel(
    spot_ref, stream_ref, lines_ref, resid_ref, rows_ref, up_sum_ref, dq_ref, own_ref, g1, g2, g3,
    one_n, two_n, one_f, two_f, normed_ref, low_ref, near_ref, far_ref,
    kept_ref, given_ref, small_ref, w_kept_ref, w_given_ref, pulled_ref, terms_ref,
):
    span, width = stream_ref.shape
    cols = dq_ref.shape[1] // 2
    hidden = up_sum_ref.shape[1] // 2
    half, size = span // 2, width // 2
    shard, slot = spot_ref[2], spot_ref[3]
    bit, far = shard % 2, shard ^ 2
    one, two = halves(spot_ref, size)
    small_ref[...] = jnp.zeros_like(small_ref)
    got = (own_ref[...] + g1[...].astype(F32)) + (g2[...].astype(F32) + g3[...].astype(F32))
    for side, place in enumerate((shard, far)):
        dq = dq_ref[:, side * cols : (side + 1) * cols]
        dkv = got[:, 2 * side * cols : 2 * (side + 1) * cols]
        at = side * 3 * cols
        pulled_ref[:, at : at + cols] = dq.astype(BF16)
        pulled_ref[:, at + cols : at + 3 * cols] = dkv.astype(BF16)
        small_ref[6:7, window(place, cols)] = column_sum(dq)
        small_ref[7:8, window(place, cols)] = column_sum(dkv[:, cols:])
        small_ref[pl.ds(8 + place, 1), :] = up_sum_ref[:, side * hidden : (side + 1) * hidden]
    for columns, near_w, far_w in ((one, one_n, one_f), (two, two_n, two_f)):
        back = dot_nt(pulled_ref[:, : 3 * cols], near_w[:size, : 3 * cols])
        back = back + dot_nt(pulled_ref[:, 3 * cols :], far_w[:size, : 3 * cols])
        terms_ref[:, columns] = back
    back = terms_ref[...]
    hat, inverse = norm_parts(stream_ref[...])
    small_ref[0:1, :] = column_sum(back * hat)
    small_ref[1:2, :] = column_sum(back)
    small_ref[2:6, :] = rows_ref[...]
    grad = norm_back(back, hat, inverse, lines_ref[0:1, :])
    small_ref[pl.ds(12 + slot, 1), :] = column_sum(grad) + rows_ref[2:3, :]
    terms_ref[...] = grad
    given_ref[...] = terms_ref[window(1 - bit, half), :].astype(BF16)
    kept_ref[...] = resid_ref[...] + terms_ref[window(bit, half), :]
    for columns, out_ref in ((two, w_given_ref), (one, w_kept_ref)):
        normed, low = normed_ref[:, columns], low_ref[:, columns]
        for side, mixed in enumerate((near_ref, far_ref)):
            at, start = side * 3 * cols, side * 4 * cols
            qkv = dot_tn(normed, pulled_ref[:, at : at + 3 * cols])
            out_ref[:, start : start + 3 * cols] = qkv.astype(out_ref.dtype)
            out = dot_tn(low, mixed[...])
            out_ref[:, start + 3 * cols : start + 4 * cols] = out.astype(out_ref.dtype)


def turn_bits(spot_ref):
    return 1 + spot_ref[0], 2 - spot_ref[0]


def split_two(values):
    high = values.astype(BF16)
    return high, (values - high.astype(F32)).astype(BF16)


def both(high, low):
    return high.astype(F32) + low.astype(F32)


def cut_kernel(spot_ref, kept_ref, got_ref, *refs):
    small_ref = refs[0] if len(refs) == 3 else None
    own_ref, send_ref = refs[-2:]
    rows = own_ref.shape[0] // 2
    chunk = spot_ref[1]
    first, second = turn_bits(spot_ref)
    for spot, place in enumerate((chunk, chunk ^ second)):
        at, to = window(place, rows), slice(spot * rows, (spot + 1) * rows)
        own_ref[to, :] = kept_ref[at, :] + got_ref[at, :].astype(F32)
        at = window(place ^ first, rows)
        send_ref[to, :] = (kept_ref[at, :] + got_ref[at, :].astype(F32)).astype(BF16)
    if small_ref is not None:
        width = small_ref.shape[1]
        send_ref[2 * rows :, :width], send_ref[2 * rows :, width:] = split_two(small_ref[...])


def middle_kernel(spot_ref, kept_ref, sent_ref, got_ref, own_ref, send_ref):
    rows = own_ref.shape[0]
    own_ref[...] = kept_ref[:rows, :] + got_ref[:rows, :].astype(F32)
    more = kept_ref[rows:, :] + got_ref[rows : 2 * rows, :].astype(F32)
    send_ref[:rows, :] = more.astype(BF16)
    if send_ref.shape[0] > rows:
        width = own_ref.shape[1] // 2
        mine, far = sent_ref[2 * rows :, :], got_ref[2 * rows :, :]
        small = both(mine[:, :width], mine[:, width:]) + both(far[:, :width], far[:, width:])
        send_ref[rows:, :width], send_ref[rows:, width:] = split_two(small)


def shards_kernel(spot_ref, own_ref, sent_ref, got_ref, kept_ref, send_ref):
    rows, width = kept_ref.shape
    values = own_ref[...] + got_ref[:rows, :].astype(F32)
    kept_ref[...] = values[:, :width]
    send_ref[:rows, :] = values[:, width:].astype(BF16)
    count = got_ref.shape[0] - rows
    if count:
        mine, far = sent_ref[rows:, :], got_ref[rows:, :]
        small = both(mine[:, :width], mine[:, width:]) + both(far[:, :width], far[:, width:])
        send_ref[rows : rows + count, :], send_ref[rows + count :, :] = split_two(small)


def owned_kernel(spot_ref, kept_ref, sent_ref, got_ref, out_ref, *small):
    rows = out_ref.shape[0]
    out_ref[...] = (kept_ref[...] + got_ref[:rows, :].astype(F32)).astype(BF16)
    if small:
        count = small[0].shape[0]
        top, end = slice(rows, rows + count), slice(rows + count, rows + 2 * count)
        mine = both(sent_ref[top, :], sent_ref[end, :])
        small[0][...] = mine + both(got_ref[top, :], got_ref[end, :])


def stack_kernel(spot_ref, one_ref, two_ref, out_ref):
    rows = one_ref.shape[0]
    out_ref[:rows, :] = one_ref[...]
    out_ref[rows:, :] = two_ref[...]


def places(spot_ref, rows):
    first, second = turn_bits(spot_ref)
    chunk = spot_ref[1]
    return [window(chunk ^ bits, rows) for bits in (0, second, first, 3)]


def own_ffn_kernel(spot_ref, p0, p1, p2, up_ref, down_ref):
    rows, hidden = p0.shape[0], up_ref.shape[1]
    pieces = (p0[...], p1[...], p2[:rows, :], p2[rows:, :])
    for at, piece in zip(places(spot_ref, rows), pieces):
        up_ref[at, :] = piece[:, :hidden].astype(F32)
        down_ref[at, :] = piece[:, hidden:].astype(F32)


def own_attention_kernel(spot_ref, p0, p1, p2, qkv_ref, out_ref):
    rows, cols = p0.shape[0], out_ref.shape[1]
    pieces = (p0[...], p1[...], p2[:rows, :], p2[rows:, :])
    for at, piece in zip(places(spot_ref, rows), pieces):
        for i in range(3):
            qkv_ref[i, at, :] = piece[:, i * cols : (i + 1) * cols].astype(F32)
        out_ref[at, :] = piece[:, 3 * cols :].astype(F32)


def add_low_kernel(spot_ref, kept_ref, got_ref, out_ref):
    out_ref[...] = (kept_ref[...] + got_ref[...].astype(F32)).astype(BF16)


def add_kernel(spot_ref, own_ref, got_ref, out_ref):
    out_ref[...] = own_ref[...] + got_ref[...]


def sums_kernel(spot_ref, steps_ref, own_ref, got_ref, table_ref, rows_ref, up_ref, qv_ref):
    cols = qv_ref.shape[1]
    shard = spot_ref[2]
    rows_ref[...] = own_ref[...] + got_ref[...]
    table_ref[...] = jnp.zeros_like(table_ref)
    for place in range(steps_ref.shape[0]):
        at = pl.ds(steps_ref[place], 1)
        table_ref[at, :] = table_ref[at, :] + rows_ref[12 + place : 13 + place, :]
    up_ref[...] = rows_ref[pl.ds(8 + shard, 1), :]
    qv_ref[...] = rows_ref[6:8, window(shard, cols)]


class Reduction:
    def __init__(self, order, kept, small=None):
        self.order, self.small = order, small
        self.rows, self.width = kept.shape[0] // 4, kept.shape[1]
        self.more = 0 if small is None else small.shape[0]
        self.kept = kept

    def cut(self, got):
        rows, width = self.rows, self.width
        extra = [] if self.small is None else [self.small]
        self.own, self.sent = self.order.call(
            cut_kernel,
            [((2 * rows, width), F32), ((2 * rows + self.more, width), BF16)],
            [self.kept, got, *extra],
        )
        self.got = self.order.swap_turn(self.sent, 0)

    def middle(self):
        rows, width = self.rows, self.width
        self.own, self.sent = self.order.call(
            middle_kernel,
            [((rows, width), F32), ((rows + self.more, width), BF16)],
            [self.own, self.sent, self.got],
        )
        self.got = self.order.swap_turn(self.sent, 1)

    def shards(self):
        rows, width = self.rows, self.width // 2
        self.own, self.sent = self.order.call(
            shards_kernel,
            [((rows, width), F32), ((rows + 2 * self.more, width), BF16)],
            [self.own, self.sent, self.got],
        )
        self.got = self.order.swap(self.sent, "tp", 2)

    def owned(self):
        rows, width = self.rows, self.width // 2
        extra = [] if self.small is None else [(self.small.shape, F32)]
        self.own, *small = self.order.call(
            owned_kernel,
            [((rows, width), BF16)] + extra,
            [self.own, self.sent, self.got],
        )
        self.small = small[0] if small else None
        self.got = self.order.swap_turn(self.own, 1)

    def stack(self):
        both_rows = self.order.call(
            stack_kernel, [((2 * self.rows, self.width // 2), BF16)], [self.own, self.got]
        )[0]
        self.last = self.order.swap_turn(both_rows, 0)

    def finish(self, kernel, shapes):
        return self.order.call(
            kernel, [(shape, F32) for shape in shapes], [self.own, self.got, self.last]
        )


def reduce_plainly(kept, given, chunk):
    whole = jnp.concatenate([kept, given.astype(F32)])
    mine = lax.psum_scatter(whole, "fsdp", scatter_dimension=0, tiled=True)
    quarter = lax.psum_scatter(mine, "ctx", scatter_dimension=0, tiled=True)
    width = quarter.shape[1] // 2
    far = lax.ppermute(quarter[:, width:], "tp", [(i, i ^ 2) for i in range(4)])
    return lax.all_gather(quarter[:, :width] + far, "ctx", axis=0, tiled=True)


def pieces_of(order, part, parts, rows):
    if parts == 2:
        return part, order.swap(part, "fsdp", 1)
    whole = lax.all_gather(part[:rows], "fsdp", axis=0, tiled=True)
    size = whole.shape[0] // 2
    return whole[:size], whole[size:]


def per_device(
    layer_input,
    timesteps,
    segment_ids,
    time_table,
    ln1_gain,
    ln1_bias,
    w_qkv,
    b_qv,
    w_out_t,
    b_out,
    ln2_gain,
    ln2_bias,
    w_up,
    b_up,
    w_down_t,
    b_down,
    out_grad,
    *,
    parts,
):
    span, width = layer_input.shape[1:]
    rows, cols = w_qkv.shape[1:]
    hidden = w_up.shape[1]
    half, size = span // 2, width // 2
    core = lax.axis_index("fsdp")
    chunk = lax.axis_index("ctx")
    shard = lax.axis_index("tp")
    place = core if parts == 2 else 0 * core
    spot = jnp.stack([place, chunk, shard, 2 * core + shard // 2]).astype(jnp.int32)
    order = Order(spot)
    line = lambda values: values.reshape(1, -1)
    dma = lambda count: pltpu.SemaphoreType.DMA((count,))

    pack = order.call(
        pack_first_kernel,
        [((rows + BIAS_ROWS, 4 * cols), BF16)],
        [timesteps, w_qkv, w_out_t, b_qv, line(b_up)],
        far=(1, 2, 3, 4),
        scratch=[
            pltpu.VMEM(w_qkv.shape, F32),
            pltpu.VMEM(w_out_t.shape, F32),
            pltpu.VMEM(b_qv.shape, F32),
            pltpu.VMEM((1, hidden), F32),
            dma(4),
        ],
    )[0]
    near = pieces_of(order, pack, parts, rows)
    pack_far = order.swap(pack, "tp", 2)
    stream, normed, seg, lines = order.call(
        stream_kernel,
        [
            ((span, width), F32), ((span, width), BF16), ((1, segment_ids.shape[1]), jnp.int32),
            ((8, width), F32),
        ],
        [timesteps, layer_input, time_table, segment_ids]
        + [line(v) for v in (ln1_gain, ln1_bias, ln2_gain, ln2_bias, b_out, b_down)],
        far=range(1, 10),
        scratch=[
            pltpu.VMEM((span, width), F32),
            pltpu.VMEM((8, width), F32),
            pltpu.VMEM(segment_ids.shape, jnp.int32),
            pltpu.VMEM((6, 1, width), F32),
            dma(9),
        ],
    )
    projected = [((span, cols), BF16), ((span, 2 * cols), BF16)]
    project = functools.partial(project_kernel, row=rows)
    q_near, kv_near = order.call(project, projected, [normed, *near, pack])
    kvs_near = [kv_near] + order.swap_three(kv_near, "ctx")

    rest, rest_half, cotan = order.call(
        pack_rest_kernel,
        [((rows, 2 * hidden), BF16), ((rows // 2, 2 * hidden), BF16), ((span, width), F32)],
        [w_up, w_down_t, out_grad],
        far=(0, 1, 2),
        scratch=[pltpu.VMEM(w_up.shape, F32), pltpu.VMEM(w_down_t.shape, F32), dma(3)],
    )
    rest_near = pieces_of(order, rest, parts, rows)
    rest_far = order.swap(rest_half if parts == 2 else rest, "tp", 2)

    pack_far, *kvs_near[1:] = hold(pack_far, *kvs_near[1:])
    far = pieces_of(order, pack_far, parts, rows)
    q_far, kv_far = order.call(project, projected, [normed, *far, pack_far])
    kvs_far = [kv_far] + order.swap_three(kv_far, "ctx")
    attended = [((span, cols), BF16), ((span, cols), F32)]
    mixed_near, lse_near = order.call(attend_one_kernel, attended, [seg, q_near, *kvs_near])
    if parts == 2:
        rest_more = order.swap(rest_far, "ctx", 1)
        rest_far = [rest_far, rest_more, order.swap(rest_far, "fsdp", 1)]
    else:
        rest_far = pieces_of(order, rest_far, parts, rows)
    mixed_far, lse_far, terms, given = order.call(
        attend_two_kernel,
        attended + [((span, width), F32), ((span, width), BF16)],
        [seg, q_far, *kvs_far, mixed_near, *near, *far],
    )
    got = order.swap(given, "tp", 1)
    if parts == 2:
        rest_far.append(order.swap(rest_more, "fsdp", 1))

    (
        back_given, back_kept, ffn_given, out_kept, resid, normed_two, act, pre, low, up_sum,
    ) = order.call(
        functools.partial(ffn_kernel, row=rows),
        [
            ((half, width), BF16), ((half, width), F32), ((half, width), BF16),
            ((half, width), F32), ((half, width), F32), ((span, width), BF16),
            ((span, 2 * hidden), BF16), ((span, 2 * hidden), BF16), ((span, width), BF16),
            ((1, 2 * hidden), F32),
        ],
        [stream, terms, got, cotan, lines, pack, pack_far, *rest_near, *rest_far],
        scratch=[pltpu.VMEM((span, width), F32)] * 2
        + [pltpu.VMEM((size, 2 * hidden), BF16)] * 2,
        limit=24,
    )
    back_got = order.swap(back_given, "tp", 1)
    ffn_kept, ffn_sent = order.call(
        ffn_grads_kernel,
        [((size, 4 * hidden), F32), ((size, 4 * hidden), BF16)],
        [normed_two, low, act, pre],
    )
    if parts == 2:
        ffn_far = order.swap(ffn_sent, "fsdp", 1)
    resid_grad, resid_low, resid_rows = order.call(
        resid_kernel,
        [((half, width), F32), ((half, width), BF16), ((4, width), F32)],
        [back_kept, back_got, resid, cotan, lines],
    )
    resid_got = order.swap(resid_low, "tp", 1)
    if parts == 2:
        ffn_sum = Reduction(order, ffn_kept)
        ffn_sum.cut(ffn_far)
    dq, own, *shares, low_all = order.call(
        pull_kernel,
        [((span, 2 * cols), F32), ((span, 4 * cols), F32)]
        + [((span, 4 * cols), BF16)] * 3
        + [((span, width), BF16)],
        [
            seg, q_near, lse_near, *kvs_near, q_far, lse_far, *kvs_far, resid_low, resid_got,
            *near, *far,
        ],
    )
    shared = [order.swap(piece, "ctx", bits + 1) for bits, piece in enumerate(shares)]

    ffn_got = order.swap(ffn_given, "tp", 1)
    if parts == 2:
        ffn_sum.middle()
    out_half = order.call(add_low_kernel, [((half, width), BF16)], [out_kept, ffn_got])[0]
    out_halves = [out_half] + order.swap_three(out_half, "tp")

    seqs = 2 * parts
    small_rows = -(-(12 + seqs) // 16) * 16
    in_kept, in_given, small, attention_kept, attention_sent = order.call(
        input_kernel,
        [
            ((half, width), F32), ((half, width), BF16), ((small_rows, width), F32),
            ((size, 8 * cols), F32), ((size, 8 * cols), BF16),
        ],
        [
            stream, lines, resid_grad, resid_rows, up_sum, dq, own, *shared, *near, *far,
            normed, low_all, mixed_near, mixed_far,
        ],
        scratch=[pltpu.VMEM((span, 6 * cols), BF16), pltpu.VMEM((span, width), F32)],
    )
    if parts == 2:
        attention_far = order.swap(attention_sent, "fsdp", 1)
    in_got = order.swap(in_given, "tp", 1)
    if parts == 2:
        attention_sum = Reduction(order, attention_kept, small)
        ffn_sum.shards()
        attention_sum.cut(attention_far)
    in_half = order.call(add_low_kernel, [((half, width), BF16)], [in_kept, in_got])[0]
    in_halves = [in_half] + order.swap_three(in_half, "tp")
    if parts == 2:
        ffn_sum.owned()
        attention_sum.middle()
        output = join(order, 2, out_halves, F32)
        ffn_sum.stack()
        attention_sum.shards()
        grads_up, grads_down = ffn_sum.finish(own_ffn_kernel, [(rows, hidden)] * 2)
        attention_sum.owned()
        small = attention_sum.small
        small_got = order.swap(small, "tp", 1)
        attention_sum.stack()
        small = order.call(add_kernel, [(small.shape, F32)], [small, small_got])[0]
        small_got = order.swap(small, "fsdp", 1)
        grad_input = join(order, 2, in_halves, F32)
        bits = near[1][rows : rows + 6 : 2, 2 * cols : 2 * cols + 2].astype(F32)
        far_steps = jnp.sum(bits, axis=0).astype(jnp.int32)
        steps = jnp.where(
            core == 0,
            jnp.concatenate([timesteps, far_steps]),
            jnp.concatenate([far_steps, timesteps]),
        )
    else:
        output = join(order, 2, out_halves, F32)
        grad_input = join(order, 2, in_halves, F32)
        both_grads = reduce_plainly(ffn_kept, ffn_sent, chunk)
        grads_up, grads_down = both_grads[:, :hidden], both_grads[:, hidden:]
        small = lax.psum(small, ("fsdp", "ctx", "tp"))
        small_got = jnp.zeros_like(small)
        steps = lax.all_gather(timesteps, "fsdp", axis=0, tiled=True)
    table, sums, up_line, qv_lines = order.call(
        sums_kernel,
        [(time_table.shape, F32), (small.shape, F32), ((1, hidden), F32), ((2, cols), F32)],
        [steps, small, small_got],
    )
    if parts == 2:
        grads_qkv, grads_out = attention_sum.finish(
            own_attention_kernel, [(3, rows, cols), (rows, cols)]
        )
    else:
        every = reduce_plainly(attention_kept, attention_sent, chunk)
        grads_qkv = jnp.stack([every[:, i * cols : (i + 1) * cols] for i in range(3)])
        grads_out = every[:, 3 * cols :]

    shape = layer_input.shape
    return (
        output.reshape(shape),
        grad_input.reshape(shape),
        table,
        sums[0],
        sums[1],
        grads_qkv,
        qv_lines,
        grads_out,
        sums[4],
        sums[2],
        sums[3],
        grads_up,
        up_line.reshape(-1),
        grads_down,
        sums[5],
    )


def solution(mesh):
    placed = (
        P("fsdp", "ctx", None),
        P("fsdp"),
        P("fsdp", None),
        P(),
        P(),
        P(),
        P(None, "fsdp", "tp"),
        P(None, "tp"),
        P("fsdp", "tp"),
        P(),
        P(),
        P(),
        P("fsdp", "tp"),
        P("tp"),
        P("fsdp", "tp"),
        P(),
        P("fsdp", "ctx", None),
    )
    return jax.shard_map(
        functools.partial(per_device, parts=mesh.shape["fsdp"]),
        mesh=mesh,
        in_specs=placed,
        out_specs=(
            P("fsdp", "ctx", None),
            P("fsdp", "ctx", None),
            P(),
            P(),
            P(),
            P(None, "fsdp", "tp"),
            P(None, "tp"),
            P("fsdp", "tp"),
            P(),
            P(),
            P(),
            P("fsdp", "tp"),
            P("tp"),
            P("fsdp", "tp"),
            P(),
        ),
        check_vma=False,
    )
```

```python
import functools
import jax
import jax.numpy as jnp
from jax import lax
from jax.experimental import pallas as pl
from jax.experimental.pallas import tpu as pltpu
from jax.sharding import PartitionSpec as P

HEAD_DIM = 64
SCALE = HEAD_DIM ** (-0.5)
EPSILON = 1e-05
NEGATIVE = -1e30
F32 = jnp.float32
BF16 = jnp.bfloat16
BIAS_ROWS = 16
PAD = 16
CUBE = 0.044715
ROOT = 0.7978845608028654
COST, QUICK, LONG = 8_000_000_000, 1_000, 20_000_000_000
VMEM = pl.BlockSpec(memory_space=pltpu.VMEM)
SMEM = pl.BlockSpec(memory_space=pltpu.SMEM)


def dot_nn(left, right):
    return lax.dot_general(left, right, (((1,), (0,)), ((), ())), preferred_element_type=F32)


def dot_nt(left, right):
    return lax.dot_general(left, right, (((1,), (1,)), ((), ())), preferred_element_type=F32)


def dot_tn(left, right):
    return lax.dot_general(left, right, (((0,), (0,)), ((), ())), preferred_element_type=F32)


def total(values):
    return functools.reduce(jnp.add, values)


def norm_parts(values):
    centre = values - jnp.mean(values, axis=-1, keepdims=True)
    spread = jnp.mean(centre * centre, axis=-1, keepdims=True)
    inverse = lax.rsqrt(spread + EPSILON)
    return centre * inverse, inverse


def norm_back(grad, hat, inverse, gain):
    scaled = grad * gain
    mean_one = jnp.mean(scaled, axis=-1, keepdims=True)
    mean_two = jnp.mean(scaled * hat, axis=-1, keepdims=True)
    return inverse * (scaled - mean_one - hat * mean_two)


def column_sum(values):
    return jnp.sum(values, axis=0, keepdims=True)


def window(index, size):
    return pl.ds(pl.multiple_of(index * size, size), size)


def halves(spot_ref, size):
    return window(spot_ref[0], size), window(1 - spot_ref[0], size)


def hold(*values):
    return lax.optimization_barrier(values)


class Order:
    def __init__(self, spot, parts):
        self.spot, self.parts, self.cost = spot, parts, COST

    def call(self, kernel, outs, operands, *, far=(), scratch=(), limit=5, cost=None):
        specs = [
            SMEM if operand.ndim == 1
            else pl.BlockSpec(memory_space=pltpu.HBM if i in far else pltpu.VMEM)
            for i, operand in enumerate(operands)
        ]
        operands = [
            pltpu.with_memory_space_constraint(operand, pltpu.HBM) if i in far else operand
            for i, operand in enumerate(operands)
        ]
        count = len(operands)

        def body(*refs):
            kernel(refs[count], *refs[:count], *refs[count + 1 :])

        results = pl.pallas_call(
            body,
            out_shape=tuple(jax.ShapeDtypeStruct(shape, dtype) for shape, dtype in outs),
            in_specs=specs + [SMEM],
            out_specs=(VMEM,) * len(outs),
            scratch_shapes=list(scratch),
            compiler_params=pltpu.CompilerParams(vmem_limit_bytes=limit << 20),
            cost_estimate=pl.CostEstimate(
                flops=cost or self.cost, bytes_accessed=1 << 16, transcendentals=0
            ),
        )(*operands, self.spot)
        first, self.spot = hold(results[0], self.spot)
        return [first, *results[1:]]

    def swap(self, values, axis, bits):
        values, self.spot = hold(values, self.spot)
        size = 2 if axis == "fsdp" else 4
        with jax.named_scope("swap_%s_%d" % (axis, bits)):
            return lax.ppermute(values, axis, [(i, i ^ bits) for i in range(size)])

    def swap_three(self, values, axis):
        return [self.swap(values, axis, bits) for bits in (1, 2, 3)]

    def swap_turn(self, values, turn):
        if self.parts != 2:
            return self.swap(values, "ctx", 1 + turn)
        values, self.spot = hold(values, self.spot)
        pairs = [
            (4 * core + i, 4 * core + (i ^ (1 + (core + turn) % 2)))
            for core in range(2)
            for i in range(4)
        ]
        with jax.named_scope("swap_turn_%d" % turn):
            return lax.ppermute(values, ("fsdp", "ctx"), pairs)


def clear_below(ref, rows):
    if ref.shape[0] > rows:
        ref[rows:, :] = jnp.zeros((ref.shape[0] - rows, ref.shape[1]), ref.dtype)


def fetch(copies, sems):
    started = [
        pltpu.make_async_copy(source, target, sems.at[i])
        for i, (source, target) in enumerate(copies)
    ]
    for copy in started:
        copy.start()
    for copy in started:
        copy.wait()


def split_three(values):
    high = values.astype(BF16)
    rest = values - high.astype(F32)
    middle = rest.astype(BF16)
    return [high, middle, (rest - middle.astype(F32)).astype(BF16)]


def pack_kernel(
    spot_ref, steps_ref, w_hbm, out_hbm, qv_hbm, up_bias_hbm, up_hbm, down_hbm,
    pack_ref, rest_ref, quarter_ref,
    w_ref, o_ref, qv_ref, up_bias_ref, up_ref, down_ref, sems,
):
    rows, cols = w_ref.shape[1:]
    hidden = up_ref.shape[1]
    fetch(
        [
            (w_hbm, w_ref), (out_hbm, o_ref), (qv_hbm, qv_ref), (up_bias_hbm, up_bias_ref),
            (up_hbm, up_ref), (down_hbm, down_ref),
        ],
        sems,
    )
    for i in range(3):
        pack_ref[:rows, i * cols : (i + 1) * cols] = w_ref[i].astype(BF16)
    pack_ref[:rows, 3 * cols :] = o_ref[...].astype(BF16)
    lanes = lax.broadcasted_iota(jnp.int32, (1, cols), 1)
    steps = jnp.zeros((1, cols), F32)
    for i in range(steps_ref.shape[0]):
        steps = jnp.where(lanes == i, steps_ref[i].astype(F32), steps)
    fill = jnp.zeros((1, cols), F32)
    up_bias = up_bias_ref[...]
    lines = [
        jnp.concatenate([qv_ref[0:1], qv_ref[1:2], steps, fill], axis=1),
        jnp.concatenate([up_bias[:, : 2 * cols], fill, fill], axis=1),
        jnp.concatenate([up_bias[:, 2 * cols :], fill, fill], axis=1),
    ]
    parts = split_three(jnp.concatenate(lines, axis=0))
    fill = jnp.zeros((BIAS_ROWS - 9, 4 * cols), F32)
    stack = jnp.concatenate([v.astype(F32) for v in parts] + [fill], axis=0)
    pack_ref[rows:, :] = stack.astype(BF16)
    rest_ref[:, :hidden] = up_ref[...].astype(BF16)
    rest_ref[:, hidden:] = down_ref[...].astype(BF16)
    quarter = rows // 4
    mine = window(spot_ref[1], quarter)
    quarter_ref[:quarter, :hidden] = up_ref[mine, :].astype(BF16)
    quarter_ref[:quarter, hidden:] = down_ref[mine, :].astype(BF16)
    clear_below(quarter_ref, quarter)


def bias_lines(pack_ref, row):
    bits = pack_ref[row : row + BIAS_ROWS, :].astype(F32)
    lines = bits[0:3] + bits[3:6] + bits[6:9]
    half = 4 * HEAD_DIM
    return lines[0:1], jnp.concatenate([lines[1:2, :half], lines[2:3, :half]], axis=1)


def out_part(ref, size):
    cols = 2 * HEAD_DIM
    return ref[:size, ref.shape[1] - cols :]


def pair_kernel(spot_ref, own_ref, got_ref, out_ref):
    pair, span = spot_ref[2] // 2, own_ref.shape[0]
    out_ref[window(pair, span), :] = own_ref[...].astype(F32)
    out_ref[window(1 - pair, span), :] = got_ref[...].astype(F32)


def add_pair_kernel(spot_ref, base_ref, own_ref, got_ref, out_ref):
    span = base_ref.shape[0]
    terms = own_ref[:span, :].astype(F32) + got_ref[:span, :].astype(F32)
    out_ref[...] = (base_ref[...] + terms).astype(BF16)


def stream_kernel(
    spot_ref, steps_ref, x_hbm, table_hbm, seg_hbm, cotan_hbm, g1, b1, g2, b2, bo, bd,
    stream_ref, normed_ref, seg_ref, lines_ref, cotan_ref, x_ref, table_ref, ids_ref, line_ref,
    sems,
):
    pair = spot_ref[2] // 2
    step = steps_ref[pair]
    block = pl.multiple_of(step // 8 * 8, 8)
    copies = [
        (x_hbm.at[pair], x_ref),
        (table_hbm.at[pl.ds(block, 8), :], table_ref),
        (seg_hbm, ids_ref),
        (cotan_hbm.at[pair], cotan_ref),
    ]
    vectors = (g1, b1, g2, b2, bo, bd)
    fetch(copies + [(v, line_ref.at[i]) for i, v in enumerate(vectors)], sems)
    for i in range(len(vectors)):
        lines_ref[i : i + 1, :] = line_ref[i]
    seg_ref[...] = ids_ref[pl.ds(pair, 1), :]
    stream = x_ref[...] + table_ref[pl.ds(step % 8, 1), :]
    hat, _ = norm_parts(stream)
    stream_ref[...] = stream
    normed_ref[...] = (hat * line_ref[0] + line_ref[1]).astype(BF16)


def project_kernel(spot_ref, normed_ref, one_ref, two_ref, bias_ref, q_ref, kv_ref, *, row):
    span, cols = q_ref.shape
    size = normed_ref.shape[1] // 2
    one, two = halves(spot_ref, size)
    raw = dot_nn(normed_ref[:, one], one_ref[:size, : 3 * cols])
    raw = raw + dot_nn(normed_ref[:, two], two_ref[:size, : 3 * cols])
    line, _ = bias_lines(bias_ref, row)
    q_bias, v_bias = line[:, :cols], line[:, cols : 2 * cols]
    q_ref[...] = (raw[:, :cols] + q_bias).astype(BF16)
    kv_ref[:span, :cols] = raw[:, cols : 2 * cols].astype(BF16)
    kv_ref[:span, cols:] = (raw[:, 2 * cols :] + v_bias).astype(BF16)
    clear_below(kv_ref, span)


def mask_biases(spot_ref, seg_ref, span):
    chunk = spot_ref[1]
    ids = [seg_ref[:, window(chunk ^ step, span)] for step in range(seg_ref.shape[1] // span)]
    own = jnp.broadcast_to(ids[0], (span, span)).T
    return [
        jnp.where(own == jnp.broadcast_to(step_ids, (span, span)), 0.0, NEGATIVE)
        for step_ids in ids
    ]


def lane_mask(shape, head):
    return (lax.broadcasted_iota(jnp.int32, shape, 1) // HEAD_DIM) == head


def attend_forward(spot_ref, seg_ref, q_ref, kvs, mixed_ref, lse_ref):
    span, width = q_ref.shape
    biases = mask_biases(spot_ref, seg_ref, span)
    query = q_ref[...]
    mixed, lse = None, None
    for head in range(width // HEAD_DIM):
        mine = lane_mask((span, width), head)
        masked = jnp.where(mine, query, jnp.zeros_like(query))
        scores = [
            dot_nt(masked, kv[:span, :width]) * SCALE + bias for kv, bias in zip(kvs, biases)
        ]
        top = functools.reduce(
            jnp.maximum, [jnp.max(block, axis=-1, keepdims=True) for block in scores]
        )
        grown = [jnp.exp(block - top) for block in scores]
        mass = total([jnp.sum(block, axis=-1, keepdims=True) for block in grown])
        share = 1.0 / mass
        out = total(
            [
                dot_nn((block * share).astype(BF16), kv[:span, width:])
                for block, kv in zip(grown, kvs)
            ]
        )
        log_mass = jnp.broadcast_to(top + jnp.log(mass), (span, width))
        mixed = out if head == 0 else jnp.where(mine, out, mixed)
        lse = log_mass if head == 0 else jnp.where(mine, log_mass, lse)
    mixed_ref[...] = mixed.astype(BF16)
    lse_ref[...] = lse


def attend_one_kernel(spot_ref, seg_ref, q_ref, kv0, kv1, kv2, kv3, mixed_ref, lse_ref):
    attend_forward(spot_ref, seg_ref, q_ref, (kv0, kv1, kv2, kv3), mixed_ref, lse_ref)


def attend_two_kernel(
    spot_ref, seg_ref, q_ref, kv0, kv1, kv2, kv3, near_ref, one_n, two_n, one_f, two_f,
    mixed_ref, lse_ref, given_ref,
):
    attend_forward(spot_ref, seg_ref, q_ref, (kv0, kv1, kv2, kv3), mixed_ref, lse_ref)
    size = given_ref.shape[1] // 2
    one, two = halves(spot_ref, size)
    near, far = near_ref[...], mixed_ref[...]
    for columns, near_w, far_w in ((one, one_n, one_f), (two, two_n, two_f)):
        terms = dot_nt(near, out_part(near_w, size)) + dot_nt(far, out_part(far_w, size))
        given_ref[: near.shape[0], columns] = terms.astype(BF16)
    clear_below(given_ref, near.shape[0])


def stack_kernel(spot_ref, one_ref, two_ref, out_ref):
    rows = out_ref.shape[0] // 2
    out_ref[:rows, :] = one_ref[:rows, :]
    out_ref[rows:, :] = two_ref[:rows, :]


def gelu_parts(x):
    square = x * x
    curve = jnp.tanh(ROOT * (x + CUBE * (x * square)))
    half = 0.5 * (1.0 + curve)
    slope = half + 0.5 * x * (1.0 - curve * curve) * (ROOT * (1.0 + 3.0 * CUBE * square))
    return x * half, slope


def ffn_side(
    normed_ref, low_ref, bias, first, second, columns, act_ref, pre_ref, sum_ref, *sums
):
    hidden = act_ref.shape[1]
    one, two = columns
    pre = dot_nn(normed_ref[:, one], first[:, :hidden])
    pre = pre + dot_nn(normed_ref[:, two], second[:, :hidden]) + bias
    value, slope = gelu_parts(pre)
    grad = dot_nn(low_ref[:, one], first[:, hidden:])
    grad = (grad + dot_nn(low_ref[:, two], second[:, hidden:])) * slope
    sum_ref[...] = column_sum(grad)
    act_ref[...] = value.astype(BF16)
    pre_ref[...] = grad.astype(BF16)
    act, pre_low = act_ref[...], pre_ref[...]
    for at, weights in zip(columns, (first, second)):
        back = dot_nt(pre_low, weights[:, :hidden])
        down = dot_nt(act, weights[:, hidden:])
        if len(sums) == 2:
            back_ref, out_ref = sums
        else:
            back_near, out_near, back_ref, out_ref = sums
            back, down = back + back_near[:, at], down + out_near[:, at]
        back_ref[: act.shape[0], at] = back.astype(back_ref.dtype)
        out_ref[: act.shape[0], at] = down.astype(out_ref.dtype)
    clear_below(sums[-2], act.shape[0])
    clear_below(sums[-1], act.shape[0])


def ffn_near_kernel(
    spot_ref, stream_ref, mine_ref, got_ref, cotan_ref, lines_ref, pack_ref, first, second,
    back_ref, ffn_ref, out_ref, resid_ref, normed_ref, act_ref, pre_ref, low_ref, sum_ref, *, row,
):
    span = stream_ref.shape[0]
    terms = mine_ref[:span, :].astype(F32) + got_ref[:span, :].astype(F32)
    resid = stream_ref[...] + terms + lines_ref[4:5, :]
    resid_ref[...] = resid
    out_ref[...] = resid + lines_ref[5:6, :]
    hat, _ = norm_parts(resid)
    normed_ref[...] = (hat * lines_ref[2:3, :] + lines_ref[3:4, :]).astype(BF16)
    low_ref[...] = cotan_ref[...].astype(BF16)
    ffn_side(
        normed_ref, low_ref, bias_lines(pack_ref, row)[1], first, second,
        halves(spot_ref, first.shape[0]), act_ref, pre_ref, sum_ref, back_ref, ffn_ref,
    )


def ffn_far_kernel(spot_ref, normed_ref, low_ref, back_near, ffn_near, pack_ref, *refs, row):
    count = len(refs) - 7
    pieces, outs, (first, second) = refs[:count], refs[count:-2], refs[-2:]
    if count == 2:
        first, second = pieces
    else:
        rows = pieces[0].shape[0] // 2
        turn, other = turn_bits(spot_ref)
        for target, pairs, bits in (
            (first, pieces[:2], (0, turn, other, 3)),
            (second, pieces[2:], (0, other, turn, 3)),
        ):
            for i in range(4):
                block = pairs[i // 2][i % 2 * rows : (i % 2 + 1) * rows, :]
                target[window(spot_ref[1] ^ bits[i], rows), :] = block
    act_ref, pre_ref, sum_ref, back_ref, ffn_ref = outs
    ffn_side(
        normed_ref, low_ref, bias_lines(pack_ref, row)[1], first, second,
        halves(spot_ref, first.shape[0]), act_ref, pre_ref, sum_ref, back_near, ffn_near,
        back_ref, ffn_ref,
    )


def ffn_grads_kernel(
    spot_ref, normed_ref, low_ref, act_n, pre_n, act_f, pre_f, kept_ref, *given
):
    hidden = act_n.shape[1]
    one, two = halves(spot_ref, normed_ref.shape[1] // 2)
    for columns in (two, one):
        normed, low = normed_ref[:, columns], low_ref[:, columns]
        for i, (left, right) in enumerate(((normed, pre_n), (low, act_n), (normed, pre_f), (low, act_f))):
            grads = dot_tn(left, right[...])
            if columns is one:
                kept_ref[:, i * hidden : (i + 1) * hidden] = grads
            else:
                given[i][...] = grads.astype(BF16)


def resid_part(
    spot_ref, mine_ref, got_ref, resid_ref, cotan_ref, lines_ref, grad_ref, low_ref, rows_ref,
    work_ref,
):
    half = resid_ref.shape[0] // 2
    mine = window(spot_ref[2] % 2, half)
    span = resid_ref.shape[0]
    grad = mine_ref[:span, :].astype(F32) + got_ref[:span, :].astype(F32)
    hat, inverse = norm_parts(resid_ref[...])
    resid_grad = cotan_ref[...] + norm_back(grad, hat, inverse, lines_ref[2:3, :])
    grad_ref[...] = resid_grad
    low_ref[...] = resid_grad.astype(BF16)
    work_ref[0] = grad * hat
    work_ref[1] = grad
    sums = [work_ref[0, mine, :], work_ref[1, mine, :], grad_ref[mine, :], cotan_ref[mine, :]]
    rows_ref[...] = jnp.concatenate([column_sum(v) for v in sums], axis=0)


def attend_backward(spot_ref, seg_ref, q_ref, grad, lse_ref, kvs, dq_ref, outs, side):
    span, width = q_ref.shape
    biases = mask_biases(spot_ref, seg_ref, span)
    query = q_ref[...]
    dq, dks, dvs = None, [None] * 4, [None] * 4
    for head in range(width // HEAD_DIM):
        mine = lane_mask((span, width), head)
        masked_q = jnp.where(mine, query, jnp.zeros_like(query))
        masked_g = jnp.where(mine, grad, jnp.zeros_like(grad))
        lse = lse_ref[:, head * HEAD_DIM : head * HEAD_DIM + 1]
        probs = [
            jnp.exp(dot_nt(masked_q, kv[:span, :width]) * SCALE + bias - lse)
            for kv, bias in zip(kvs, biases)
        ]
        grads = [dot_nt(masked_g, kv[:span, width:]) for kv in kvs]
        inner = total([jnp.sum(p * g, axis=-1, keepdims=True) for p, g in zip(probs, grads)])
        raws = [(p * (g - inner) * SCALE).astype(BF16) for p, g in zip(probs, grads)]
        head_dq = total([dot_nn(raw, kv[:span, :width]) for raw, kv in zip(raws, kvs)])
        dq = head_dq if head == 0 else jnp.where(mine, head_dq, dq)
        for step in range(4):
            head_dk = dot_tn(raws[step], query)
            head_dv = dot_tn(probs[step].astype(BF16), grad)
            dks[step] = head_dk if head == 0 else jnp.where(mine, head_dk, dks[step])
            dvs[step] = head_dv if head == 0 else jnp.where(mine, head_dv, dvs[step])
    dq_ref[:, side * width : (side + 1) * width] = dq
    at = 2 * side * width
    for step in range(4):
        outs[step][:span, at : at + width] = dks[step].astype(outs[step].dtype)
        outs[step][:span, at + width : at + 2 * width] = dvs[step].astype(outs[step].dtype)


def pull_kernel(
    spot_ref, seg_ref, q_n, lse_n, n0, n1, n2, n3, q_f, lse_f, f0, f1, f2, f3,
    mine_ref, got_ref, resid_ref, cotan_ref, lines_ref, one_n, two_n, one_f, two_f,
    dq_ref, own_ref, out1, out2, out3, grad_ref, low_ref, rows_ref, work_ref,
):
    size = low_ref.shape[1] // 2
    resid_part(
        spot_ref, mine_ref, got_ref, resid_ref, cotan_ref, lines_ref, grad_ref, low_ref, rows_ref,
        work_ref,
    )
    one, two = halves(spot_ref, size)
    outs = (own_ref, out1, out2, out3)
    near = (q_n, lse_n, (n0, n1, n2, n3), one_n, two_n)
    far = (q_f, lse_f, (f0, f1, f2, f3), one_f, two_f)
    for side, (q_ref, lse_ref, kvs, first, second) in enumerate((near, far)):
        grad = dot_nn(low_ref[:, one], out_part(first, size))
        grad = grad + dot_nn(low_ref[:, two], out_part(second, size))
        attend_backward(
            spot_ref, seg_ref, q_ref, grad.astype(BF16), lse_ref, kvs, dq_ref, outs, side
        )
    for out_ref in (out1, out2, out3):
        clear_below(out_ref, q_n.shape[0])


def input_kernel(
    spot_ref, stream_ref, lines_ref, rows_ref, up_near, up_far, dq_ref, own_ref, g1, g2, g3,
    one_n, two_n, one_f, two_f, normed_ref, low_ref, near_ref, far_ref,
    given_ref, small_ref, w_kept_ref, w_near_ref, w_far_ref, pulled_ref, terms_ref,
):
    span, width = stream_ref.shape
    cols = dq_ref.shape[1] // 2
    size = width // 2
    shard, slot = spot_ref[2], spot_ref[3]
    far = shard ^ 2
    one, two = halves(spot_ref, size)
    small_ref[...] = jnp.zeros_like(small_ref)
    parts = [ref[:span, :].astype(F32) for ref in (g1, g2, g3)]
    got = (own_ref[...] + parts[0]) + (parts[1] + parts[2])
    for side, (place, up_sum) in enumerate(((shard, up_near), (far, up_far))):
        dq = dq_ref[:, side * cols : (side + 1) * cols]
        dkv = got[:, 2 * side * cols : 2 * (side + 1) * cols]
        at = side * 3 * cols
        pulled_ref[:, at : at + cols] = dq.astype(BF16)
        pulled_ref[:, at + cols : at + 3 * cols] = dkv.astype(BF16)
        small_ref[6:7, window(place, cols)] = column_sum(dq)
        small_ref[7:8, window(place, cols)] = column_sum(dkv[:, cols:])
        small_ref[pl.ds(8 + place, 1), :] = up_sum[...]
    for columns, near_w, far_w in ((one, one_n, one_f), (two, two_n, two_f)):
        back = dot_nt(pulled_ref[:, : 3 * cols], near_w[:size, : 3 * cols])
        back = back + dot_nt(pulled_ref[:, 3 * cols :], far_w[:size, : 3 * cols])
        terms_ref[:, columns] = back
    back = terms_ref[...]
    hat, inverse = norm_parts(stream_ref[...])
    small_ref[0:1, :] = column_sum(back * hat)
    small_ref[1:2, :] = column_sum(back)
    small_ref[2:6, :] = rows_ref[...]
    grad = norm_back(back, hat, inverse, lines_ref[0:1, :])
    small_ref[pl.ds(12 + slot, 1), :] = column_sum(grad) + rows_ref[2:3, :]
    given_ref[...] = grad.astype(BF16)
    given = (w_near_ref, w_far_ref)
    for columns in (two, one):
        normed, low = normed_ref[:, columns], low_ref[:, columns]
        for side, mixed in enumerate((near_ref, far_ref)):
            at, start = side * 3 * cols, side * 4 * cols
            qkv = dot_tn(normed, pulled_ref[:, at : at + 3 * cols])
            out = dot_tn(low, mixed[...])
            if columns is one:
                w_kept_ref[:, start : start + 3 * cols] = qkv
                w_kept_ref[:, start + 3 * cols : start + 4 * cols] = out
            else:
                given[side][:size, : 3 * cols] = qkv.astype(BF16)
                given[side][:size, 3 * cols :] = out.astype(BF16)
    w_near_ref[size:, :], w_far_ref[size:, :] = split_two(small_ref[...])


def turn_bits(spot_ref):
    return 1 + spot_ref[0], 2 - spot_ref[0]


def split_two(values):
    high = values.astype(BF16)
    return high, (values - high.astype(F32)).astype(BF16)


def both(high, low):
    return high.astype(F32) + low.astype(F32)


def cut_kernel(spot_ref, kept_ref, *refs):
    got, (own_ref, send_ref) = refs[:4], refs[4:]
    rows, width = own_ref.shape[0] // 2, got[0].shape[1]
    chunk = spot_ref[1]
    first, second = turn_bits(spot_ref)
    for spot, place in enumerate((chunk, chunk ^ second)):
        to = slice(spot * rows, (spot + 1) * rows)
        for i, piece in enumerate(got):
            columns = slice(i * width, (i + 1) * width)
            at = window(place, rows)
            own_ref[to, columns] = kept_ref[at, columns] + piece[at, :].astype(F32)
            at = window(place ^ first, rows)
            values = kept_ref[at, columns] + piece[at, :].astype(F32)
            send_ref[to, columns] = values.astype(BF16)


def middle_kernel(
    spot_ref, kept_ref, got_ref, base_ref, own_terms, got_terms, near_ref, send_ref, out_ref
):
    rows, width = near_ref.shape
    span = base_ref.shape[0]
    values = kept_ref[...] + got_ref[...].astype(F32)
    near_ref[...] = values[:, :width]
    terms = own_terms[:span, :].astype(F32) + got_terms[:span, :].astype(F32)
    out_ref[...] = (base_ref[...] + terms).astype(BF16)
    send_ref[: span // 2, :] = out_ref[window(spot_ref[2] % 2, span // 2), :]
    half = send_ref.shape[1]
    for i in range(width // half):
        at = span // 2 + i * rows
        columns = slice(width + i * half, width + (i + 1) * half)
        send_ref[at : at + rows, :] = values[:, columns].astype(BF16)


def settle_kernel(spot_ref, near_ref, got_ref, out_ref, own_ref, send_ref):
    rows, width = own_ref.shape
    span = out_ref.shape[0]
    out_ref[...] = got_ref[:span, :]
    half = got_ref.shape[1]
    for i in range(width // half):
        at, columns = span + 2 * i * rows, slice(i * half, (i + 1) * half)
        own_ref[:, columns] = near_ref[:rows, columns] + got_ref[at : at + rows, :].astype(F32)
        more = near_ref[rows:, columns] + got_ref[at + rows : at + 2 * rows, :].astype(F32)
        send_ref[:, columns] = more.astype(BF16)


def rows_kernel(spot_ref, own_ref, one_ref, two_ref, in_own, in_got, out_ref, in_ref):
    pair, bit, span = spot_ref[2] // 2, spot_ref[2] % 2, own_ref.shape[0]
    half = span // 2
    out_ref[window(pair, span), :] = own_ref[...].astype(F32)
    out_ref[window(2 * (1 - pair) + bit, half), :] = one_ref[...].astype(F32)
    out_ref[window(2 * (1 - pair) + 1 - bit, half), :] = two_ref[...].astype(F32)
    in_ref[window(pair, span), :] = in_own[...].astype(F32)
    in_ref[window(1 - pair, span), :] = in_got[...].astype(F32)


def cut_small_kernel(
    spot_ref, kept_ref, got_near, got_far, small_ref, own_ref, o1, o2, o3, sum_ref
):
    rows, width = own_ref.shape[0], small_ref.shape[1]
    whole = kept_ref.shape[0]
    for bits, out_ref in enumerate((own_ref, o1, o2, o3)):
        at = window(spot_ref[1] ^ bits, rows)
        for side, got_ref in enumerate((got_near, got_far)):
            columns = slice(side * width, (side + 1) * width)
            values = kept_ref[at, columns] + got_ref[at, :].astype(F32)
            out_ref[:rows, columns] = values.astype(out_ref.dtype)
    mine = both(*split_two(small_ref[...]))
    high, low = split_two(mine + both(got_near[whole:, :], got_far[whole:, :]))
    for out_ref in (o1, o2, o3):
        out_ref[rows:, :width] = high
        out_ref[rows:, width:] = low
    sum_ref[...] = both(high, low)


def shards_small_kernel(spot_ref, own_ref, g1, g2, g3, small_ref, kept_ref, send_ref):
    rows, width = kept_ref.shape
    got = [piece[:rows, :].astype(F32) for piece in (g1, g2, g3)]
    values = (own_ref[...] + got[0]) + (got[1] + got[2])
    kept_ref[...] = values[:, :width]
    send_ref[:rows, :] = values[:, width:].astype(BF16)
    count = small_ref.shape[0]
    got = [both(piece[rows:, :width], piece[rows:, width:]) for piece in (g1, g2, g3)]
    high, low = split_two((small_ref[...] + got[0]) + (got[1] + got[2]))
    send_ref[rows : rows + count, :] = high
    send_ref[rows + count :, :] = low


def owned_kernel(
    spot_ref, ffn_kept, ffn_got, kept_ref, sent_ref, got_ref, out_ref, small_ref
):
    rows, width = ffn_kept.shape
    out_ref[:, :width] = (ffn_kept[...] + ffn_got[...].astype(F32)).astype(BF16)
    out_ref[:, width:] = (kept_ref[...] + got_ref[:rows, :].astype(F32)).astype(BF16)
    count = small_ref.shape[0]
    top, end = slice(rows, rows + count), slice(rows + count, rows + 2 * count)
    mine = both(sent_ref[top, :], sent_ref[end, :])
    small_ref[...] = mine + both(got_ref[top, :], got_ref[end, :])


def own_kernel(spot_ref, p0, p1, p2, p3, up_ref, down_ref, qkv_ref, out_ref):
    rows, hidden, cols = p0.shape[0], up_ref.shape[1], out_ref.shape[1]
    for bits, piece in enumerate((p0, p1, p2, p3)):
        at = window(spot_ref[1] ^ bits, rows)
        up_ref[at, :] = piece[:, :hidden].astype(F32)
        down_ref[at, :] = piece[:, hidden : 2 * hidden].astype(F32)
        start = 2 * hidden
        for i in range(3):
            qkv_ref[i, at, :] = piece[:, start + i * cols : start + (i + 1) * cols].astype(F32)
        out_ref[at, :] = piece[:, start + 3 * cols :].astype(F32)


def sums_kernel(spot_ref, steps_ref, own_ref, got_ref, table_ref, up_ref, qv_ref, *refs):
    lines, rows_ref = refs[:-1], refs[-1]
    cols = qv_ref.shape[1]
    shard = spot_ref[2]
    rows_ref[...] = own_ref[...] + got_ref[...]
    table_ref[...] = jnp.zeros_like(table_ref)
    for place in range(steps_ref.shape[0]):
        at = pl.ds(steps_ref[place], 1)
        table_ref[at, :] = table_ref[at, :] + rows_ref[12 + place : 13 + place, :]
    up_ref[...] = rows_ref[pl.ds(8 + shard, 1), :]
    qv_ref[...] = rows_ref[6:8, window(shard, cols)]
    for i, line_ref in enumerate(lines):
        line_ref[...] = rows_ref[i : i + 1, :]


class Reduction:
    def __init__(self, order, kept, small):
        self.order, self.kept, self.small = order, kept, small
        self.rows, self.width = kept.shape[0] // 4, kept.shape[1]

    def cut(self, got):
        rows, width, more = self.rows, self.width, self.small.shape[0]
        self.own, *cuts, self.small = self.order.call(
            cut_small_kernel,
            [((rows, width), F32)]
            + [((rows + more, width), BF16)] * 3
            + [(self.small.shape, F32)],
            [self.kept, *got, self.small],
        )
        self.got = [self.order.swap(cuts[bits - 1], "ctx", bits) for bits in (1, 2, 3)]

    def shards(self):
        rows, width, more = self.rows, self.width // 2, 2 * self.small.shape[0]
        self.own, self.sent = self.order.call(
            shards_small_kernel,
            [((rows, width), F32), ((rows + more, width), BF16)],
            [self.own, *self.got, self.small],
        )
        self.got = self.order.swap(self.sent, "tp", 2)


def reduce_plainly(kept, given, chunk):
    whole = jnp.concatenate([kept, given.astype(F32)])
    mine = lax.psum_scatter(whole, "fsdp", scatter_dimension=0, tiled=True)
    quarter = lax.psum_scatter(mine, "ctx", scatter_dimension=0, tiled=True)
    width = quarter.shape[1] // 2
    far = lax.ppermute(quarter[:, width:], "tp", [(i, i ^ 2) for i in range(4)])
    return lax.all_gather(quarter[:, :width] + far, "ctx", axis=0, tiled=True)


def pieces_of(order, part, parts, rows):
    if parts == 2:
        return part, order.swap(part, "fsdp", 1)
    whole = lax.all_gather(part[:rows], "fsdp", axis=0, tiled=True)
    size = whole.shape[0] // 2
    return whole[:size], whole[size:]


def per_device(
    layer_input,
    timesteps,
    segment_ids,
    time_table,
    ln1_gain,
    ln1_bias,
    w_qkv,
    b_qv,
    w_out_t,
    b_out,
    ln2_gain,
    ln2_bias,
    w_up,
    b_up,
    w_down_t,
    b_down,
    out_grad,
    *,
    parts,
):
    span, width = layer_input.shape[1:]
    rows, cols = w_qkv.shape[1:]
    hidden = w_up.shape[1]
    size = width // 2
    core = lax.axis_index("fsdp")
    chunk = lax.axis_index("ctx")
    shard = lax.axis_index("tp")
    place = core if parts == 2 else 0 * core
    spot = jnp.stack([place, chunk, shard, 2 * core + shard // 2]).astype(jnp.int32)
    order = Order(spot, parts)
    line = lambda values: values.reshape(1, -1)
    dma = lambda count: pltpu.SemaphoreType.DMA((count,))

    pack, rest, quarter = order.call(
        pack_kernel,
        [
            ((rows + BIAS_ROWS, 4 * cols), BF16), ((rows, 2 * hidden), BF16),
            ((rows // 4 + PAD * (parts == 2), 2 * hidden), BF16),
        ],
        [timesteps, w_qkv, w_out_t, b_qv, line(b_up), w_up, w_down_t],
        far=range(7),
        scratch=[
            pltpu.VMEM(w_qkv.shape, F32),
            pltpu.VMEM(w_out_t.shape, F32),
            pltpu.VMEM(b_qv.shape, F32),
            pltpu.VMEM((1, hidden), F32),
            pltpu.VMEM(w_up.shape, F32),
            pltpu.VMEM(w_down_t.shape, F32),
            dma(6),
        ],
    )
    near = pieces_of(order, pack, parts, rows)
    pack_far = order.swap(pack, "tp", 2)
    stream, normed, seg, lines, cotan = order.call(
        stream_kernel,
        [
            ((span, width), F32), ((span, width), BF16), ((1, segment_ids.shape[1]), jnp.int32),
            ((8, width), F32), ((span, width), F32),
        ],
        [timesteps, layer_input, time_table, segment_ids, out_grad]
        + [line(v) for v in (ln1_gain, ln1_bias, ln2_gain, ln2_bias, b_out, b_down)],
        far=range(11),
        scratch=[
            pltpu.VMEM((span, width), F32),
            pltpu.VMEM((8, width), F32),
            pltpu.VMEM(segment_ids.shape, jnp.int32),
            pltpu.VMEM((6, 1, width), F32),
            dma(10),
        ],
    )
    projected = [((span, cols), BF16), ((span, 2 * cols), BF16)]
    more = [((span, cols), BF16), ((span + PAD, 2 * cols), BF16)]
    project = functools.partial(project_kernel, row=rows)
    q_near, kv_near = order.call(project, projected, [normed, *near, pack])
    kvs_near = [kv_near] + order.swap_three(kv_near, "ctx")
    rest_far = order.swap(quarter if parts == 2 else rest, "tp", 2)
    rest_near = pieces_of(order, rest, parts, rows)

    attended = [((span, cols), BF16), ((span, cols), F32)]
    pack_far, *kvs_near[1:] = hold(pack_far, *kvs_near[1:])
    far = pieces_of(order, pack_far, parts, rows)
    mixed_near, lse_near = order.call(
        attend_one_kernel, attended, [seg, q_near, *kvs_near], cost=QUICK
    )
    q_far, kv_far = order.call(project, more, [normed, *far, pack_far], cost=QUICK)
    kvs_far = [kv_far] + order.swap_three(kv_far, "ctx")
    if parts == 2:
        rest_turn = order.swap_turn(rest_far, 0)
    mixed_far, lse_far, given = order.call(
        attend_two_kernel,
        attended + [((span + PAD, width), BF16)],
        [seg, q_far, *kvs_far, mixed_near, *near, *far],
    )
    got = order.swap(given, "tp", 1)
    if parts == 2:
        rest_one = order.call(
            stack_kernel, [((rows // 2, 2 * hidden), BF16)], [rest_far, rest_turn], cost=QUICK
        )[0]
        rest_two = order.swap_turn(rest_one, 1)
        rest_far = [
            rest_one, rest_two, order.swap(rest_one, "fsdp", 1), order.swap(rest_two, "fsdp", 1)
        ]
    else:
        rest_far = pieces_of(order, rest_far, parts, rows)

    acts = [((span, hidden), BF16), ((span, hidden), BF16)]
    back_near, ffn_near, out_base, resid, normed_two, act_n, pre_n, low, up_near = order.call(
        functools.partial(ffn_near_kernel, row=rows),
        [((span, width), F32)] * 4
        + [((span, width), BF16), *acts, ((span, width), BF16), ((1, hidden), F32)],
        [stream, given, got, cotan, lines, pack, *rest_near],
    )
    act_f, pre_f, up_far, back, ffn_terms = order.call(
        functools.partial(ffn_far_kernel, row=rows),
        [*acts, ((1, hidden), F32), ((span + PAD, width), BF16), ((span, width), BF16)],
        [normed_two, low, back_near, ffn_near, pack_far, *rest_far],
        scratch=[pltpu.VMEM((size, 2 * hidden), BF16)] * 2,
    )
    back_got = order.swap(back, "tp", 1)
    ffn_kept, *ffn_sent = order.call(
        ffn_grads_kernel,
        [((size, 4 * hidden), F32)] + [((size, hidden), BF16)] * 4,
        [normed_two, low, act_n, pre_n, act_f, pre_f],
    )
    if parts == 2:
        ffn_got = [order.swap(piece, "fsdp", 1) for piece in ffn_sent]
        ffn_own, ffn_cut = order.call(
            cut_kernel,
            [((rows // 2, 4 * hidden), F32), ((rows // 2, 4 * hidden), BF16)],
            [ffn_kept, *ffn_got],
            cost=QUICK,
        )
        ffn_turn = order.swap_turn(ffn_cut, 0)
    dq, own, *shares, resid_grad, low_all, resid_rows = order.call(
        pull_kernel,
        [((span, 2 * cols), F32), ((span, 4 * cols), F32)]
        + [((span + PAD, 4 * cols), BF16)] * 3
        + [((span, width), F32), ((span, width), BF16), ((4, width), F32)],
        [
            seg, q_near, lse_near, *kvs_near, q_far, lse_far, *kvs_far, back, back_got, resid,
            cotan, lines, *near, *far,
        ],
        scratch=[pltpu.VMEM((2, span, width), F32)],
        limit=6,
    )
    shared = [order.swap(shares[bits - 1], "ctx", bits) for bits in (1, 2, 3)]

    terms_got = order.swap(ffn_terms, "tp", 1)
    if parts == 2:
        ffn_near, sent, out_low = order.call(
            middle_kernel,
            [
                ((rows // 2, 2 * hidden), F32), ((span // 2 + rows, width), BF16),
                ((span, width), BF16),
            ],
            [ffn_own, ffn_turn, out_base, ffn_terms, terms_got],
            cost=QUICK,
        )
        sent_got = order.swap(sent, "tp", 2)
    else:
        out_low = order.call(
            add_pair_kernel, [((span, width), BF16)], [out_base, ffn_terms, terms_got]
        )[0]
        out_got = order.swap(out_low, "tp", 2)

    seqs = 2 * parts
    small_rows = -(-(12 + seqs) // 16) * 16
    in_terms, small, attention_kept, *attention_sent = order.call(
        input_kernel,
        [
            ((span, width), BF16), ((small_rows, width), F32),
            ((size, 8 * cols), F32), ((size + small_rows, 4 * cols), BF16),
            ((size + small_rows, 4 * cols), BF16),
        ],
        [
            stream, lines, resid_rows, up_near, up_far, dq, own, *shared, *near, *far,
            normed, low_all, mixed_near, mixed_far,
        ],
        scratch=[pltpu.VMEM((span, 6 * cols), BF16), pltpu.VMEM((span, width), F32)],
    )
    order.cost = QUICK
    if parts == 2:
        attention_far = [order.swap(piece, "fsdp", 1) for piece in attention_sent]
    in_got = order.swap(in_terms, "tp", 1)
    if parts == 2:
        attention_sum = Reduction(order, attention_kept, small)
        attention_sum.cut(attention_far)
        out_half, ffn_own, ffn_cut = order.call(
            settle_kernel,
            [
                ((span // 2, width), BF16), ((rows // 4, 2 * hidden), F32),
                ((rows // 4, 2 * hidden), BF16),
            ],
            [ffn_near, sent_got],
            cost=COST,
        )
        ffn_turn = order.swap_turn(ffn_cut, 1)
        out_more = order.swap(out_half, "tp", 1)
        attention_sum.shards()
    else:
        output = order.call(pair_kernel, [((2 * span, width), F32)], [out_low, out_got])[0]
    in_low = order.call(
        add_pair_kernel, [((span, width), BF16)], [resid_grad, in_terms, in_got]
    )[0]
    in_far = order.swap(in_low, "tp", 2)
    if parts == 2:
        attention = attention_sum
        owned, small = order.call(
            owned_kernel,
            [((rows // 4, 2 * hidden + 4 * cols), BF16), (small.shape, F32)],
            [ffn_own, ffn_turn, attention.own, attention.sent, attention.got],
        )
        small_got = order.swap(small, "tp", 1)
        pieces = [owned] + order.swap_three(owned, "ctx")
    if parts == 2:
        output, grad_input = order.call(
            rows_kernel,
            [((2 * span, width), F32)] * 2,
            [out_low, out_half, out_more, in_low, in_far],
        )
    else:
        grad_input = order.call(pair_kernel, [((2 * span, width), F32)], [in_low, in_far])[0]
    if parts == 2:
        bits = near[1][rows : rows + 9 : 3, 2 * cols : 2 * cols + 2].astype(F32)
        far_steps = jnp.sum(bits, axis=0).astype(jnp.int32)
        steps = jnp.where(
            core == 0,
            jnp.concatenate([timesteps, far_steps]),
            jnp.concatenate([far_steps, timesteps]),
        )
    else:
        ffn_sent = jnp.concatenate(ffn_sent, axis=1)
        both_grads = reduce_plainly(ffn_kept, ffn_sent, chunk)
        grads_up, grads_down = both_grads[:, :hidden], both_grads[:, hidden:]
        small = lax.psum(small, ("fsdp", "ctx", "tp"))
        small_got = jnp.zeros_like(small)
        steps = lax.all_gather(timesteps, "fsdp", axis=0, tiled=True)
    table, up_line, qv_lines, *sums = order.call(
        sums_kernel,
        [(time_table.shape, F32), ((1, hidden), F32), ((2, cols), F32)] + [((1, width), F32)] * 6,
        [steps, small, small_got],
        scratch=[pltpu.VMEM(small.shape, F32)],
    )
    sums = [values.reshape(-1) for values in sums]
    if parts == 2:
        grads_up, grads_down, grads_qkv, grads_out = order.call(
            own_kernel,
            [((rows, hidden), F32)] * 2 + [((3, rows, cols), F32), ((rows, cols), F32)],
            pieces,
        )
    else:
        attention_sent = jnp.concatenate(attention_sent, axis=1)[:size]
        every = reduce_plainly(attention_kept, attention_sent, chunk)
        grads_qkv = jnp.stack([every[:, i * cols : (i + 1) * cols] for i in range(3)])
        grads_out = every[:, 3 * cols :]

    shape = layer_input.shape
    return (
        output.reshape(shape),
        grad_input.reshape(shape),
        table,
        sums[0],
        sums[1],
        grads_qkv,
        qv_lines,
        grads_out,
        sums[4],
        sums[2],
        sums[3],
        grads_up,
        up_line.reshape(-1),
        grads_down,
        sums[5],
    )


def solution(mesh):
    placed = (
        P("fsdp", "ctx", None),
        P("fsdp"),
        P("fsdp", None),
        P(),
        P(),
        P(),
        P(None, "fsdp", "tp"),
        P(None, "tp"),
        P("fsdp", "tp"),
        P(),
        P(),
        P(),
        P("fsdp", "tp"),
        P("tp"),
        P("fsdp", "tp"),
        P(),
        P("fsdp", "ctx", None),
    )
    return jax.shard_map(
        functools.partial(per_device, parts=mesh.shape["fsdp"]),
        mesh=mesh,
        in_specs=placed,
        out_specs=(
            P("fsdp", "ctx", None),
            P("fsdp", "ctx", None),
            P(),
            P(),
            P(),
            P(None, "fsdp", "tp"),
            P(None, "tp"),
            P("fsdp", "tp"),
            P(),
            P(),
            P(),
            P("fsdp", "tp"),
            P("tp"),
            P("fsdp", "tp"),
            P(),
        ),
        check_vma=False,
    )
```

```python
import functools
import jax
import jax.numpy as jnp
from jax import lax
from jax.experimental import pallas as pl
from jax.experimental.pallas import tpu as pltpu
from jax.sharding import PartitionSpec as P

HEAD_DIM = 64
SCALE = HEAD_DIM ** (-0.5)
EPSILON = 1e-05
NEGATIVE = -1e30
F32 = jnp.float32
BF16 = jnp.bfloat16
BIAS_ROWS = 16
PAD = 16
CUBE = 0.044715
ROOT = 0.7978845608028654
COST, QUICK, LONG = 8_000_000_000, 1_000, 20_000_000_000
VMEM = pl.BlockSpec(memory_space=pltpu.VMEM)
SMEM = pl.BlockSpec(memory_space=pltpu.SMEM)


def dot_nn(left, right):
    return lax.dot_general(left, right, (((1,), (0,)), ((), ())), preferred_element_type=F32)


def dot_nt(left, right):
    return lax.dot_general(left, right, (((1,), (1,)), ((), ())), preferred_element_type=F32)


def dot_tn(left, right):
    return lax.dot_general(left, right, (((0,), (0,)), ((), ())), preferred_element_type=F32)


def total(values):
    return functools.reduce(jnp.add, values)


def norm_parts(values):
    centre = values - jnp.mean(values, axis=-1, keepdims=True)
    spread = jnp.mean(centre * centre, axis=-1, keepdims=True)
    inverse = lax.rsqrt(spread + EPSILON)
    return centre * inverse, inverse


def norm_back(grad, hat, inverse, gain):
    scaled = grad * gain
    mean_one = jnp.mean(scaled, axis=-1, keepdims=True)
    mean_two = jnp.mean(scaled * hat, axis=-1, keepdims=True)
    return inverse * (scaled - mean_one - hat * mean_two)


def column_sum(values):
    return jnp.sum(values, axis=0, keepdims=True)


def window(index, size):
    return pl.ds(pl.multiple_of(index * size, size), size)


def halves(spot_ref, size):
    return window(spot_ref[0], size), window(1 - spot_ref[0], size)


def hold(*values):
    return lax.optimization_barrier(values)


class Order:
    def __init__(self, spot, parts):
        self.spot, self.parts, self.cost = spot, parts, COST

    def call(self, kernel, outs, operands, *, far=(), kept=(), alias=None, scratch=(), limit=5, cost=None):
        specs = [
            SMEM if operand.ndim == 1
            else pl.BlockSpec(memory_space=pltpu.HBM if i in far else pltpu.VMEM)
            for i, operand in enumerate(operands)
        ]
        operands = [
            pltpu.with_memory_space_constraint(operand, pltpu.HBM) if i in far else operand
            for i, operand in enumerate(operands)
        ]
        count = len(operands)

        def body(*refs):
            kernel(refs[count], *refs[:count], *refs[count + 1 :])

        results = pl.pallas_call(
            body,
            out_shape=tuple(jax.ShapeDtypeStruct(shape, dtype) for shape, dtype in outs),
            in_specs=specs + [SMEM],
            out_specs=tuple(
                pl.BlockSpec(memory_space=pltpu.HBM) if i in kept else VMEM
                for i in range(len(outs))
            ),
            input_output_aliases=alias or {},
            scratch_shapes=list(scratch),
            compiler_params=pltpu.CompilerParams(vmem_limit_bytes=limit << 20),
            cost_estimate=pl.CostEstimate(
                flops=cost or self.cost, bytes_accessed=1 << 16, transcendentals=0
            ),
        )(*operands, self.spot)
        first, self.spot = hold(results[0], self.spot)
        return [first, *results[1:]]

    def swap(self, values, axis, bits):
        values, self.spot = hold(values, self.spot)
        size = 2 if axis == "fsdp" else 4
        with jax.named_scope("swap_%s_%d" % (axis, bits)):
            return lax.ppermute(values, axis, [(i, i ^ bits) for i in range(size)])

    def swap_three(self, values, axis):
        return [self.swap(values, axis, bits) for bits in (1, 2, 3)]

    def swap_turn(self, values, turn):
        if self.parts != 2:
            return self.swap(values, "ctx", 1 + turn)
        values, self.spot = hold(values, self.spot)
        pairs = [
            (4 * core + i, 4 * core + (i ^ (1 + (core + turn) % 2)))
            for core in range(2)
            for i in range(4)
        ]
        with jax.named_scope("swap_turn_%d" % turn):
            return lax.ppermute(values, ("fsdp", "ctx"), pairs)


def clear_below(ref, rows):
    if ref.shape[0] > rows:
        ref[rows:, :] = jnp.zeros((ref.shape[0] - rows, ref.shape[1]), ref.dtype)


def fetch(copies, sems):
    started = [
        pltpu.make_async_copy(source, target, sems.at[i])
        for i, (source, target) in enumerate(copies)
    ]
    for copy in started:
        copy.start()
    for copy in started:
        copy.wait()


def split_three(values):
    high = values.astype(BF16)
    rest = values - high.astype(F32)
    middle = rest.astype(BF16)
    return [high, middle, (rest - middle.astype(F32)).astype(BF16)]


def pack_kernel(
    spot_ref, steps_ref, w_hbm, out_hbm, qv_hbm, up_bias_hbm, pack_ref, qkv_ref, out_ref,
    w_ref, o_ref, qv_ref, up_bias_ref, sems,
):
    rows, cols = w_ref.shape[1:]
    fetch(
        [(w_hbm, w_ref), (out_hbm, o_ref), (qv_hbm, qv_ref), (up_bias_hbm, up_bias_ref)], sems
    )
    for i in range(3):
        pack_ref[:rows, i * cols : (i + 1) * cols] = w_ref[i].astype(BF16)
    pack_ref[:rows, 3 * cols :] = o_ref[...].astype(BF16)
    lanes = lax.broadcasted_iota(jnp.int32, (1, cols), 1)
    steps = jnp.zeros((1, cols), F32)
    for i in range(steps_ref.shape[0]):
        steps = jnp.where(lanes == i, steps_ref[i].astype(F32), steps)
    fill = jnp.zeros((1, cols), F32)
    up_bias = up_bias_ref[...]
    lines = [
        jnp.concatenate([qv_ref[0:1], qv_ref[1:2], steps, fill], axis=1),
        jnp.concatenate([up_bias[:, : 2 * cols], fill, fill], axis=1),
        jnp.concatenate([up_bias[:, 2 * cols :], fill, fill], axis=1),
    ]
    parts = split_three(jnp.concatenate(lines, axis=0))
    fill = jnp.zeros((BIAS_ROWS - 9, 4 * cols), F32)
    stack = jnp.concatenate([v.astype(F32) for v in parts] + [fill], axis=0)
    pack_ref[rows:, :] = stack.astype(BF16)
    qkv_ref[...] = pack_ref[:, : 3 * cols]
    out_ref[...] = pack_ref[:rows, 3 * cols :]


def pack_rest_kernel(
    spot_ref, own_out, up_hbm, down_hbm, cotan_hbm, rest_ref, side_ref, cotan_ref,
    up_ref, down_ref, sems,
):
    rows, hidden = up_ref.shape
    cols = own_out.shape[1]
    pair = spot_ref[2] // 2
    fetch([(up_hbm, up_ref), (down_hbm, down_ref), (cotan_hbm.at[pair], cotan_ref)], sems)
    rest_ref[:, :hidden] = up_ref[...].astype(BF16)
    rest_ref[:, hidden:] = down_ref[...].astype(BF16)
    if side_ref.shape[0] == rows:
        side_ref[...] = own_out[...]
        return
    quarter, fold = rows // 4, rows // 8
    mine = window(spot_ref[1], quarter)
    side_ref[:quarter, :hidden] = up_ref[mine, :].astype(BF16)
    side_ref[:quarter, hidden:] = down_ref[mine, :].astype(BF16)
    for i in range(8):
        block = own_out[i * fold : (i + 1) * fold, :]
        side_ref[quarter : quarter + fold, i * cols : (i + 1) * cols] = block
    clear_below(side_ref, quarter + fold)


def unpack_kernel(spot_ref, side_ref, quarter_ref, out_ref):
    rows, cols = out_ref.shape
    quarter, fold = rows // 4, rows // 8
    quarter_ref[...] = side_ref[:quarter, :]
    for i in range(8):
        block = side_ref[quarter : quarter + fold, i * cols : (i + 1) * cols]
        out_ref[i * fold : (i + 1) * fold, :] = block


def bias_lines(pack_ref, row):
    bits = pack_ref[row : row + BIAS_ROWS, :].astype(F32)
    lines = bits[0:3] + bits[3:6] + bits[6:9]
    half = 4 * HEAD_DIM
    return lines[0:1], jnp.concatenate([lines[1:2, :half], lines[2:3, :half]], axis=1)


def out_part(ref, size):
    cols = 2 * HEAD_DIM
    return ref[:size, ref.shape[1] - cols :]


def add_pair_kernel(spot_ref, base_ref, own_ref, got_ref, out_ref):
    span = base_ref.shape[0]
    terms = own_ref[:span, :].astype(F32) + got_ref[:span, :].astype(F32)
    out_ref[...] = (base_ref[...] + terms).astype(BF16)


def open_kernel(
    spot_ref, steps_ref, x_hbm, table_hbm, seg_hbm, g1, b1, g2, b2, bo, bd, one_ref, two_ref,
    bias_ref, q_ref, kv_ref, stream_ref, normed_ref, seg_ref, lines_ref,
    x_ref, table_ref, ids_ref, line_ref, sems, *, row,
):
    pair = spot_ref[2] // 2
    step = steps_ref[pair]
    block = pl.multiple_of(step // 8 * 8, 8)
    copies = [
        (x_hbm.at[pair], x_ref),
        (table_hbm.at[pl.ds(block, 8), :], table_ref),
        (seg_hbm, ids_ref),
    ]
    vectors = (g1, b1, g2, b2, bo, bd)
    fetch(copies + [(v, line_ref.at[i]) for i, v in enumerate(vectors)], sems)
    for i in range(len(vectors)):
        lines_ref[i : i + 1, :] = line_ref[i]
    seg_ref[...] = ids_ref[pl.ds(pair, 1), :]
    stream = x_ref[...] + table_ref[pl.ds(step % 8, 1), :]
    hat, _ = norm_parts(stream)
    stream_ref[...] = stream
    normed_ref[...] = (hat * line_ref[0] + line_ref[1]).astype(BF16)
    project_kernel(spot_ref, normed_ref, one_ref, two_ref, bias_ref, q_ref, kv_ref, row=row)


def project_kernel(spot_ref, normed_ref, one_ref, two_ref, bias_ref, q_ref, kv_ref, *, row):
    span, cols = q_ref.shape
    size = normed_ref.shape[1] // 2
    one, two = halves(spot_ref, size)
    raw = dot_nn(normed_ref[:, one], one_ref[:size, : 3 * cols])
    raw = raw + dot_nn(normed_ref[:, two], two_ref[:size, : 3 * cols])
    line, _ = bias_lines(bias_ref, row)
    q_bias, v_bias = line[:, :cols], line[:, cols : 2 * cols]
    q_ref[...] = (raw[:, :cols] + q_bias).astype(BF16)
    kv_ref[:span, :cols] = raw[:, cols : 2 * cols].astype(BF16)
    kv_ref[:span, cols:] = (raw[:, 2 * cols :] + v_bias).astype(BF16)
    clear_below(kv_ref, span)


def mask_biases(spot_ref, seg_ref, span):
    chunk = spot_ref[1]
    ids = [seg_ref[:, window(chunk ^ step, span)] for step in range(seg_ref.shape[1] // span)]
    own = jnp.broadcast_to(ids[0], (span, span)).T
    return [
        jnp.where(own == jnp.broadcast_to(step_ids, (span, span)), 0.0, NEGATIVE)
        for step_ids in ids
    ]


def lane_mask(shape, head):
    return (lax.broadcasted_iota(jnp.int32, shape, 1) // HEAD_DIM) == head


def attend_forward(spot_ref, seg_ref, q_ref, kvs, mixed_ref, lse_ref):
    span, width = q_ref.shape
    biases = mask_biases(spot_ref, seg_ref, span)
    query = q_ref[...]
    mixed, lse = None, None
    for head in range(width // HEAD_DIM):
        mine = lane_mask((span, width), head)
        masked = jnp.where(mine, query, jnp.zeros_like(query))
        scores = [
            dot_nt(masked, kv[:span, :width]) * SCALE + bias for kv, bias in zip(kvs, biases)
        ]
        top = functools.reduce(
            jnp.maximum, [jnp.max(block, axis=-1, keepdims=True) for block in scores]
        )
        grown = [jnp.exp(block - top) for block in scores]
        mass = total([jnp.sum(block, axis=-1, keepdims=True) for block in grown])
        share = 1.0 / mass
        out = total(
            [
                dot_nn((block * share).astype(BF16), kv[:span, width:])
                for block, kv in zip(grown, kvs)
            ]
        )
        log_mass = jnp.broadcast_to(top + jnp.log(mass), (span, width))
        mixed = out if head == 0 else jnp.where(mine, out, mixed)
        lse = log_mass if head == 0 else jnp.where(mine, log_mass, lse)
    mixed_ref[...] = mixed.astype(BF16)
    lse_ref[...] = lse


def attend_one_kernel(spot_ref, seg_ref, q_ref, kv0, kv1, kv2, kv3, mixed_ref, lse_ref):
    attend_forward(spot_ref, seg_ref, q_ref, (kv0, kv1, kv2, kv3), mixed_ref, lse_ref)


def attend_two_kernel(
    spot_ref, seg_ref, q_ref, kv0, kv1, kv2, kv3, near_ref, one_n, two_n, one_f, two_f,
    mixed_ref, lse_ref, given_ref,
):
    attend_forward(spot_ref, seg_ref, q_ref, (kv0, kv1, kv2, kv3), mixed_ref, lse_ref)
    size = given_ref.shape[1] // 2
    one, two = halves(spot_ref, size)
    near, far = near_ref[...], mixed_ref[...]
    for columns, near_w, far_w in ((one, one_n, one_f), (two, two_n, two_f)):
        terms = dot_nt(near, out_part(near_w, size)) + dot_nt(far, out_part(far_w, size))
        given_ref[: near.shape[0], columns] = terms.astype(BF16)
    clear_below(given_ref, near.shape[0])


def stack_kernel(spot_ref, one_ref, two_ref, out_ref):
    rows = out_ref.shape[0] // 2
    out_ref[:rows, :] = one_ref[:rows, :]
    out_ref[rows:, :] = two_ref[:rows, :]


def gelu_parts(x):
    square = x * x
    curve = jnp.tanh(ROOT * (x + CUBE * (x * square)))
    half = 0.5 * (1.0 + curve)
    slope = half + 0.5 * x * (1.0 - curve * curve) * (ROOT * (1.0 + 3.0 * CUBE * square))
    return x * half, slope


def ffn_side(
    normed_ref, low_ref, bias, first, second, columns, act_ref, pre_ref, sum_ref, *sums
):
    hidden = act_ref.shape[1]
    one, two = columns
    pre = dot_nn(normed_ref[:, one], first[:, :hidden])
    pre = pre + dot_nn(normed_ref[:, two], second[:, :hidden]) + bias
    value, slope = gelu_parts(pre)
    grad = dot_nn(low_ref[:, one], first[:, hidden:])
    grad = (grad + dot_nn(low_ref[:, two], second[:, hidden:])) * slope
    sum_ref[...] = column_sum(grad)
    act_ref[...] = value.astype(BF16)
    pre_ref[...] = grad.astype(BF16)
    act, pre_low = act_ref[...], pre_ref[...]
    for at, weights in zip(columns, (first, second)):
        back = dot_nt(pre_low, weights[:, :hidden])
        down = dot_nt(act, weights[:, hidden:])
        if len(sums) == 2:
            back_ref, out_ref = sums
        else:
            back_near, out_near, back_ref, out_ref = sums
            back, down = back + back_near[:, at], down + out_near[:, at]
        back_ref[: act.shape[0], at] = back.astype(back_ref.dtype)
        out_ref[: act.shape[0], at] = down.astype(out_ref.dtype)
    clear_below(sums[-2], act.shape[0])
    clear_below(sums[-1], act.shape[0])


def ffn_near_kernel(
    spot_ref, stream_ref, mine_ref, got_ref, cotan_ref, lines_ref, pack_ref, first, second,
    back_ref, ffn_ref, out_ref, resid_ref, normed_ref, act_ref, pre_ref, low_ref, sum_ref, *, row,
):
    span = stream_ref.shape[0]
    terms = mine_ref[:span, :].astype(F32) + got_ref[:span, :].astype(F32)
    resid = stream_ref[...] + terms + lines_ref[4:5, :]
    resid_ref[...] = resid
    out_ref[...] = resid + lines_ref[5:6, :]
    hat, _ = norm_parts(resid)
    normed_ref[...] = (hat * lines_ref[2:3, :] + lines_ref[3:4, :]).astype(BF16)
    low_ref[...] = cotan_ref[...].astype(BF16)
    ffn_side(
        normed_ref, low_ref, bias_lines(pack_ref, row)[1], first, second,
        halves(spot_ref, first.shape[0]), act_ref, pre_ref, sum_ref, back_ref, ffn_ref,
    )


def ffn_far_kernel(spot_ref, normed_ref, low_ref, back_near, ffn_near, pack_ref, *refs, row):
    count = len(refs) - 7
    pieces, outs, (first, second) = refs[:count], refs[count:-2], refs[-2:]
    if count == 2:
        first, second = pieces
    else:
        rows = pieces[0].shape[0] // 2
        turn, other = turn_bits(spot_ref)
        for target, pairs, bits in (
            (first, pieces[:2], (0, turn, other, 3)),
            (second, pieces[2:], (0, other, turn, 3)),
        ):
            for i in range(4):
                block = pairs[i // 2][i % 2 * rows : (i % 2 + 1) * rows, :]
                target[window(spot_ref[1] ^ bits[i], rows), :] = block
    act_ref, pre_ref, sum_ref, back_ref, ffn_ref = outs
    ffn_side(
        normed_ref, low_ref, bias_lines(pack_ref, row)[1], first, second,
        halves(spot_ref, first.shape[0]), act_ref, pre_ref, sum_ref, back_near, ffn_near,
        back_ref, ffn_ref,
    )


def ffn_grads_kernel(
    spot_ref, normed_ref, low_ref, act_n, pre_n, act_f, pre_f, kept_ref, *given
):
    hidden = act_n.shape[1]
    one, two = halves(spot_ref, normed_ref.shape[1] // 2)
    for columns in (two, one):
        normed, low = normed_ref[:, columns], low_ref[:, columns]
        for i, (left, right) in enumerate(((normed, pre_n), (low, act_n), (normed, pre_f), (low, act_f))):
            grads = dot_tn(left, right[...])
            if columns is one:
                kept_ref[:, i * hidden : (i + 1) * hidden] = grads
            else:
                given[i][...] = grads.astype(BF16)


def resid_part(
    spot_ref, mine_ref, got_ref, resid_ref, cotan_ref, lines_ref, grad_ref, low_ref, rows_ref,
    work_ref,
):
    half = resid_ref.shape[0] // 2
    mine = window(spot_ref[2] % 2, half)
    span = resid_ref.shape[0]
    grad = mine_ref[:span, :].astype(F32) + got_ref[:span, :].astype(F32)
    hat, inverse = norm_parts(resid_ref[...])
    resid_grad = cotan_ref[...] + norm_back(grad, hat, inverse, lines_ref[2:3, :])
    grad_ref[...] = resid_grad
    low_ref[...] = resid_grad.astype(BF16)
    work_ref[0] = grad * hat
    work_ref[1] = grad
    sums = [work_ref[0, mine, :], work_ref[1, mine, :], grad_ref[mine, :], cotan_ref[mine, :]]
    rows_ref[...] = jnp.concatenate([column_sum(v) for v in sums], axis=0)


def attend_backward(spot_ref, seg_ref, q_ref, grad, lse_ref, kvs, dq_ref, outs, side):
    span, width = q_ref.shape
    biases = mask_biases(spot_ref, seg_ref, span)
    query = q_ref[...]
    dq, dks, dvs = None, [None] * 4, [None] * 4
    for head in range(width // HEAD_DIM):
        mine = lane_mask((span, width), head)
        masked_q = jnp.where(mine, query, jnp.zeros_like(query))
        masked_g = jnp.where(mine, grad, jnp.zeros_like(grad))
        lse = lse_ref[:, head * HEAD_DIM : head * HEAD_DIM + 1]
        probs = [
            jnp.exp(dot_nt(masked_q, kv[:span, :width]) * SCALE + bias - lse)
            for kv, bias in zip(kvs, biases)
        ]
        grads = [dot_nt(masked_g, kv[:span, width:]) for kv in kvs]
        inner = total([jnp.sum(p * g, axis=-1, keepdims=True) for p, g in zip(probs, grads)])
        raws = [(p * (g - inner) * SCALE).astype(BF16) for p, g in zip(probs, grads)]
        head_dq = total([dot_nn(raw, kv[:span, :width]) for raw, kv in zip(raws, kvs)])
        dq = head_dq if head == 0 else jnp.where(mine, head_dq, dq)
        for step in range(4):
            head_dk = dot_tn(raws[step], query)
            head_dv = dot_tn(probs[step].astype(BF16), grad)
            dks[step] = head_dk if head == 0 else jnp.where(mine, head_dk, dks[step])
            dvs[step] = head_dv if head == 0 else jnp.where(mine, head_dv, dvs[step])
    dq_ref[:, side * width : (side + 1) * width] = dq
    at = 2 * side * width
    for step in range(4):
        outs[step][:span, at : at + width] = dks[step].astype(outs[step].dtype)
        outs[step][:span, at + width : at + 2 * width] = dvs[step].astype(outs[step].dtype)


def pull_kernel(
    spot_ref, seg_ref, q_n, lse_n, n0, n1, n2, n3, q_f, lse_f, f0, f1, f2, f3,
    mine_ref, got_ref, resid_ref, cotan_ref, lines_ref, one_n, two_n, one_f, two_f,
    dq_ref, own_ref, out1, out2, out3, grad_ref, low_ref, rows_ref, work_ref,
):
    size = low_ref.shape[1] // 2
    resid_part(
        spot_ref, mine_ref, got_ref, resid_ref, cotan_ref, lines_ref, grad_ref, low_ref, rows_ref,
        work_ref,
    )
    one, two = halves(spot_ref, size)
    outs = (own_ref, out1, out2, out3)
    near = (q_n, lse_n, (n0, n1, n2, n3), one_n, two_n)
    far = (q_f, lse_f, (f0, f1, f2, f3), one_f, two_f)
    for side, (q_ref, lse_ref, kvs, first, second) in enumerate((near, far)):
        grad = dot_nn(low_ref[:, one], out_part(first, size))
        grad = grad + dot_nn(low_ref[:, two], out_part(second, size))
        attend_backward(
            spot_ref, seg_ref, q_ref, grad.astype(BF16), lse_ref, kvs, dq_ref, outs, side
        )
    for out_ref in (out1, out2, out3):
        clear_below(out_ref, q_n.shape[0])


def input_kernel(
    spot_ref, stream_ref, lines_ref, rows_ref, up_near, up_far, dq_ref, own_ref, g1, g2, g3,
    one_n, two_n, one_f, two_f, normed_ref, low_ref, near_ref, far_ref,
    given_ref, small_ref, w_kept_ref, w_near_ref, w_far_ref, w_out_ref, pulled_ref, terms_ref,
):
    span, width = stream_ref.shape
    cols = dq_ref.shape[1] // 2
    size = width // 2
    shard, slot = spot_ref[2], spot_ref[3]
    far = shard ^ 2
    one, two = halves(spot_ref, size)
    small_ref[...] = jnp.zeros_like(small_ref)
    parts = [ref[:span, :].astype(F32) for ref in (g1, g2, g3)]
    got = (own_ref[...] + parts[0]) + (parts[1] + parts[2])
    for side, (place, up_sum) in enumerate(((shard, up_near), (far, up_far))):
        dq = dq_ref[:, side * cols : (side + 1) * cols]
        dkv = got[:, 2 * side * cols : 2 * (side + 1) * cols]
        at = side * 3 * cols
        pulled_ref[:, at : at + cols] = dq.astype(BF16)
        pulled_ref[:, at + cols : at + 3 * cols] = dkv.astype(BF16)
        small_ref[6:7, window(place, cols)] = column_sum(dq)
        small_ref[7:8, window(place, cols)] = column_sum(dkv[:, cols:])
        small_ref[pl.ds(8 + place, 1), :] = up_sum[...]
    for columns, near_w, far_w in ((one, one_n, one_f), (two, two_n, two_f)):
        back = dot_nt(pulled_ref[:, : 3 * cols], near_w[:size, : 3 * cols])
        back = back + dot_nt(pulled_ref[:, 3 * cols :], far_w[:size, : 3 * cols])
        terms_ref[:, columns] = back
    back = terms_ref[...]
    hat, inverse = norm_parts(stream_ref[...])
    small_ref[0:1, :] = column_sum(back * hat)
    small_ref[1:2, :] = column_sum(back)
    small_ref[2:6, :] = rows_ref[...]
    grad = norm_back(back, hat, inverse, lines_ref[0:1, :])
    small_ref[pl.ds(12 + slot, 1), :] = column_sum(grad) + rows_ref[2:3, :]
    given_ref[...] = grad.astype(BF16)
    given = (w_near_ref, w_far_ref)
    for columns in (two, one):
        normed, low = normed_ref[:, columns], low_ref[:, columns]
        for side, mixed in enumerate((near_ref, far_ref)):
            at, start = side * 3 * cols, side * 4 * cols
            qkv = dot_tn(normed, pulled_ref[:, at : at + 3 * cols])
            out = dot_tn(low, mixed[...])
            if columns is one:
                w_kept_ref[:, start : start + 3 * cols] = qkv
                w_kept_ref[:, start + 3 * cols : start + 4 * cols] = out
            else:
                given[side][:size, :] = qkv.astype(BF16)
                w_out_ref[:size, side * cols : (side + 1) * cols] = out.astype(BF16)
    both_parts = jnp.concatenate(split_two(small_ref[...]), axis=1)
    w_near_ref[size:, :] = both_parts[:, : 3 * cols]
    w_far_ref[size:, :] = both_parts[:, 3 * cols : 6 * cols]
    w_out_ref[size:, :] = both_parts[:, 6 * cols :]


def turn_bits(spot_ref):
    return 1 + spot_ref[0], 2 - spot_ref[0]


def split_two(values):
    high = values.astype(BF16)
    return high, (values - high.astype(F32)).astype(BF16)


def both(high, low):
    return high.astype(F32) + low.astype(F32)


def cut_kernel(spot_ref, kept_ref, *refs):
    got, (own_ref, send_ref) = refs[:4], refs[4:]
    rows, width = own_ref.shape[0] // 2, got[0].shape[1]
    chunk = spot_ref[1]
    first, second = turn_bits(spot_ref)
    for spot, place in enumerate((chunk, chunk ^ second)):
        to = slice(spot * rows, (spot + 1) * rows)
        for i, piece in enumerate(got):
            columns = slice(i * width, (i + 1) * width)
            at = window(place, rows)
            own_ref[to, columns] = kept_ref[at, columns] + piece[at, :].astype(F32)
            at = window(place ^ first, rows)
            values = kept_ref[at, columns] + piece[at, :].astype(F32)
            send_ref[to, columns] = values.astype(BF16)


def middle_kernel(
    spot_ref, kept_ref, got_ref, base_ref, own_terms, got_terms, near_ref, send_ref, out_ref
):
    rows, width = near_ref.shape
    span = base_ref.shape[0]
    values = kept_ref[...] + got_ref[...].astype(F32)
    near_ref[...] = values[:, :width]
    terms = own_terms[:span, :].astype(F32) + got_terms[:span, :].astype(F32)
    out_ref[...] = (base_ref[...] + terms).astype(BF16)
    send_ref[: span // 2, :] = out_ref[window(spot_ref[2] % 2, span // 2), :]
    half = send_ref.shape[1]
    for i in range(width // half):
        at = span // 2 + i * rows
        columns = slice(width + i * half, width + (i + 1) * half)
        send_ref[at : at + rows, :] = values[:, columns].astype(BF16)
    clear_below(send_ref, span // 2 + width // half * rows)


def settle_kernel(spot_ref, near_ref, got_ref, out_ref, own_ref, *sends):
    rows, width = own_ref.shape
    span = out_ref.shape[0]
    out_ref[...] = got_ref[:span, :]
    half = got_ref.shape[1]
    for i in range(width // half):
        at, columns = span + 2 * i * rows, slice(i * half, (i + 1) * half)
        own_ref[:, columns] = near_ref[:rows, columns] + got_ref[at : at + rows, :].astype(F32)
        more = near_ref[rows:, columns] + got_ref[at + rows : at + 2 * rows, :].astype(F32)
        sends[i][...] = more.astype(BF16)


def fill_rows(spot_ref, own_ref, others, out_ref):
    pair, bit, span = spot_ref[2] // 2, spot_ref[2] % 2, own_ref.shape[0]
    out_ref[window(pair, span), :] = own_ref[...].astype(F32)
    if len(others) == 1:
        out_ref[window(1 - pair, span), :] = others[0][...].astype(F32)
    else:
        for i, other in enumerate(others):
            at = 2 * (1 - pair) + (bit ^ i)
            out_ref[window(at, span // 2), :] = other[: span // 2, :].astype(F32)


def rows_kernel(spot_ref, out_own, out_one, out_two, in_own, in_far, out_ref, in_ref):
    fill_rows(spot_ref, out_own, (out_one, out_two), out_ref)
    fill_rows(spot_ref, in_own, (in_far,), in_ref)


def cut_small_kernel(
    spot_ref, kept_ref, got_near, got_far, got_out, small_ref, own_ref, o1, o2, o3, sum_ref
):
    rows, width = own_ref.shape[0], small_ref.shape[1]
    whole = kept_ref.shape[0]
    for bits, out_ref in enumerate((own_ref, o1, o2, o3)):
        at = window(spot_ref[1] ^ bits, rows)
        for side, got_ref in enumerate((got_near, got_far)):
            cols = got_ref.shape[1] // 3
            got = (got_ref[at, :], got_out[at, side * cols : (side + 1) * cols])
            for part, start, stop in ((got[0], 0, 3 * cols), (got[1], 3 * cols, 4 * cols)):
                columns = slice(side * width + start, side * width + stop)
                values = kept_ref[at, columns] + part.astype(F32)
                out_ref[:rows, columns] = values.astype(out_ref.dtype)
    mine = both(*split_two(small_ref[...]))
    got = [piece[whole:, :].astype(F32) for piece in (got_near, got_far, got_out)]
    got = jnp.concatenate(got, axis=1)
    high, low = split_two(mine + (got[:, :width] + got[:, width:]))
    for out_ref in (o1, o2, o3):
        out_ref[rows:, :width] = high
        out_ref[rows:, width:] = low
    sum_ref[...] = both(high, low)


def shards_small_kernel(spot_ref, own_ref, g1, g2, g3, small_ref, kept_ref, send_ref):
    rows, width = kept_ref.shape
    got = [piece[:rows, :].astype(F32) for piece in (g1, g2, g3)]
    values = (own_ref[...] + got[0]) + (got[1] + got[2])
    kept_ref[...] = values[:, :width]
    send_ref[:rows, :] = values[:, width:].astype(BF16)
    count = small_ref.shape[0]
    got = [both(piece[rows:, :width], piece[rows:, width:]) for piece in (g1, g2, g3)]
    high, low = split_two((small_ref[...] + got[0]) + (got[1] + got[2]))
    send_ref[rows : rows + count, :] = high
    send_ref[rows + count :, :] = low


def owned_kernel(
    spot_ref, ffn_kept, ffn_one, ffn_two, kept_ref, sent_ref, got_ref, half_ref,
    out_ref, pass_ref,
):
    rows, width = kept_ref.shape
    half = half_ref.shape[0]
    pass_ref[:half, :] = half_ref[...]
    for i, piece in enumerate((ffn_one, ffn_two)):
        at = slice(i * width, (i + 1) * width)
        out_ref[:, at] = (ffn_kept[:, at] + piece[...].astype(F32)).astype(BF16)
    out_ref[:, 2 * width :] = (kept_ref[...] + got_ref[:rows, :].astype(F32)).astype(BF16)
    count = (sent_ref.shape[0] - rows) // 2
    top, end = slice(rows, rows + count), slice(rows + count, rows + 2 * count)
    mine = both(sent_ref[top, :], sent_ref[end, :])
    high, low = split_two(mine + both(got_ref[top, :], got_ref[end, :]))
    pass_ref[half : half + count, :] = high
    pass_ref[half + count :, :] = low


def sums_out(spot_ref, rows_ref, up_ref, qv_ref, lines):
    up_ref[...] = rows_ref[pl.ds(8 + spot_ref[2], 1), :]
    qv_ref[...] = rows_ref[6:8, window(spot_ref[2], qv_ref.shape[1])]
    for i, line_ref in enumerate(lines):
        line_ref[...] = rows_ref[i : i + 1, :]


def plain_sums_kernel(spot_ref, steps_ref, small_ref, table_ref, up_ref, qv_ref, *lines):
    table_ref[...] = jnp.zeros_like(table_ref)
    for place in range(steps_ref.shape[0]):
        at = pl.ds(steps_ref[place], 1)
        table_ref[at, :] = table_ref[at, :] + small_ref[12 + place : 13 + place, :]
    sums_out(spot_ref, small_ref, up_ref, qv_ref, lines)


def zero_kernel(spot_ref, table_hbm, block_ref, sems):
    block_ref[...] = jnp.zeros_like(block_ref)
    rows = block_ref.shape[0]
    fetch(
        [
            (block_ref, table_hbm.at[i * rows : (i + 1) * rows, :])
            for i in range(table_hbm.shape[0] // rows)
        ],
        sems,
    )


def close_kernel(
    spot_ref, steps_ref, p0, p1, p2, p3, out_own, out_one, out_two, in_own, in_far,
    zero_hbm,
    out_hbm, in_hbm, up_hbm, down_hbm, qkv_hbm, proj_hbm, table_hbm, up_ref, qv_ref, *refs,
):
    lines, refs = refs[:6], refs[6:]
    out_all, in_all, up_all, down_all, qkv_all, proj_all, rows_ref, blocks_ref, sems = refs
    copies = []

    def send(source, target, alone=None):
        copy = pltpu.make_async_copy(source, target, sems.at[len(copies)])
        copies.append((copy, alone))
        copy.start() if alone is None else pl.when(alone)(copy.start)

    fill_rows(spot_ref, out_own, (out_one, out_two), out_all)
    send(out_all, out_hbm)
    start, count = out_one.shape[0] - 2 * rows_ref.shape[0], rows_ref.shape[0]
    parts = [
        both(ref[start : start + count, :], ref[start + count :, :]) for ref in (out_one, out_two)
    ]
    rows_ref[...] = parts[0] + parts[1]
    places = range(steps_ref.shape[0])
    at = lax.broadcasted_iota(jnp.int32, (8, 1), 0)
    for place in places:
        block = steps_ref[place] // 8
        total_rows = jnp.zeros(blocks_ref.shape[1:], F32)
        for other in places:
            step = steps_ref[other]
            row = jnp.where(step // 8 == block, step % 8, -1)
            total_rows = total_rows + jnp.where(at == row, rows_ref[12 + other : 13 + other, :], 0.0)
        blocks_ref[place] = total_rows
        seen = [steps_ref[other] // 8 == block for other in range(place)]
        alone = jnp.logical_not(functools.reduce(jnp.logical_or, seen)) if seen else None
        send(blocks_ref.at[place], table_hbm.at[pl.ds(pl.multiple_of(block * 8, 8), 8), :], alone)
    sums_out(spot_ref, rows_ref, up_ref, qv_ref, lines)
    rows, hidden, cols = p0.shape[0], up_all.shape[1], proj_all.shape[1]
    pieces = (p0, p1, p2, p3)
    spots = [window(spot_ref[1] ^ bits, rows) for bits in range(4)]
    for i, (whole, target) in enumerate(((up_all, up_hbm), (down_all, down_hbm))):
        for spot, piece in zip(spots, pieces):
            whole[spot, :] = piece[:, i * hidden : (i + 1) * hidden].astype(F32)
        send(whole, target)
    start = 2 * hidden
    for spot, piece in zip(spots, pieces):
        for i in range(3):
            qkv_all[i, spot, :] = piece[:, start + i * cols : start + (i + 1) * cols].astype(F32)
        proj_all[spot, :] = piece[:, start + 3 * cols :].astype(F32)
    send(qkv_all, qkv_hbm)
    send(proj_all, proj_hbm)
    fill_rows(spot_ref, in_own, (in_far,), in_all)
    send(in_all, in_hbm)
    for copy, alone in copies:
        copy.wait() if alone is None else pl.when(alone)(copy.wait)


class Reduction:
    def __init__(self, order, kept, small):
        self.order, self.kept, self.small = order, kept, small
        self.rows, self.width = kept.shape[0] // 4, kept.shape[1]

    def cut(self, got):
        rows, width, more = self.rows, self.width, self.small.shape[0]
        self.own, *cuts, self.small = self.order.call(
            cut_small_kernel,
            [((rows, width), F32)]
            + [((rows + more, width), BF16)] * 3
            + [(self.small.shape, F32)],
            [self.kept, *got, self.small],
        )
        self.got = [self.order.swap(cuts[bits - 1], "ctx", bits) for bits in (1, 2, 3)]

    def shards(self):
        rows, width, more = self.rows, self.width // 2, 2 * self.small.shape[0]
        self.own, self.sent = self.order.call(
            shards_small_kernel,
            [((rows, width), F32), ((rows + more, width), BF16)],
            [self.own, *self.got, self.small],
        )
        self.got = self.order.swap(self.sent, "tp", 2)


def reduce_plainly(kept, given, chunk):
    whole = jnp.concatenate([kept, given.astype(F32)])
    mine = lax.psum_scatter(whole, "fsdp", scatter_dimension=0, tiled=True)
    quarter = lax.psum_scatter(mine, "ctx", scatter_dimension=0, tiled=True)
    width = quarter.shape[1] // 2
    far = lax.ppermute(quarter[:, width:], "tp", [(i, i ^ 2) for i in range(4)])
    return lax.all_gather(quarter[:, :width] + far, "ctx", axis=0, tiled=True)


def pieces_of(order, part, parts, rows):
    if parts == 2:
        return part, order.swap(part, "fsdp", 1)
    whole = lax.all_gather(part[:rows], "fsdp", axis=0, tiled=True)
    size = whole.shape[0] // 2
    return whole[:size], whole[size:]


def per_device(
    layer_input,
    timesteps,
    segment_ids,
    time_table,
    ln1_gain,
    ln1_bias,
    w_qkv,
    b_qv,
    w_out_t,
    b_out,
    ln2_gain,
    ln2_bias,
    w_up,
    b_up,
    w_down_t,
    b_down,
    out_grad,
    *,
    parts,
):
    span, width = layer_input.shape[1:]
    rows, cols = w_qkv.shape[1:]
    hidden = w_up.shape[1]
    size = width // 2
    core = lax.axis_index("fsdp")
    chunk = lax.axis_index("ctx")
    shard = lax.axis_index("tp")
    place = core if parts == 2 else 0 * core
    spot = jnp.stack([place, chunk, shard, 2 * core + shard // 2]).astype(jnp.int32)
    order = Order(spot, parts)
    line = lambda values: values.reshape(1, -1)
    dma = lambda count: pltpu.SemaphoreType.DMA((count,))

    pack, qkv_part, out_part_own = order.call(
        pack_kernel,
        [
            ((rows + BIAS_ROWS, 4 * cols), BF16), ((rows + BIAS_ROWS, 3 * cols), BF16),
            ((rows, cols), BF16),
        ],
        [timesteps, w_qkv, w_out_t, b_qv, line(b_up)],
        far=range(5),
        scratch=[
            pltpu.VMEM(w_qkv.shape, F32),
            pltpu.VMEM(w_out_t.shape, F32),
            pltpu.VMEM(b_qv.shape, F32),
            pltpu.VMEM((1, hidden), F32),
            dma(4),
        ],
    )
    near = pieces_of(order, pack, parts, rows)
    pack_far = order.swap(qkv_part, "tp", 2)
    projected = [((span, cols), BF16), ((span, 2 * cols), BF16)]
    more = [((span, cols), BF16), ((span + PAD, 2 * cols), BF16)]
    q_near, kv_near, stream, normed, seg, lines = order.call(
        functools.partial(open_kernel, row=rows),
        projected
        + [
            ((span, width), F32), ((span, width), BF16), ((1, segment_ids.shape[1]), jnp.int32),
            ((8, width), F32),
        ],
        [timesteps, layer_input, time_table, segment_ids]
        + [line(v) for v in (ln1_gain, ln1_bias, ln2_gain, ln2_bias, b_out, b_down)]
        + [*near, pack],
        far=range(10),
        scratch=[
            pltpu.VMEM((span, width), F32),
            pltpu.VMEM((8, width), F32),
            pltpu.VMEM(segment_ids.shape, jnp.int32),
            pltpu.VMEM((6, 1, width), F32),
            dma(9),
        ],
    )
    kvs_near = [kv_near] + order.swap_three(kv_near, "ctx")
    project = functools.partial(project_kernel, row=rows)

    side_shape = (rows // 4 + rows // 8, 2 * hidden) if parts == 2 else (rows, cols)
    rest, side, cotan = order.call(
        pack_rest_kernel,
        [((rows, 2 * hidden), BF16), (side_shape, BF16), ((span, width), F32)],
        [out_part_own, w_up, w_down_t, out_grad],
        far=(1, 2, 3),
        scratch=[pltpu.VMEM(w_up.shape, F32), pltpu.VMEM(w_down_t.shape, F32), dma(3)],
        cost=QUICK,
    )
    side_far = order.swap(side, "tp", 2)
    if parts == 2:
        table = order.call(
            zero_kernel,
            [(time_table.shape, F32)],
            [],
            kept=(0,),
            scratch=[pltpu.VMEM((time_table.shape[0] // 5, width), F32), dma(5)],
            cost=QUICK,
        )[0]
    rest_near = pieces_of(order, rest, parts, rows)

    attended = [((span, cols), BF16), ((span, cols), F32)]
    pack_far, *kvs_near[1:] = hold(pack_far, *kvs_near[1:])
    far = pieces_of(order, pack_far, parts, rows)
    mixed_near, lse_near = order.call(
        attend_one_kernel, attended, [seg, q_near, *kvs_near], cost=COST
    )
    q_far, kv_far = order.call(project, more, [normed, *far, pack_far], cost=QUICK)
    kvs_far = [kv_far] + order.swap_three(kv_far, "ctx")
    if parts == 2:
        rest_far, out_far = order.call(
            unpack_kernel,
            [((rows // 4, 2 * hidden), BF16), ((rows, cols), BF16)],
            [side_far],
            cost=QUICK,
        )
        rest_turn = order.swap_turn(rest_far, 0)
    else:
        rest_far, out_far = order.swap(rest, "tp", 2), side_far
    out_far = pieces_of(order, out_far, parts, rows)
    mixed_far, lse_far, given = order.call(
        attend_two_kernel,
        attended + [((span + PAD, width), BF16)],
        [seg, q_far, *kvs_far, mixed_near, *near, *out_far],
    )
    got = order.swap(given, "tp", 1)
    if parts == 2:
        rest_one = order.call(
            stack_kernel, [((rows // 2, 2 * hidden), BF16)], [rest_far, rest_turn], cost=QUICK
        )[0]
        rest_two = order.swap_turn(rest_one, 1)
        rest_far = [
            rest_one, rest_two, order.swap(rest_one, "fsdp", 1), order.swap(rest_two, "fsdp", 1)
        ]
    else:
        rest_far = pieces_of(order, rest_far, parts, rows)

    acts = [((span, hidden), BF16), ((span, hidden), BF16)]
    back_near, down_near, out_base, resid, normed_two, act_n, pre_n, low, up_near = order.call(
        functools.partial(ffn_near_kernel, row=rows),
        [((span, width), F32)] * 4
        + [((span, width), BF16), *acts, ((span, width), BF16), ((1, hidden), F32)],
        [stream, given, got, cotan, lines, pack, *rest_near],
    )
    act_f, pre_f, up_far, back, ffn_terms = order.call(
        functools.partial(ffn_far_kernel, row=rows),
        [*acts, ((1, hidden), F32), ((span + PAD, width), BF16), ((span, width), BF16)],
        [normed_two, low, back_near, down_near, pack_far, *rest_far],
        scratch=[pltpu.VMEM((size, 2 * hidden), BF16)] * 2,
    )
    back_got = order.swap(back, "tp", 1)
    ffn_kept, *ffn_sent = order.call(
        ffn_grads_kernel,
        [((size, 4 * hidden), F32)] + [((size, hidden), BF16)] * 4,
        [normed_two, low, act_n, pre_n, act_f, pre_f],
    )
    if parts == 2:
        ffn_got = [order.swap(piece, "fsdp", 1) for piece in ffn_sent]
        ffn_own, ffn_cut = order.call(
            cut_kernel,
            [((rows // 2, 4 * hidden), F32), ((rows // 2, 4 * hidden), BF16)],
            [ffn_kept, *ffn_got],
            cost=QUICK,
        )
        ffn_turn = order.swap_turn(ffn_cut, 0)
    dq, own, *shares, resid_grad, low_all, resid_rows = order.call(
        pull_kernel,
        [((span, 2 * cols), F32), ((span, 4 * cols), F32)]
        + [((span + PAD, 4 * cols), BF16)] * 3
        + [((span, width), F32), ((span, width), BF16), ((4, width), F32)],
        [
            seg, q_near, lse_near, *kvs_near, q_far, lse_far, *kvs_far, back, back_got, resid,
            cotan, lines, *near, *out_far,
        ],
        scratch=[pltpu.VMEM((2, span, width), F32)],
        limit=6,
    )
    shared = [order.swap(shares[bits - 1], "ctx", bits) for bits in (1, 2, 3)]

    terms_got = order.swap(ffn_terms, "tp", 1)
    if parts == 2:
        ffn_near, sent, out_low = order.call(
            middle_kernel,
            [
                ((rows // 2, 2 * hidden), F32), ((span // 2 + rows + 2 * PAD, width), BF16),
                ((span, width), BF16),
            ],
            [ffn_own, ffn_turn, out_base, ffn_terms, terms_got],
            cost=QUICK,
        )
        sent_got = order.swap(sent, "tp", 2)
    else:
        out_low = order.call(
            add_pair_kernel, [((span, width), BF16)], [out_base, ffn_terms, terms_got]
        )[0]
        half_rows = lax.dynamic_slice_in_dim(out_low, shard % 2 * (span // 2), span // 2, 0)
        out_half = order.swap(half_rows, "tp", 2)

    seqs = 2 * parts
    small_rows = -(-(12 + seqs) // 16) * 16
    in_terms, small, attention_kept, *attention_sent = order.call(
        input_kernel,
        [
            ((span, width), BF16), ((small_rows, width), F32),
            ((size, 8 * cols), F32), ((size + small_rows, 3 * cols), BF16),
            ((size + small_rows, 3 * cols), BF16), ((size + small_rows, 2 * cols), BF16),
        ],
        [
            stream, lines, resid_rows, up_near, up_far, dq, own, *shared, *near, *far,
            normed, low_all, mixed_near, mixed_far,
        ],
        scratch=[pltpu.VMEM((span, 6 * cols), BF16), pltpu.VMEM((span, width), F32)],
    )
    order.cost = QUICK
    if parts == 2:
        attention_far = [order.swap(piece, "fsdp", 1) for piece in attention_sent]
    in_got = order.swap(in_terms, "tp", 1)
    if parts == 2:
        sums = Reduction(order, attention_kept, small)
        sums.cut(attention_far)
        out_half, ffn_own, *ffn_cuts = order.call(
            settle_kernel,
            [((span // 2, width), BF16), ((rows // 4, 2 * hidden), F32)]
            + [((rows // 4, hidden), BF16)] * 2,
            [ffn_near, sent_got],
        )
        ffn_turns = [order.swap_turn(piece, 1) for piece in ffn_cuts]
        sums.shards()
    in_low = order.call(
        add_pair_kernel, [((span, width), BF16)], [resid_grad, in_terms, in_got]
    )[0]
    if parts == 2:
        in_low, sums.got = hold(in_low, sums.got)
    in_far = order.swap(in_low, "tp", 2)
    vectors = [((1, hidden), F32), ((2, cols), F32)] + [((1, width), F32)] * 6
    large = [((2 * span, width), F32)] * 2
    if parts == 2:
        owned, passed = order.call(
            owned_kernel,
            [
                ((rows // 4, 2 * hidden + 4 * cols), BF16),
                ((span // 2 + 2 * small_rows, width), BF16),
            ],
            [ffn_own, *ffn_turns, sums.own, sums.sent, sums.got, out_half],
        )
        passed_got = order.swap(passed, "tp", 1)
        pieces = [owned] + order.swap_three(owned, "ctx")
        bits = near[1][rows : rows + 9 : 3, 2 * cols : 2 * cols + 2].astype(F32)
        far_steps = jnp.sum(bits, axis=0).astype(jnp.int32)
        steps = jnp.where(
            core == 0,
            jnp.concatenate([timesteps, far_steps]),
            jnp.concatenate([far_steps, timesteps]),
        )
        large = large + [((rows, hidden), F32)] * 2 + [((3, rows, cols), F32), ((rows, cols), F32)]
        output, grad_input, grads_up, grads_down, grads_qkv, grads_out, table, *rest = order.call(
            close_kernel,
            large + [(time_table.shape, F32)] + vectors,
            [
                steps, *pieces, out_low, passed, passed_got, in_low, in_far, table,
            ],
            far=(10,),
            kept=range(7),
            alias={10: 6},
            scratch=[pltpu.VMEM(shape, dtype) for shape, dtype in large]
            + [pltpu.VMEM((small_rows, width), F32), pltpu.VMEM((seqs, 8, width), F32)]
            + [dma(6 + seqs)],
            limit=8,
        )
    else:
        output, grad_input = order.call(
            rows_kernel, large, [out_low, out_half, order.swap(out_half, "tp", 1), in_low, in_far]
        )
        ffn_sent = jnp.concatenate(ffn_sent, axis=1)
        both_grads = reduce_plainly(ffn_kept, ffn_sent, chunk)
        grads_up, grads_down = both_grads[:, :hidden], both_grads[:, hidden:]
        near_part, far_part, out_columns = [piece[:size] for piece in attention_sent]
        attention_sent = jnp.concatenate(
            [near_part, out_columns[:, :cols], far_part, out_columns[:, cols:]], axis=1
        )
        every = reduce_plainly(attention_kept, attention_sent, chunk)
        grads_qkv = jnp.stack([every[:, i * cols : (i + 1) * cols] for i in range(3)])
        grads_out = every[:, 3 * cols :]
        small = lax.psum(small, ("fsdp", "ctx", "tp"))
        steps = lax.all_gather(timesteps, "fsdp", axis=0, tiled=True)
        table, *rest = order.call(
            plain_sums_kernel, [(time_table.shape, F32)] + vectors, [steps, small]
        )
    up_line, qv_lines, *sums = rest
    sums = [values.reshape(-1) for values in sums]

    shape = layer_input.shape
    return (
        output.reshape(shape),
        grad_input.reshape(shape),
        table,
        sums[0],
        sums[1],
        grads_qkv,
        qv_lines,
        grads_out,
        sums[4],
        sums[2],
        sums[3],
        grads_up,
        up_line.reshape(-1),
        grads_down,
        sums[5],
    )


def solution(mesh):
    placed = (
        P("fsdp", "ctx", None),
        P("fsdp"),
        P("fsdp", None),
        P(),
        P(),
        P(),
        P(None, "fsdp", "tp"),
        P(None, "tp"),
        P("fsdp", "tp"),
        P(),
        P(),
        P(),
        P("fsdp", "tp"),
        P("tp"),
        P("fsdp", "tp"),
        P(),
        P("fsdp", "ctx", None),
    )
    return jax.shard_map(
        functools.partial(per_device, parts=mesh.shape["fsdp"]),
        mesh=mesh,
        in_specs=placed,
        out_specs=(
            P("fsdp", "ctx", None),
            P("fsdp", "ctx", None),
            P(),
            P(),
            P(),
            P(None, "fsdp", "tp"),
            P(None, "tp"),
            P("fsdp", "tp"),
            P(),
            P(),
            P(),
            P("fsdp", "tp"),
            P("tp"),
            P("fsdp", "tp"),
            P(),
        ),
        check_vma=False,
    )
```

```python
import functools
import jax
import jax.numpy as jnp
from jax import lax
from jax.experimental import pallas as pl
from jax.experimental.pallas import tpu as pltpu
from jax.sharding import PartitionSpec as P

HEAD_DIM = 64
SCALE = HEAD_DIM ** (-0.5)
EPSILON = 1e-05
NEGATIVE = -1e30
F32 = jnp.float32
BF16 = jnp.bfloat16
BIAS_ROWS = 16
PAD = 16
CUBE = 0.044715
ROOT = 0.7978845608028654
COST, QUICK, LONG = 8_000_000_000, 1_000, 20_000_000_000
VMEM = pl.BlockSpec(memory_space=pltpu.VMEM)
SMEM = pl.BlockSpec(memory_space=pltpu.SMEM)


def dot_nn(left, right):
    return lax.dot_general(left, right, (((1,), (0,)), ((), ())), preferred_element_type=F32)


def dot_nt(left, right):
    return lax.dot_general(left, right, (((1,), (1,)), ((), ())), preferred_element_type=F32)


def dot_tn(left, right):
    return lax.dot_general(left, right, (((0,), (0,)), ((), ())), preferred_element_type=F32)


def total(values):
    return functools.reduce(jnp.add, values)


def norm_parts(values):
    centre = values - jnp.mean(values, axis=-1, keepdims=True)
    spread = jnp.mean(centre * centre, axis=-1, keepdims=True)
    inverse = lax.rsqrt(spread + EPSILON)
    return centre * inverse, inverse


def norm_back(grad, hat, inverse, gain):
    scaled = grad * gain
    mean_one = jnp.mean(scaled, axis=-1, keepdims=True)
    mean_two = jnp.mean(scaled * hat, axis=-1, keepdims=True)
    return inverse * (scaled - mean_one - hat * mean_two)


def column_sum(values):
    return jnp.sum(values, axis=0, keepdims=True)


def window(index, size):
    return pl.ds(pl.multiple_of(index * size, size), size)


def halves(spot_ref, size):
    return window(spot_ref[0], size), window(1 - spot_ref[0], size)


def hold(*values):
    return lax.optimization_barrier(values)


class Order:
    def __init__(self, spot, parts):
        self.spot, self.parts, self.cost = spot, parts, COST

    def call(self, kernel, outs, operands, *, far=(), kept=(), alias=None, scratch=(), limit=5, cost=None):
        specs = [
            SMEM if operand.ndim == 1
            else pl.BlockSpec(memory_space=pltpu.HBM if i in far else pltpu.VMEM)
            for i, operand in enumerate(operands)
        ]
        operands = [
            pltpu.with_memory_space_constraint(operand, pltpu.HBM) if i in far else operand
            for i, operand in enumerate(operands)
        ]
        count = len(operands)

        def body(*refs):
            kernel(refs[count], *refs[:count], *refs[count + 1 :])

        results = pl.pallas_call(
            body,
            out_shape=tuple(jax.ShapeDtypeStruct(shape, dtype) for shape, dtype in outs),
            in_specs=specs + [SMEM],
            out_specs=tuple(
                pl.BlockSpec(memory_space=pltpu.HBM) if i in kept else VMEM
                for i in range(len(outs))
            ),
            input_output_aliases=alias or {},
            scratch_shapes=list(scratch),
            compiler_params=pltpu.CompilerParams(vmem_limit_bytes=limit << 20),
            cost_estimate=pl.CostEstimate(
                flops=cost or self.cost, bytes_accessed=1 << 16, transcendentals=0
            ),
        )(*operands, self.spot)
        first, self.spot = hold(results[0], self.spot)
        return [first, *results[1:]]

    def swap(self, values, axis, bits):
        values, self.spot = hold(values, self.spot)
        size = 2 if axis == "fsdp" else 4
        with jax.named_scope("swap_%s_%d" % (axis, bits)):
            return lax.ppermute(values, axis, [(i, i ^ bits) for i in range(size)])

    def swap_three(self, values, axis):
        return [self.swap(values, axis, bits) for bits in (1, 2, 3)]

    def swap_turn(self, values, turn):
        if self.parts != 2:
            return self.swap(values, "ctx", 1 + turn)
        values, self.spot = hold(values, self.spot)
        pairs = [
            (4 * core + i, 4 * core + (i ^ (1 + (core + turn) % 2)))
            for core in range(2)
            for i in range(4)
        ]
        with jax.named_scope("swap_turn_%d" % turn):
            return lax.ppermute(values, ("fsdp", "ctx"), pairs)


def clear_below(ref, rows):
    if ref.shape[0] > rows:
        ref[rows:, :] = jnp.zeros((ref.shape[0] - rows, ref.shape[1]), ref.dtype)


def fetch(copies, sems):
    started = [
        pltpu.make_async_copy(source, target, sems.at[i])
        for i, (source, target) in enumerate(copies)
    ]
    for copy in started:
        copy.start()
    for copy in started:
        copy.wait()


def split_three(values):
    high = values.astype(BF16)
    rest = values - high.astype(F32)
    middle = rest.astype(BF16)
    return [high, middle, (rest - middle.astype(F32)).astype(BF16)]


def pack_kernel(
    spot_ref, steps_ref, w_hbm, out_hbm, qv_hbm, up_bias_hbm, pack_ref, qkv_ref, out_ref,
    w_ref, o_ref, qv_ref, up_bias_ref, sems,
):
    rows, cols = w_ref.shape[1:]
    fetch(
        [(w_hbm, w_ref), (out_hbm, o_ref), (qv_hbm, qv_ref), (up_bias_hbm, up_bias_ref)], sems
    )
    for i in range(3):
        pack_ref[:rows, i * cols : (i + 1) * cols] = w_ref[i].astype(BF16)
    pack_ref[:rows, 3 * cols :] = o_ref[...].astype(BF16)
    lanes = lax.broadcasted_iota(jnp.int32, (1, cols), 1)
    steps = jnp.zeros((1, cols), F32)
    for i in range(steps_ref.shape[0]):
        steps = jnp.where(lanes == i, steps_ref[i].astype(F32), steps)
    fill = jnp.zeros((1, cols), F32)
    up_bias = up_bias_ref[...]
    lines = [
        jnp.concatenate([qv_ref[0:1], qv_ref[1:2], steps, fill], axis=1),
        jnp.concatenate([up_bias[:, : 2 * cols], fill, fill], axis=1),
        jnp.concatenate([up_bias[:, 2 * cols :], fill, fill], axis=1),
    ]
    parts = split_three(jnp.concatenate(lines, axis=0))
    fill = jnp.zeros((BIAS_ROWS - 9, 4 * cols), F32)
    stack = jnp.concatenate([v.astype(F32) for v in parts] + [fill], axis=0)
    pack_ref[rows:, :] = stack.astype(BF16)
    qkv_ref[...] = pack_ref[:, : 3 * cols]
    out_ref[...] = pack_ref[:rows, 3 * cols :]


def pack_rest_kernel(
    spot_ref, own_out, up_hbm, down_hbm, cotan_hbm, rest_ref, side_ref, cotan_ref,
    up_ref, down_ref, sems,
):
    rows, hidden = up_ref.shape
    cols = own_out.shape[1]
    pair = spot_ref[2] // 2
    fetch([(up_hbm, up_ref), (down_hbm, down_ref), (cotan_hbm.at[pair], cotan_ref)], sems)
    rest_ref[:, :hidden] = up_ref[...].astype(BF16)
    rest_ref[:, hidden:] = down_ref[...].astype(BF16)
    if side_ref.shape[0] == rows:
        side_ref[...] = own_out[...]
        return
    quarter, fold = rows // 4, rows // 8
    mine = window(spot_ref[1], quarter)
    side_ref[:quarter, :hidden] = up_ref[mine, :].astype(BF16)
    side_ref[:quarter, hidden:] = down_ref[mine, :].astype(BF16)
    for i in range(8):
        block = own_out[i * fold : (i + 1) * fold, :]
        side_ref[quarter : quarter + fold, i * cols : (i + 1) * cols] = block
    clear_below(side_ref, quarter + fold)


def unpack_kernel(spot_ref, side_ref, quarter_ref, out_ref):
    rows, cols = out_ref.shape
    quarter, fold = rows // 4, rows // 8
    quarter_ref[...] = side_ref[:quarter, :]
    for i in range(8):
        block = side_ref[quarter : quarter + fold, i * cols : (i + 1) * cols]
        out_ref[i * fold : (i + 1) * fold, :] = block


def bias_lines(pack_ref, row):
    bits = pack_ref[row : row + BIAS_ROWS, :].astype(F32)
    lines = bits[0:3] + bits[3:6] + bits[6:9]
    half = 4 * HEAD_DIM
    return lines[0:1], jnp.concatenate([lines[1:2, :half], lines[2:3, :half]], axis=1)


def out_part(ref, size):
    cols = 2 * HEAD_DIM
    return ref[:size, ref.shape[1] - cols :]


def add_pair_kernel(spot_ref, base_ref, own_ref, got_ref, out_ref):
    span = base_ref.shape[0]
    terms = own_ref[:span, :].astype(F32) + got_ref[:span, :].astype(F32)
    out_ref[...] = (base_ref[...] + terms).astype(BF16)


def open_kernel(
    spot_ref, steps_ref, x_hbm, table_hbm, seg_hbm, g1, b1, g2, b2, bo, bd, one_ref, two_ref,
    bias_ref, q_ref, kv_ref, stream_ref, normed_ref, seg_ref, lines_ref,
    x_ref, table_ref, ids_ref, line_ref, sems, *, row,
):
    pair = spot_ref[2] // 2
    step = steps_ref[pair]
    block = pl.multiple_of(step // 8 * 8, 8)
    copies = [
        (x_hbm.at[pair], x_ref),
        (table_hbm.at[pl.ds(block, 8), :], table_ref),
        (seg_hbm, ids_ref),
    ]
    vectors = (g1, b1, g2, b2, bo, bd)
    fetch(copies + [(v, line_ref.at[i]) for i, v in enumerate(vectors)], sems)
    for i in range(len(vectors)):
        lines_ref[i : i + 1, :] = line_ref[i]
    seg_ref[...] = ids_ref[pl.ds(pair, 1), :]
    stream = x_ref[...] + table_ref[pl.ds(step % 8, 1), :]
    hat, _ = norm_parts(stream)
    stream_ref[...] = stream
    normed_ref[...] = (hat * line_ref[0] + line_ref[1]).astype(BF16)
    project_kernel(spot_ref, normed_ref, one_ref, two_ref, bias_ref, q_ref, kv_ref, row=row)


def project_kernel(spot_ref, normed_ref, one_ref, two_ref, bias_ref, q_ref, kv_ref, *, row):
    span, cols = q_ref.shape
    size = normed_ref.shape[1] // 2
    one, two = halves(spot_ref, size)
    raw = dot_nn(normed_ref[:, one], one_ref[:size, : 3 * cols])
    raw = raw + dot_nn(normed_ref[:, two], two_ref[:size, : 3 * cols])
    line, _ = bias_lines(bias_ref, row)
    q_bias, v_bias = line[:, :cols], line[:, cols : 2 * cols]
    q_ref[...] = (raw[:, :cols] + q_bias).astype(BF16)
    kv_ref[:span, :cols] = raw[:, cols : 2 * cols].astype(BF16)
    kv_ref[:span, cols:] = (raw[:, 2 * cols :] + v_bias).astype(BF16)
    clear_below(kv_ref, span)


def mask_biases(spot_ref, seg_ref, span):
    chunk = spot_ref[1]
    ids = [seg_ref[:, window(chunk ^ step, span)] for step in range(seg_ref.shape[1] // span)]
    own = jnp.broadcast_to(ids[0], (span, span)).T
    return [
        jnp.where(own == jnp.broadcast_to(step_ids, (span, span)), 0.0, NEGATIVE)
        for step_ids in ids
    ]


def lane_mask(shape, head):
    return (lax.broadcasted_iota(jnp.int32, shape, 1) // HEAD_DIM) == head


def attend_forward(spot_ref, seg_ref, q_ref, kvs, mixed_ref, lse_ref):
    span, width = q_ref.shape
    biases = mask_biases(spot_ref, seg_ref, span)
    query = q_ref[...]
    mixed, lse = None, None
    for head in range(width // HEAD_DIM):
        mine = lane_mask((span, width), head)
        masked = jnp.where(mine, query, jnp.zeros_like(query))
        scores = [
            dot_nt(masked, kv[:span, :width]) * SCALE + bias for kv, bias in zip(kvs, biases)
        ]
        top = functools.reduce(
            jnp.maximum, [jnp.max(block, axis=-1, keepdims=True) for block in scores]
        )
        grown = [jnp.exp(block - top) for block in scores]
        mass = total([jnp.sum(block, axis=-1, keepdims=True) for block in grown])
        share = 1.0 / mass
        out = total(
            [
                dot_nn((block * share).astype(BF16), kv[:span, width:])
                for block, kv in zip(grown, kvs)
            ]
        )
        log_mass = jnp.broadcast_to(top + jnp.log(mass), (span, width))
        mixed = out if head == 0 else jnp.where(mine, out, mixed)
        lse = log_mass if head == 0 else jnp.where(mine, log_mass, lse)
    mixed_ref[...] = mixed.astype(BF16)
    lse_ref[...] = lse


def attend_one_kernel(spot_ref, seg_ref, q_ref, kv0, kv1, kv2, kv3, mixed_ref, lse_ref):
    attend_forward(spot_ref, seg_ref, q_ref, (kv0, kv1, kv2, kv3), mixed_ref, lse_ref)


def attend_two_kernel(
    spot_ref, seg_ref, q_ref, kv0, kv1, kv2, kv3, near_ref, one_n, two_n, one_f, two_f,
    mixed_ref, lse_ref, given_ref,
):
    attend_forward(spot_ref, seg_ref, q_ref, (kv0, kv1, kv2, kv3), mixed_ref, lse_ref)
    size = given_ref.shape[1] // 2
    one, two = halves(spot_ref, size)
    near, far = near_ref[...], mixed_ref[...]
    for columns, near_w, far_w in ((one, one_n, one_f), (two, two_n, two_f)):
        terms = dot_nt(near, out_part(near_w, size)) + dot_nt(far, out_part(far_w, size))
        given_ref[: near.shape[0], columns] = terms.astype(BF16)
    clear_below(given_ref, near.shape[0])


def stack_kernel(spot_ref, one_ref, two_ref, out_ref):
    rows = out_ref.shape[0] // 2
    out_ref[:rows, :] = one_ref[:rows, :]
    out_ref[rows:, :] = two_ref[:rows, :]


def gelu_parts(x):
    square = x * x
    curve = jnp.tanh(ROOT * (x + CUBE * (x * square)))
    half = 0.5 * (1.0 + curve)
    slope = half + 0.5 * x * (1.0 - curve * curve) * (ROOT * (1.0 + 3.0 * CUBE * square))
    return x * half, slope


def ffn_side(
    normed_ref, low_ref, bias, first, second, columns, act_ref, pre_ref, sum_ref, *sums
):
    hidden = act_ref.shape[1]
    one, two = columns
    pre = dot_nn(normed_ref[:, one], first[:, :hidden])
    pre = pre + dot_nn(normed_ref[:, two], second[:, :hidden]) + bias
    value, slope = gelu_parts(pre)
    grad = dot_nn(low_ref[:, one], first[:, hidden:])
    grad = (grad + dot_nn(low_ref[:, two], second[:, hidden:])) * slope
    sum_ref[...] = column_sum(grad)
    act_ref[...] = value.astype(BF16)
    pre_ref[...] = grad.astype(BF16)
    act, pre_low = act_ref[...], pre_ref[...]
    for at, weights in zip(columns, (first, second)):
        back = dot_nt(pre_low, weights[:, :hidden])
        down = dot_nt(act, weights[:, hidden:])
        if len(sums) == 2:
            back_ref, out_ref = sums
        else:
            back_near, out_near, back_ref, out_ref = sums
            back, down = back + back_near[:, at], down + out_near[:, at]
        back_ref[: act.shape[0], at] = back.astype(back_ref.dtype)
        out_ref[: act.shape[0], at] = down.astype(out_ref.dtype)
    clear_below(sums[-2], act.shape[0])
    clear_below(sums[-1], act.shape[0])


def ffn_near_kernel(
    spot_ref, stream_ref, mine_ref, got_ref, cotan_ref, lines_ref, pack_ref, first, second,
    back_ref, ffn_ref, out_ref, resid_ref, normed_ref, act_ref, pre_ref, low_ref, sum_ref, *, row,
):
    span = stream_ref.shape[0]
    terms = mine_ref[:span, :].astype(F32) + got_ref[:span, :].astype(F32)
    resid = stream_ref[...] + terms + lines_ref[4:5, :]
    resid_ref[...] = resid
    out_ref[...] = resid + lines_ref[5:6, :]
    hat, _ = norm_parts(resid)
    normed_ref[...] = (hat * lines_ref[2:3, :] + lines_ref[3:4, :]).astype(BF16)
    low_ref[...] = cotan_ref[...].astype(BF16)
    ffn_side(
        normed_ref, low_ref, bias_lines(pack_ref, row)[1], first, second,
        halves(spot_ref, first.shape[0]), act_ref, pre_ref, sum_ref, back_ref, ffn_ref,
    )


def ffn_far_kernel(spot_ref, normed_ref, low_ref, back_near, ffn_near, pack_ref, *refs, row):
    count = len(refs) - 7
    pieces, outs, (first, second) = refs[:count], refs[count:-2], refs[-2:]
    if count == 2:
        first, second = pieces
    else:
        rows = pieces[0].shape[0] // 2
        turn, other = turn_bits(spot_ref)
        for target, pairs, bits in (
            (first, pieces[:2], (0, turn, other, 3)),
            (second, pieces[2:], (0, other, turn, 3)),
        ):
            for i in range(4):
                block = pairs[i // 2][i % 2 * rows : (i % 2 + 1) * rows, :]
                target[window(spot_ref[1] ^ bits[i], rows), :] = block
    act_ref, pre_ref, sum_ref, back_ref, ffn_ref = outs
    ffn_side(
        normed_ref, low_ref, bias_lines(pack_ref, row)[1], first, second,
        halves(spot_ref, first.shape[0]), act_ref, pre_ref, sum_ref, back_near, ffn_near,
        back_ref, ffn_ref,
    )


def ffn_kernel(
    spot_ref, stream_ref, mine_ref, got_ref, cotan_ref, lines_ref, pack_ref, far_pack, first, second,
    *refs, row,
):
    pieces, outs, scratch = refs[:-16], refs[-16:-4], refs[-4:]
    back_ref, down_ref, out_ref, resid_ref, normed_ref, low_ref = outs[:6]
    act_n, pre_n, sum_n, act_f, pre_f, sum_f = outs[6:]
    back_near, down_near, one, two = scratch
    ffn_near_kernel(
        spot_ref, stream_ref, mine_ref, got_ref, cotan_ref, lines_ref, pack_ref, first, second,
        back_near, down_near, out_ref, resid_ref, normed_ref, act_n, pre_n, low_ref, sum_n, row=row,
    )
    ffn_far_kernel(
        spot_ref, normed_ref, low_ref, back_near, down_near, far_pack, *pieces,
        act_f, pre_f, sum_f, back_ref, down_ref, one, two, row=row,
    )


def ffn_grads_kernel(
    spot_ref, normed_ref, low_ref, act_n, pre_n, act_f, pre_f, kept_ref, *given
):
    hidden = act_n.shape[1]
    one, two = halves(spot_ref, normed_ref.shape[1] // 2)
    for columns in (two, one):
        normed, low = normed_ref[:, columns], low_ref[:, columns]
        for i, (left, right) in enumerate(((normed, pre_n), (low, act_n), (normed, pre_f), (low, act_f))):
            grads = dot_tn(left, right[...])
            if columns is one:
                kept_ref[:, i * hidden : (i + 1) * hidden] = grads
            else:
                given[i][...] = grads.astype(BF16)


def resid_part(
    spot_ref, mine_ref, got_ref, resid_ref, cotan_ref, lines_ref, grad_ref, low_ref, rows_ref,
    work_ref,
):
    half = resid_ref.shape[0] // 2
    mine = window(spot_ref[2] % 2, half)
    span = resid_ref.shape[0]
    grad = mine_ref[:span, :].astype(F32) + got_ref[:span, :].astype(F32)
    hat, inverse = norm_parts(resid_ref[...])
    resid_grad = cotan_ref[...] + norm_back(grad, hat, inverse, lines_ref[2:3, :])
    grad_ref[...] = resid_grad
    low_ref[...] = resid_grad.astype(BF16)
    work_ref[0] = grad * hat
    work_ref[1] = grad
    sums = [work_ref[0, mine, :], work_ref[1, mine, :], grad_ref[mine, :], cotan_ref[mine, :]]
    rows_ref[...] = jnp.concatenate([column_sum(v) for v in sums], axis=0)


def attend_backward(spot_ref, seg_ref, q_ref, grad, lse_ref, kvs, dq_ref, outs, side):
    span, width = q_ref.shape
    biases = mask_biases(spot_ref, seg_ref, span)
    query = q_ref[...]
    dq, dks, dvs = None, [None] * 4, [None] * 4
    for head in range(width // HEAD_DIM):
        mine = lane_mask((span, width), head)
        masked_q = jnp.where(mine, query, jnp.zeros_like(query))
        masked_g = jnp.where(mine, grad, jnp.zeros_like(grad))
        lse = lse_ref[:, head * HEAD_DIM : head * HEAD_DIM + 1]
        probs = [
            jnp.exp(dot_nt(masked_q, kv[:span, :width]) * SCALE + bias - lse)
            for kv, bias in zip(kvs, biases)
        ]
        grads = [dot_nt(masked_g, kv[:span, width:]) for kv in kvs]
        inner = total([jnp.sum(p * g, axis=-1, keepdims=True) for p, g in zip(probs, grads)])
        raws = [(p * (g - inner) * SCALE).astype(BF16) for p, g in zip(probs, grads)]
        head_dq = total([dot_nn(raw, kv[:span, :width]) for raw, kv in zip(raws, kvs)])
        dq = head_dq if head == 0 else jnp.where(mine, head_dq, dq)
        for step in range(4):
            head_dk = dot_tn(raws[step], query)
            head_dv = dot_tn(probs[step].astype(BF16), grad)
            dks[step] = head_dk if head == 0 else jnp.where(mine, head_dk, dks[step])
            dvs[step] = head_dv if head == 0 else jnp.where(mine, head_dv, dvs[step])
    dq_ref[:, side * width : (side + 1) * width] = dq
    at = 2 * side * width
    for step in range(4):
        outs[step][:span, at : at + width] = dks[step].astype(outs[step].dtype)
        outs[step][:span, at + width : at + 2 * width] = dvs[step].astype(outs[step].dtype)


def pull_kernel(
    spot_ref, seg_ref, q_n, lse_n, n0, n1, n2, n3, q_f, lse_f, f0, f1, f2, f3,
    mine_ref, got_ref, resid_ref, cotan_ref, lines_ref, one_n, two_n, one_f, two_f,
    dq_ref, own_ref, out1, out2, out3, grad_ref, low_ref, rows_ref, work_ref,
):
    size = low_ref.shape[1] // 2
    resid_part(
        spot_ref, mine_ref, got_ref, resid_ref, cotan_ref, lines_ref, grad_ref, low_ref, rows_ref,
        work_ref,
    )
    one, two = halves(spot_ref, size)
    outs = (own_ref, out1, out2, out3)
    near = (q_n, lse_n, (n0, n1, n2, n3), one_n, two_n)
    far = (q_f, lse_f, (f0, f1, f2, f3), one_f, two_f)
    for side, (q_ref, lse_ref, kvs, first, second) in enumerate((near, far)):
        grad = dot_nn(low_ref[:, one], out_part(first, size))
        grad = grad + dot_nn(low_ref[:, two], out_part(second, size))
        attend_backward(
            spot_ref, seg_ref, q_ref, grad.astype(BF16), lse_ref, kvs, dq_ref, outs, side
        )
    for out_ref in (out1, out2, out3):
        clear_below(out_ref, q_n.shape[0])


def input_kernel(
    spot_ref, stream_ref, lines_ref, rows_ref, up_near, up_far, dq_ref, own_ref, g1, g2, g3,
    one_n, two_n, one_f, two_f, normed_ref, low_ref, near_ref, far_ref,
    given_ref, small_ref, w_kept_ref, w_near_ref, w_far_ref, w_out_ref, pulled_ref, terms_ref,
):
    span, width = stream_ref.shape
    cols = dq_ref.shape[1] // 2
    size = width // 2
    shard, slot = spot_ref[2], spot_ref[3]
    far = shard ^ 2
    one, two = halves(spot_ref, size)
    small_ref[...] = jnp.zeros_like(small_ref)
    parts = [ref[:span, :].astype(F32) for ref in (g1, g2, g3)]
    got = (own_ref[...] + parts[0]) + (parts[1] + parts[2])
    for side, (place, up_sum) in enumerate(((shard, up_near), (far, up_far))):
        dq = dq_ref[:, side * cols : (side + 1) * cols]
        dkv = got[:, 2 * side * cols : 2 * (side + 1) * cols]
        at = side * 3 * cols
        pulled_ref[:, at : at + cols] = dq.astype(BF16)
        pulled_ref[:, at + cols : at + 3 * cols] = dkv.astype(BF16)
        small_ref[6:7, window(place, cols)] = column_sum(dq)
        small_ref[7:8, window(place, cols)] = column_sum(dkv[:, cols:])
        small_ref[pl.ds(8 + place, 1), :] = up_sum[...]
    for columns, near_w, far_w in ((one, one_n, one_f), (two, two_n, two_f)):
        back = dot_nt(pulled_ref[:, : 3 * cols], near_w[:size, : 3 * cols])
        back = back + dot_nt(pulled_ref[:, 3 * cols :], far_w[:size, : 3 * cols])
        terms_ref[:, columns] = back
    back = terms_ref[...]
    hat, inverse = norm_parts(stream_ref[...])
    small_ref[0:1, :] = column_sum(back * hat)
    small_ref[1:2, :] = column_sum(back)
    small_ref[2:6, :] = rows_ref[...]
    grad = norm_back(back, hat, inverse, lines_ref[0:1, :])
    small_ref[pl.ds(12 + slot, 1), :] = column_sum(grad) + rows_ref[2:3, :]
    given_ref[...] = grad.astype(BF16)
    given = (w_near_ref, w_far_ref)
    for columns in (two, one):
        normed, low = normed_ref[:, columns], low_ref[:, columns]
        for side, mixed in enumerate((near_ref, far_ref)):
            at, start = side * 3 * cols, side * 4 * cols
            qkv = dot_tn(normed, pulled_ref[:, at : at + 3 * cols])
            out = dot_tn(low, mixed[...])
            if columns is one:
                w_kept_ref[:, start : start + 3 * cols] = qkv
                w_kept_ref[:, start + 3 * cols : start + 4 * cols] = out
            else:
                given[side][:size, :] = qkv.astype(BF16)
                w_out_ref[:size, side * cols : (side + 1) * cols] = out.astype(BF16)
    both_parts = jnp.concatenate(split_two(small_ref[...]), axis=1)
    w_near_ref[size:, :] = both_parts[:, : 3 * cols]
    w_far_ref[size:, :] = both_parts[:, 3 * cols : 6 * cols]
    w_out_ref[size:, :] = both_parts[:, 6 * cols :]


def turn_bits(spot_ref):
    return 1 + spot_ref[0], 2 - spot_ref[0]


def split_two(values):
    high = values.astype(BF16)
    return high, (values - high.astype(F32)).astype(BF16)


def both(high, low):
    return high.astype(F32) + low.astype(F32)


def cut_kernel(spot_ref, kept_ref, *refs):
    got, (own_ref, send_ref) = refs[:4], refs[4:]
    rows, width = own_ref.shape[0] // 2, got[0].shape[1]
    chunk = spot_ref[1]
    first, second = turn_bits(spot_ref)
    for spot, place in enumerate((chunk, chunk ^ second)):
        to = slice(spot * rows, (spot + 1) * rows)
        for i, piece in enumerate(got):
            columns = slice(i * width, (i + 1) * width)
            at = window(place, rows)
            own_ref[to, columns] = kept_ref[at, columns] + piece[at, :].astype(F32)
            at = window(place ^ first, rows)
            values = kept_ref[at, columns] + piece[at, :].astype(F32)
            send_ref[to, columns] = values.astype(BF16)


def middle_kernel(
    spot_ref, kept_ref, got_ref, base_ref, own_terms, got_terms, near_ref, send_ref, out_ref
):
    rows, width = near_ref.shape
    span = base_ref.shape[0]
    values = kept_ref[...] + got_ref[...].astype(F32)
    near_ref[...] = values[:, :width]
    terms = own_terms[:span, :].astype(F32) + got_terms[:span, :].astype(F32)
    out_ref[...] = (base_ref[...] + terms).astype(BF16)
    send_ref[: span // 2, :] = out_ref[window(spot_ref[2] % 2, span // 2), :]
    half = send_ref.shape[1]
    for i in range(width // half):
        at = span // 2 + i * rows
        columns = slice(width + i * half, width + (i + 1) * half)
        send_ref[at : at + rows, :] = values[:, columns].astype(BF16)
    clear_below(send_ref, span // 2 + width // half * rows)


def settle_kernel(spot_ref, near_ref, got_ref, out_ref, own_ref, *sends):
    rows, width = own_ref.shape
    span = out_ref.shape[0]
    out_ref[...] = got_ref[:span, :]
    half = got_ref.shape[1]
    for i in range(width // half):
        at, columns = span + 2 * i * rows, slice(i * half, (i + 1) * half)
        own_ref[:, columns] = near_ref[:rows, columns] + got_ref[at : at + rows, :].astype(F32)
        more = near_ref[rows:, columns] + got_ref[at + rows : at + 2 * rows, :].astype(F32)
        sends[i][...] = more.astype(BF16)


def fill_rows(spot_ref, own_ref, others, out_ref):
    pair, bit, span = spot_ref[2] // 2, spot_ref[2] % 2, own_ref.shape[0]
    out_ref[window(pair, span), :] = own_ref[...].astype(F32)
    if len(others) == 1:
        out_ref[window(1 - pair, span), :] = others[0][...].astype(F32)
    else:
        for i, other in enumerate(others):
            at = 2 * (1 - pair) + (bit ^ i)
            out_ref[window(at, span // 2), :] = other[: span // 2, :].astype(F32)


def rows_kernel(spot_ref, out_own, out_one, out_two, in_own, in_far, out_ref, in_ref):
    fill_rows(spot_ref, out_own, (out_one, out_two), out_ref)
    fill_rows(spot_ref, in_own, (in_far,), in_ref)


def cut_small_kernel(
    spot_ref, kept_ref, got_near, got_far, got_out, small_ref, own_ref, o1, o2, o3, sum_ref
):
    rows, width = own_ref.shape[0], small_ref.shape[1]
    whole = kept_ref.shape[0]
    for bits, out_ref in enumerate((own_ref, o1, o2, o3)):
        at = window(spot_ref[1] ^ bits, rows)
        for side, got_ref in enumerate((got_near, got_far)):
            cols = got_ref.shape[1] // 3
            got = (got_ref[at, :], got_out[at, side * cols : (side + 1) * cols])
            for part, start, stop in ((got[0], 0, 3 * cols), (got[1], 3 * cols, 4 * cols)):
                columns = slice(side * width + start, side * width + stop)
                values = kept_ref[at, columns] + part.astype(F32)
                out_ref[:rows, columns] = values.astype(out_ref.dtype)
    mine = both(*split_two(small_ref[...]))
    got = [piece[whole:, :].astype(F32) for piece in (got_near, got_far, got_out)]
    got = jnp.concatenate(got, axis=1)
    high, low = split_two(mine + (got[:, :width] + got[:, width:]))
    for out_ref in (o1, o2, o3):
        out_ref[rows:, :width] = high
        out_ref[rows:, width:] = low
    sum_ref[...] = both(high, low)


def shards_small_kernel(spot_ref, own_ref, g1, g2, g3, small_ref, kept_ref, send_ref):
    rows, width = kept_ref.shape
    got = [piece[:rows, :].astype(F32) for piece in (g1, g2, g3)]
    values = (own_ref[...] + got[0]) + (got[1] + got[2])
    kept_ref[...] = values[:, :width]
    send_ref[:rows, :] = values[:, width:].astype(BF16)
    count = small_ref.shape[0]
    got = [both(piece[rows:, :width], piece[rows:, width:]) for piece in (g1, g2, g3)]
    high, low = split_two((small_ref[...] + got[0]) + (got[1] + got[2]))
    send_ref[rows : rows + count, :] = high
    send_ref[rows + count :, :] = low


def owned_kernel(
    spot_ref, ffn_kept, ffn_one, ffn_two, kept_ref, sent_ref, got_ref, half_ref,
    out_ref, pass_ref,
):
    rows, width = kept_ref.shape
    half = half_ref.shape[0]
    pass_ref[:half, :] = half_ref[...]
    for i, piece in enumerate((ffn_one, ffn_two)):
        at = slice(i * width, (i + 1) * width)
        out_ref[:, at] = (ffn_kept[:, at] + piece[...].astype(F32)).astype(BF16)
    out_ref[:, 2 * width :] = (kept_ref[...] + got_ref[:rows, :].astype(F32)).astype(BF16)
    count = (sent_ref.shape[0] - rows) // 2
    top, end = slice(rows, rows + count), slice(rows + count, rows + 2 * count)
    mine = both(sent_ref[top, :], sent_ref[end, :])
    high, low = split_two(mine + both(got_ref[top, :], got_ref[end, :]))
    pass_ref[half : half + count, :] = high
    pass_ref[half + count :, :] = low


def sums_out(spot_ref, rows_ref, up_ref, qv_ref, lines):
    up_ref[...] = rows_ref[pl.ds(8 + spot_ref[2], 1), :]
    qv_ref[...] = rows_ref[6:8, window(spot_ref[2], qv_ref.shape[1])]
    for i, line_ref in enumerate(lines):
        line_ref[...] = rows_ref[i : i + 1, :]


def plain_sums_kernel(spot_ref, steps_ref, small_ref, table_ref, up_ref, qv_ref, *lines):
    table_ref[...] = jnp.zeros_like(table_ref)
    for place in range(steps_ref.shape[0]):
        at = pl.ds(steps_ref[place], 1)
        table_ref[at, :] = table_ref[at, :] + small_ref[12 + place : 13 + place, :]
    sums_out(spot_ref, small_ref, up_ref, qv_ref, lines)


def zero_kernel(spot_ref, table_hbm, block_ref, sems):
    block_ref[...] = jnp.zeros_like(block_ref)
    rows = block_ref.shape[0]
    fetch(
        [
            (block_ref, table_hbm.at[i * rows : (i + 1) * rows, :])
            for i in range(table_hbm.shape[0] // rows)
        ],
        sems,
    )


class Sends:
    def __init__(self, sems):
        self.sems, self.copies = sems, []

    def start(self, source, target, alone=None):
        copy = pltpu.make_async_copy(source, target, self.sems.at[len(self.copies)])
        self.copies.append((copy, alone))
        copy.start() if alone is None else pl.when(alone)(copy.start)

    def wait(self):
        for copy, alone in self.copies:
            copy.wait() if alone is None else pl.when(alone)(copy.wait)


def weights_kernel(
    spot_ref, p0, p1, p2, p3, up_hbm, down_hbm, qkv_hbm, proj_hbm,
    up_all, down_all, qkv_all, proj_all, sems,
):
    sends = Sends(sems)
    rows, hidden, cols = p0.shape[0], up_all.shape[1], proj_all.shape[1]
    pieces = (p0, p1, p2, p3)
    spots = [window(spot_ref[1] ^ bits, rows) for bits in range(4)]
    for i, (whole, target) in enumerate(((up_all, up_hbm), (down_all, down_hbm))):
        for spot, piece in zip(spots, pieces):
            whole[spot, :] = piece[:, i * hidden : (i + 1) * hidden].astype(F32)
        sends.start(whole, target)
    start = 2 * hidden
    for spot, piece in zip(spots, pieces):
        for i in range(3):
            qkv_all[i, spot, :] = piece[:, start + i * cols : start + (i + 1) * cols].astype(F32)
        proj_all[spot, :] = piece[:, start + 3 * cols :].astype(F32)
    sends.start(qkv_all, qkv_hbm)
    sends.start(proj_all, proj_hbm)
    sends.wait()


def close_kernel(
    spot_ref, steps_ref, out_own, out_one, out_two, in_own, in_far, zero_hbm,
    out_hbm, in_hbm, table_hbm, up_ref, qv_ref, *refs,
):
    lines, (out_all, in_all, rows_ref, blocks_ref, sems) = refs[:6], refs[6:]
    sends = Sends(sems)
    fill_rows(spot_ref, out_own, (out_one, out_two), out_all)
    sends.start(out_all, out_hbm)
    fill_rows(spot_ref, in_own, (in_far,), in_all)
    sends.start(in_all, in_hbm)
    start, count = out_one.shape[0] - 2 * rows_ref.shape[0], rows_ref.shape[0]
    parts = [
        both(ref[start : start + count, :], ref[start + count :, :]) for ref in (out_one, out_two)
    ]
    rows_ref[...] = parts[0] + parts[1]
    places = range(steps_ref.shape[0])
    at = lax.broadcasted_iota(jnp.int32, (8, 1), 0)
    for place in places:
        block = steps_ref[place] // 8
        total_rows = jnp.zeros(blocks_ref.shape[1:], F32)
        for other in places:
            step = steps_ref[other]
            row = jnp.where(step // 8 == block, step % 8, -1)
            total_rows = total_rows + jnp.where(at == row, rows_ref[12 + other : 13 + other, :], 0.0)
        blocks_ref[place] = total_rows
        seen = [steps_ref[other] // 8 == block for other in range(place)]
        alone = jnp.logical_not(functools.reduce(jnp.logical_or, seen)) if seen else None
        target = table_hbm.at[pl.ds(pl.multiple_of(block * 8, 8), 8), :]
        sends.start(blocks_ref.at[place], target, alone)
    sums_out(spot_ref, rows_ref, up_ref, qv_ref, lines)
    sends.wait()


class Reduction:
    def __init__(self, order, kept, small):
        self.order, self.kept, self.small = order, kept, small
        self.rows, self.width = kept.shape[0] // 4, kept.shape[1]

    def cut(self, got):
        rows, width, more = self.rows, self.width, self.small.shape[0]
        self.own, *cuts, self.small = self.order.call(
            cut_small_kernel,
            [((rows, width), F32)]
            + [((rows + more, width), BF16)] * 3
            + [(self.small.shape, F32)],
            [self.kept, *got, self.small],
        )
        self.got = [self.order.swap(cuts[bits - 1], "ctx", bits) for bits in (1, 2, 3)]

    def shards(self):
        rows, width, more = self.rows, self.width // 2, 2 * self.small.shape[0]
        self.own, self.sent = self.order.call(
            shards_small_kernel,
            [((rows, width), F32), ((rows + more, width), BF16)],
            [self.own, *self.got, self.small],
        )
        self.got = self.order.swap(self.sent, "tp", 2)


def reduce_plainly(kept, given, chunk):
    whole = jnp.concatenate([kept, given.astype(F32)])
    mine = lax.psum_scatter(whole, "fsdp", scatter_dimension=0, tiled=True)
    quarter = lax.psum_scatter(mine, "ctx", scatter_dimension=0, tiled=True)
    width = quarter.shape[1] // 2
    far = lax.ppermute(quarter[:, width:], "tp", [(i, i ^ 2) for i in range(4)])
    return lax.all_gather(quarter[:, :width] + far, "ctx", axis=0, tiled=True)


def pieces_of(order, part, parts, rows):
    if parts == 2:
        return part, order.swap(part, "fsdp", 1)
    whole = lax.all_gather(part[:rows], "fsdp", axis=0, tiled=True)
    size = whole.shape[0] // 2
    return whole[:size], whole[size:]


def per_device(
    layer_input,
    timesteps,
    segment_ids,
    time_table,
    ln1_gain,
    ln1_bias,
    w_qkv,
    b_qv,
    w_out_t,
    b_out,
    ln2_gain,
    ln2_bias,
    w_up,
    b_up,
    w_down_t,
    b_down,
    out_grad,
    *,
    parts,
):
    span, width = layer_input.shape[1:]
    rows, cols = w_qkv.shape[1:]
    hidden = w_up.shape[1]
    size = width // 2
    core = lax.axis_index("fsdp")
    chunk = lax.axis_index("ctx")
    shard = lax.axis_index("tp")
    place = core if parts == 2 else 0 * core
    spot = jnp.stack([place, chunk, shard, 2 * core + shard // 2]).astype(jnp.int32)
    order = Order(spot, parts)
    line = lambda values: values.reshape(1, -1)
    dma = lambda count: pltpu.SemaphoreType.DMA((count,))

    pack, qkv_part, out_part_own = order.call(
        pack_kernel,
        [
            ((rows + BIAS_ROWS, 4 * cols), BF16), ((rows + BIAS_ROWS, 3 * cols), BF16),
            ((rows, cols), BF16),
        ],
        [timesteps, w_qkv, w_out_t, b_qv, line(b_up)],
        far=range(5),
        scratch=[
            pltpu.VMEM(w_qkv.shape, F32),
            pltpu.VMEM(w_out_t.shape, F32),
            pltpu.VMEM(b_qv.shape, F32),
            pltpu.VMEM((1, hidden), F32),
            dma(4),
        ],
    )
    near = pieces_of(order, pack, parts, rows)
    pack_far = order.swap(qkv_part, "tp", 2)
    projected = [((span, cols), BF16), ((span, 2 * cols), BF16)]
    more = [((span, cols), BF16), ((span, 2 * cols), BF16)]
    q_near, kv_near, stream, normed, seg, lines = order.call(
        functools.partial(open_kernel, row=rows),
        projected
        + [
            ((span, width), F32), ((span, width), BF16), ((1, segment_ids.shape[1]), jnp.int32),
            ((8, width), F32),
        ],
        [timesteps, layer_input, time_table, segment_ids]
        + [line(v) for v in (ln1_gain, ln1_bias, ln2_gain, ln2_bias, b_out, b_down)]
        + [*near, pack],
        far=range(10),
        scratch=[
            pltpu.VMEM((span, width), F32),
            pltpu.VMEM((8, width), F32),
            pltpu.VMEM(segment_ids.shape, jnp.int32),
            pltpu.VMEM((6, 1, width), F32),
            dma(9),
        ],
    )
    kvs_near = [kv_near] + order.swap_three(kv_near, "ctx")
    project = functools.partial(project_kernel, row=rows)

    side_shape = (rows // 4 + rows // 8, 2 * hidden) if parts == 2 else (rows, cols)
    rest, side, cotan = order.call(
        pack_rest_kernel,
        [((rows, 2 * hidden), BF16), (side_shape, BF16), ((span, width), F32)],
        [out_part_own, w_up, w_down_t, out_grad],
        far=(1, 2, 3),
        scratch=[pltpu.VMEM(w_up.shape, F32), pltpu.VMEM(w_down_t.shape, F32), dma(3)],
        cost=QUICK,
    )
    side_far = order.swap(side, "tp", 2)
    if parts == 2:
        table = order.call(
            zero_kernel,
            [(time_table.shape, F32)],
            [],
            kept=(0,),
            scratch=[pltpu.VMEM((time_table.shape[0] // 5, width), F32), dma(5)],
            cost=QUICK,
        )[0]
    rest_near = pieces_of(order, rest, parts, rows)

    attended = [((span, cols), BF16), ((span, cols), F32)]
    pack_far, *kvs_near[1:] = hold(pack_far, *kvs_near[1:])
    far = pieces_of(order, pack_far, parts, rows)
    mixed_near, lse_near = order.call(
        attend_one_kernel, attended, [seg, q_near, *kvs_near], cost=COST
    )
    q_far, kv_far = order.call(project, more, [normed, *far, pack_far], cost=QUICK)
    kvs_far = [kv_far] + order.swap_three(kv_far, "ctx")
    if parts == 2:
        rest_far, out_far = order.call(
            unpack_kernel,
            [((rows // 4, 2 * hidden), BF16), ((rows, cols), BF16)],
            [side_far],
            cost=QUICK,
        )
        rest_turn = order.swap_turn(rest_far, 0)
    else:
        rest_far, out_far = order.swap(rest, "tp", 2), side_far
    out_far = pieces_of(order, out_far, parts, rows)
    mixed_far, lse_far, given = order.call(
        attend_two_kernel,
        attended + [((span, width), BF16)],
        [seg, q_far, *kvs_far, mixed_near, *near, *out_far],
    )
    got = order.swap(given, "tp", 1)
    if parts == 2:
        rest_one = order.call(
            stack_kernel, [((rows // 2, 2 * hidden), BF16)], [rest_far, rest_turn], cost=QUICK
        )[0]
        rest_two = order.swap_turn(rest_one, 1)
        rest_far = [
            rest_one, rest_two, order.swap(rest_one, "fsdp", 1), order.swap(rest_two, "fsdp", 1)
        ]
    else:
        rest_far = pieces_of(order, rest_far, parts, rows)

    acts = [((span, hidden), BF16), ((span, hidden), BF16), ((1, hidden), F32)]
    (
        back, ffn_terms, out_base, resid, normed_two, low, act_n, pre_n, up_near, act_f, pre_f, up_far,
    ) = order.call(
        functools.partial(ffn_kernel, row=rows),
        [
            ((span + PAD, width), BF16), ((span, width), BF16), ((span, width), F32),
            ((span, width), F32), ((span, width), BF16), ((span, width), BF16), *acts, *acts,
        ],
        [stream, given, got, cotan, lines, pack, pack_far, *rest_near, *rest_far],
        scratch=[pltpu.VMEM((span, width), F32)] * 2
        + [pltpu.VMEM((size, 2 * hidden), BF16)] * 2,
        limit=8,
    )
    back_got = order.swap(back, "tp", 1)
    ffn_kept, *ffn_sent = order.call(
        ffn_grads_kernel,
        [((size, 4 * hidden), F32)] + [((size, hidden), BF16)] * 4,
        [normed_two, low, act_n, pre_n, act_f, pre_f],
    )
    if parts == 2:
        ffn_got = [order.swap(piece, "fsdp", 1) for piece in ffn_sent]
        ffn_own, ffn_cut = order.call(
            cut_kernel,
            [((rows // 2, 4 * hidden), F32), ((rows // 2, 4 * hidden), BF16)],
            [ffn_kept, *ffn_got],
            cost=QUICK,
        )
        ffn_turn = order.swap_turn(ffn_cut, 0)
    dq, own, *shares, resid_grad, low_all, resid_rows = order.call(
        pull_kernel,
        [((span, 2 * cols), F32), ((span, 4 * cols), F32)]
        + [((span + PAD, 4 * cols), BF16)] * 3
        + [((span, width), F32), ((span, width), BF16), ((4, width), F32)],
        [
            seg, q_near, lse_near, *kvs_near, q_far, lse_far, *kvs_far, back, back_got, resid,
            cotan, lines, *near, *out_far,
        ],
        scratch=[pltpu.VMEM((2, span, width), F32)],
        limit=6,
    )
    shared = [order.swap(shares[bits - 1], "ctx", bits) for bits in (1, 2, 3)]

    terms_got = order.swap(ffn_terms, "tp", 1)
    if parts == 2:
        ffn_near, sent, out_low = order.call(
            middle_kernel,
            [
                ((rows // 2, 2 * hidden), F32), ((span // 2 + rows + 0 * PAD, width), BF16),
                ((span, width), BF16),
            ],
            [ffn_own, ffn_turn, out_base, ffn_terms, terms_got],
            cost=QUICK,
        )
        sent_got = order.swap(sent, "tp", 2)
    else:
        out_low = order.call(
            add_pair_kernel, [((span, width), BF16)], [out_base, ffn_terms, terms_got]
        )[0]
        half_rows = lax.dynamic_slice_in_dim(out_low, shard % 2 * (span // 2), span // 2, 0)
        out_half = order.swap(half_rows, "tp", 2)

    seqs = 2 * parts
    small_rows = -(-(12 + seqs) // 16) * 16
    in_terms, small, attention_kept, *attention_sent = order.call(
        input_kernel,
        [
            ((span, width), BF16), ((small_rows, width), F32),
            ((size, 8 * cols), F32), ((size + small_rows, 3 * cols), BF16),
            ((size + small_rows, 3 * cols), BF16), ((size + small_rows, 2 * cols), BF16),
        ],
        [
            stream, lines, resid_rows, up_near, up_far, dq, own, *shared, *near, *far,
            normed, low_all, mixed_near, mixed_far,
        ],
        scratch=[pltpu.VMEM((span, 6 * cols), BF16), pltpu.VMEM((span, width), F32)],
    )
    order.cost = QUICK
    if parts == 2:
        attention_far = [order.swap(piece, "fsdp", 1) for piece in attention_sent]
    in_got = order.swap(in_terms, "tp", 1)
    if parts == 2:
        sums = Reduction(order, attention_kept, small)
        sums.cut(attention_far)
        out_half, ffn_own, *ffn_cuts = order.call(
            settle_kernel,
            [((span // 2, width), BF16), ((rows // 4, 2 * hidden), F32)]
            + [((rows // 4, hidden), BF16)] * 2,
            [ffn_near, sent_got],
        )
        ffn_turns = [order.swap_turn(piece, 1) for piece in ffn_cuts]
        sums.shards()
    in_low = order.call(
        add_pair_kernel, [((span, width), BF16)], [resid_grad, in_terms, in_got]
    )[0]
    if parts == 2:
        in_low, sums.got = hold(in_low, sums.got)
    in_far = order.swap(in_low, "tp", 2)
    vectors = [((1, hidden), F32), ((2, cols), F32)] + [((1, width), F32)] * 6
    large = [((2 * span, width), F32)] * 2
    if parts == 2:
        owned, passed = order.call(
            owned_kernel,
            [
                ((rows // 4, 2 * hidden + 4 * cols), BF16),
                ((span // 2 + 2 * small_rows, width), BF16),
            ],
            [ffn_own, *ffn_turns, sums.own, sums.sent, sums.got, out_half],
        )
        passed_got = order.swap(passed, "tp", 1)
        pieces = [owned] + order.swap_three(owned, "ctx")
        bits = near[1][rows : rows + 9 : 3, 2 * cols : 2 * cols + 2].astype(F32)
        far_steps = jnp.sum(bits, axis=0).astype(jnp.int32)
        steps = jnp.where(
            core == 0,
            jnp.concatenate([timesteps, far_steps]),
            jnp.concatenate([far_steps, timesteps]),
        )
        whole = [
            ((rows, hidden), F32), ((rows, hidden), F32), ((3, rows, cols), F32),
            ((rows, cols), F32),
        ]
        grads_up, grads_down, grads_qkv, grads_out = order.call(
            weights_kernel,
            whole,
            pieces,
            kept=range(4),
            scratch=[pltpu.VMEM(shape, dtype) for shape, dtype in whole] + [dma(4)],
        )
        output, grad_input, table, *rest = order.call(
            close_kernel,
            large + [(time_table.shape, F32)] + vectors,
            [steps, out_low, passed, passed_got, in_low, in_far, table],
            far=(6,),
            kept=range(3),
            alias={6: 2},
            scratch=[pltpu.VMEM((2 * span, width), F32)] * 2
            + [
                pltpu.VMEM((small_rows, width), F32), pltpu.VMEM((seqs, 8, width), F32),
                dma(2 + seqs),
            ],
        )
    else:
        output, grad_input = order.call(
            rows_kernel, large, [out_low, out_half, order.swap(out_half, "tp", 1), in_low, in_far]
        )
        ffn_sent = jnp.concatenate(ffn_sent, axis=1)
        both_grads = reduce_plainly(ffn_kept, ffn_sent, chunk)
        grads_up, grads_down = both_grads[:, :hidden], both_grads[:, hidden:]
        near_part, far_part, out_columns = [piece[:size] for piece in attention_sent]
        attention_sent = jnp.concatenate(
            [near_part, out_columns[:, :cols], far_part, out_columns[:, cols:]], axis=1
        )
        every = reduce_plainly(attention_kept, attention_sent, chunk)
        grads_qkv = jnp.stack([every[:, i * cols : (i + 1) * cols] for i in range(3)])
        grads_out = every[:, 3 * cols :]
        small = lax.psum(small, ("fsdp", "ctx", "tp"))
        steps = lax.all_gather(timesteps, "fsdp", axis=0, tiled=True)
        table, *rest = order.call(
            plain_sums_kernel, [(time_table.shape, F32)] + vectors, [steps, small]
        )
    up_line, qv_lines, *sums = rest
    sums = [values.reshape(-1) for values in sums]

    shape = layer_input.shape
    return (
        output.reshape(shape),
        grad_input.reshape(shape),
        table,
        sums[0],
        sums[1],
        grads_qkv,
        qv_lines,
        grads_out,
        sums[4],
        sums[2],
        sums[3],
        grads_up,
        up_line.reshape(-1),
        grads_down,
        sums[5],
    )


def solution(mesh):
    placed = (
        P("fsdp", "ctx", None),
        P("fsdp"),
        P("fsdp", None),
        P(),
        P(),
        P(),
        P(None, "fsdp", "tp"),
        P(None, "tp"),
        P("fsdp", "tp"),
        P(),
        P(),
        P(),
        P("fsdp", "tp"),
        P("tp"),
        P("fsdp", "tp"),
        P(),
        P("fsdp", "ctx", None),
    )
    return jax.shard_map(
        functools.partial(per_device, parts=mesh.shape["fsdp"]),
        mesh=mesh,
        in_specs=placed,
        out_specs=(
            P("fsdp", "ctx", None),
            P("fsdp", "ctx", None),
            P(),
            P(),
            P(),
            P(None, "fsdp", "tp"),
            P(None, "tp"),
            P("fsdp", "tp"),
            P(),
            P(),
            P(),
            P("fsdp", "tp"),
            P("tp"),
            P("fsdp", "tp"),
            P(),
        ),
        check_vma=False,
    )
```

```python
import functools
import jax
import jax.numpy as jnp
from jax import lax
from jax.experimental import pallas as pl
from jax.experimental.pallas import tpu as pltpu
from jax.sharding import PartitionSpec as P

HEAD_DIM = 64
SCALE = HEAD_DIM ** (-0.5)
EPSILON = 1e-05
NEGATIVE = -1e30
F32 = jnp.float32
BF16 = jnp.bfloat16
BIAS_ROWS = 16
PAD = 16
CUBE = 0.044715
ROOT = 0.7978845608028654
COST, QUICK, LONG = 8_000_000_000, 1_000, 20_000_000_000
VMEM = pl.BlockSpec(memory_space=pltpu.VMEM)
SMEM = pl.BlockSpec(memory_space=pltpu.SMEM)


def dot_nn(left, right):
    return lax.dot_general(left, right, (((1,), (0,)), ((), ())), preferred_element_type=F32)


def dot_nt(left, right):
    return lax.dot_general(left, right, (((1,), (1,)), ((), ())), preferred_element_type=F32)


def dot_tn(left, right):
    return lax.dot_general(left, right, (((0,), (0,)), ((), ())), preferred_element_type=F32)


def total(values):
    return functools.reduce(jnp.add, values)


def norm_parts(values):
    centre = values - jnp.mean(values, axis=-1, keepdims=True)
    spread = jnp.mean(centre * centre, axis=-1, keepdims=True)
    inverse = lax.rsqrt(spread + EPSILON)
    return centre * inverse, inverse


def norm_back(grad, hat, inverse, gain):
    scaled = grad * gain
    mean_one = jnp.mean(scaled, axis=-1, keepdims=True)
    mean_two = jnp.mean(scaled * hat, axis=-1, keepdims=True)
    return inverse * (scaled - mean_one - hat * mean_two)


def column_sum(values):
    return jnp.sum(values, axis=0, keepdims=True)


def window(index, size):
    return pl.ds(pl.multiple_of(index * size, size), size)


def halves(spot_ref, size):
    return window(spot_ref[0], size), window(1 - spot_ref[0], size)


def hold(*values):
    return lax.optimization_barrier(values)


class Order:
    def __init__(self, spot, parts):
        self.spot, self.parts, self.cost = spot, parts, COST

    def call(self, kernel, outs, operands, *, far=(), kept=(), alias=None, scratch=(), limit=5, cost=None):
        specs = [
            SMEM if operand.ndim == 1
            else pl.BlockSpec(memory_space=pltpu.HBM if i in far else pltpu.VMEM)
            for i, operand in enumerate(operands)
        ]
        operands = [
            pltpu.with_memory_space_constraint(operand, pltpu.HBM) if i in far else operand
            for i, operand in enumerate(operands)
        ]
        count = len(operands)

        def body(*refs):
            kernel(refs[count], *refs[:count], *refs[count + 1 :])

        results = pl.pallas_call(
            body,
            out_shape=tuple(jax.ShapeDtypeStruct(shape, dtype) for shape, dtype in outs),
            in_specs=specs + [SMEM],
            out_specs=tuple(
                pl.BlockSpec(memory_space=pltpu.HBM) if i in kept else VMEM
                for i in range(len(outs))
            ),
            input_output_aliases=alias or {},
            scratch_shapes=list(scratch),
            compiler_params=pltpu.CompilerParams(vmem_limit_bytes=limit << 20),
            cost_estimate=pl.CostEstimate(
                flops=cost or self.cost, bytes_accessed=1 << 16, transcendentals=0
            ),
        )(*operands, self.spot)
        first, self.spot = hold(results[0], self.spot)
        return [first, *results[1:]]

    def swap(self, values, axis, bits):
        values, self.spot = hold(values, self.spot)
        size = 2 if axis == "fsdp" else 4
        with jax.named_scope("swap_%s_%d" % (axis, bits)):
            return lax.ppermute(values, axis, [(i, i ^ bits) for i in range(size)])

    def swap_three(self, values, axis):
        return [self.swap(values, axis, bits) for bits in (1, 2, 3)]

    def swap_turn(self, values, turn):
        if self.parts != 2:
            return self.swap(values, "ctx", 1 + turn)
        values, self.spot = hold(values, self.spot)
        pairs = [
            (4 * core + i, 4 * core + (i ^ (1 + (core + turn) % 2)))
            for core in range(2)
            for i in range(4)
        ]
        with jax.named_scope("swap_turn_%d" % turn):
            return lax.ppermute(values, ("fsdp", "ctx"), pairs)


def clear_below(ref, rows):
    if ref.shape[0] > rows:
        ref[rows:, :] = jnp.zeros((ref.shape[0] - rows, ref.shape[1]), ref.dtype)


def fetch(copies, sems):
    started = [
        pltpu.make_async_copy(source, target, sems.at[i])
        for i, (source, target) in enumerate(copies)
    ]
    for copy in started:
        copy.start()
    for copy in started:
        copy.wait()


def split_three(values):
    high = values.astype(BF16)
    rest = values - high.astype(F32)
    middle = rest.astype(BF16)
    return [high, middle, (rest - middle.astype(F32)).astype(BF16)]


def pack_kernel(
    spot_ref, steps_ref, w_hbm, out_hbm, qv_hbm, up_bias_hbm, pack_ref, qkv_ref, out_ref,
    w_ref, o_ref, qv_ref, up_bias_ref, sems,
):
    rows, cols = w_ref.shape[1:]
    fetch(
        [(w_hbm, w_ref), (out_hbm, o_ref), (qv_hbm, qv_ref), (up_bias_hbm, up_bias_ref)], sems
    )
    for i in range(3):
        pack_ref[:rows, i * cols : (i + 1) * cols] = w_ref[i].astype(BF16)
    pack_ref[:rows, 3 * cols :] = o_ref[...].astype(BF16)
    lanes = lax.broadcasted_iota(jnp.int32, (1, cols), 1)
    steps = jnp.zeros((1, cols), F32)
    for i in range(steps_ref.shape[0]):
        steps = jnp.where(lanes == i, steps_ref[i].astype(F32), steps)
    fill = jnp.zeros((1, cols), F32)
    up_bias = up_bias_ref[...]
    lines = [
        jnp.concatenate([qv_ref[0:1], qv_ref[1:2], steps, fill], axis=1),
        jnp.concatenate([up_bias[:, : 2 * cols], fill, fill], axis=1),
        jnp.concatenate([up_bias[:, 2 * cols :], fill, fill], axis=1),
    ]
    parts = split_three(jnp.concatenate(lines, axis=0))
    fill = jnp.zeros((BIAS_ROWS - 9, 4 * cols), F32)
    stack = jnp.concatenate([v.astype(F32) for v in parts] + [fill], axis=0)
    pack_ref[rows:, :] = stack.astype(BF16)
    qkv_ref[...] = pack_ref[:, : 3 * cols]
    out_ref[...] = pack_ref[:rows, 3 * cols :]


def pack_rest_kernel(
    spot_ref, own_out, up_hbm, down_hbm, cotan_hbm, rest_ref, side_ref, cotan_ref,
    up_ref, down_ref, sems,
):
    rows, hidden = up_ref.shape
    cols = own_out.shape[1]
    pair = spot_ref[2] // 2
    fetch([(up_hbm, up_ref), (down_hbm, down_ref), (cotan_hbm.at[pair], cotan_ref)], sems)
    rest_ref[:, :hidden] = up_ref[...].astype(BF16)
    rest_ref[:, hidden:] = down_ref[...].astype(BF16)
    if side_ref.shape[0] == rows:
        side_ref[...] = own_out[...]
        return
    quarter, fold = rows // 4, rows // 8
    mine = window(spot_ref[1], quarter)
    side_ref[:quarter, :hidden] = up_ref[mine, :].astype(BF16)
    side_ref[:quarter, hidden:] = down_ref[mine, :].astype(BF16)
    for i in range(8):
        block = own_out[i * fold : (i + 1) * fold, :]
        side_ref[quarter : quarter + fold, i * cols : (i + 1) * cols] = block
    clear_below(side_ref, quarter + fold)


def unpack_kernel(spot_ref, side_ref, quarter_ref, out_ref):
    rows, cols = out_ref.shape
    quarter, fold = rows // 4, rows // 8
    quarter_ref[...] = side_ref[:quarter, :]
    for i in range(8):
        block = side_ref[quarter : quarter + fold, i * cols : (i + 1) * cols]
        out_ref[i * fold : (i + 1) * fold, :] = block


def bias_lines(pack_ref, row):
    bits = pack_ref[row : row + BIAS_ROWS, :].astype(F32)
    lines = bits[0:3] + bits[3:6] + bits[6:9]
    half = 4 * HEAD_DIM
    return lines[0:1], jnp.concatenate([lines[1:2, :half], lines[2:3, :half]], axis=1)


def out_part(ref, size):
    cols = 2 * HEAD_DIM
    return ref[:size, ref.shape[1] - cols :]


def add_pair_kernel(spot_ref, base_ref, own_ref, got_ref, out_ref):
    span = base_ref.shape[0]
    terms = own_ref[:span, :].astype(F32) + got_ref[:span, :].astype(F32)
    out_ref[...] = (base_ref[...] + terms).astype(BF16)


def open_kernel(
    spot_ref, steps_ref, x_hbm, table_hbm, seg_hbm, g1, b1, g2, b2, bo, bd, one_ref, two_ref,
    bias_ref, q_ref, kv_ref, stream_ref, normed_ref, seg_ref, lines_ref,
    x_ref, table_ref, ids_ref, line_ref, sems, *, row,
):
    pair = spot_ref[2] // 2
    step = steps_ref[pair]
    block = pl.multiple_of(step // 8 * 8, 8)
    copies = [
        (x_hbm.at[pair], x_ref),
        (table_hbm.at[pl.ds(block, 8), :], table_ref),
        (seg_hbm, ids_ref),
    ]
    vectors = (g1, b1, g2, b2, bo, bd)
    fetch(copies + [(v, line_ref.at[i]) for i, v in enumerate(vectors)], sems)
    for i in range(len(vectors)):
        lines_ref[i : i + 1, :] = line_ref[i]
    seg_ref[...] = ids_ref[pl.ds(pair, 1), :]
    stream = x_ref[...] + table_ref[pl.ds(step % 8, 1), :]
    hat, _ = norm_parts(stream)
    stream_ref[...] = stream
    normed_ref[...] = (hat * line_ref[0] + line_ref[1]).astype(BF16)
    project_kernel(spot_ref, normed_ref, one_ref, two_ref, bias_ref, q_ref, kv_ref, row=row)


def project_kernel(spot_ref, normed_ref, one_ref, two_ref, bias_ref, q_ref, kv_ref, *, row):
    span, cols = q_ref.shape
    size = normed_ref.shape[1] // 2
    one, two = halves(spot_ref, size)
    raw = dot_nn(normed_ref[:, one], one_ref[:size, : 3 * cols])
    raw = raw + dot_nn(normed_ref[:, two], two_ref[:size, : 3 * cols])
    line, _ = bias_lines(bias_ref, row)
    q_bias, v_bias = line[:, :cols], line[:, cols : 2 * cols]
    q_ref[...] = (raw[:, :cols] + q_bias).astype(BF16)
    kv_ref[:span, :cols] = raw[:, cols : 2 * cols].astype(BF16)
    kv_ref[:span, cols:] = (raw[:, 2 * cols :] + v_bias).astype(BF16)
    clear_below(kv_ref, span)


def mask_biases(spot_ref, seg_ref, span):
    chunk = spot_ref[1]
    ids = [seg_ref[:, window(chunk ^ step, span)] for step in range(seg_ref.shape[1] // span)]
    own = jnp.broadcast_to(ids[0], (span, span)).T
    return [
        jnp.where(own == jnp.broadcast_to(step_ids, (span, span)), 0.0, NEGATIVE)
        for step_ids in ids
    ]


def lane_mask(shape, head):
    return (lax.broadcasted_iota(jnp.int32, shape, 1) // HEAD_DIM) == head


def attend_forward(spot_ref, seg_ref, q_ref, kvs, mixed_ref, lse_ref):
    span, width = q_ref.shape
    biases = mask_biases(spot_ref, seg_ref, span)
    query = q_ref[...]
    mixed, lse = None, None
    for head in range(width // HEAD_DIM):
        mine = lane_mask((span, width), head)
        masked = jnp.where(mine, query * SCALE, jnp.zeros_like(query))
        scores = [
            dot_nt(masked, kv[:span, :width]) + bias for kv, bias in zip(kvs, biases)
        ]
        top = functools.reduce(
            jnp.maximum, [jnp.max(block, axis=-1, keepdims=True) for block in scores]
        )
        grown = [jnp.exp(block - top) for block in scores]
        mass = total([jnp.sum(block, axis=-1, keepdims=True) for block in grown])
        share = 1.0 / mass
        out = total(
            [
                dot_nn((block * share).astype(BF16), kv[:span, width:])
                for block, kv in zip(grown, kvs)
            ]
        )
        log_mass = jnp.broadcast_to(top + jnp.log(mass), (span, width))
        mixed = out if head == 0 else jnp.where(mine, out, mixed)
        lse = log_mass if head == 0 else jnp.where(mine, log_mass, lse)
    mixed_ref[...] = mixed.astype(BF16)
    lse_ref[...] = lse


def attend_one_kernel(spot_ref, seg_ref, q_ref, kv0, kv1, kv2, kv3, mixed_ref, lse_ref):
    attend_forward(spot_ref, seg_ref, q_ref, (kv0, kv1, kv2, kv3), mixed_ref, lse_ref)


def attend_two_kernel(
    spot_ref, seg_ref, q_ref, kv0, kv1, kv2, kv3, near_ref, one_n, two_n, one_f, two_f,
    mixed_ref, lse_ref, given_ref,
):
    attend_forward(spot_ref, seg_ref, q_ref, (kv0, kv1, kv2, kv3), mixed_ref, lse_ref)
    size = given_ref.shape[1] // 2
    one, two = halves(spot_ref, size)
    near, far = near_ref[...], mixed_ref[...]
    for columns, near_w, far_w in ((one, one_n, one_f), (two, two_n, two_f)):
        terms = dot_nt(near, out_part(near_w, size)) + dot_nt(far, out_part(far_w, size))
        given_ref[: near.shape[0], columns] = terms.astype(BF16)
    clear_below(given_ref, near.shape[0])


def stack_kernel(spot_ref, one_ref, two_ref, out_ref):
    rows = out_ref.shape[0] // 2
    out_ref[:rows, :] = one_ref[:rows, :]
    out_ref[rows:, :] = two_ref[:rows, :]


def gelu_parts(x):
    square = x * x
    curve = jnp.tanh(ROOT * (x + CUBE * (x * square)))
    half = 0.5 * (1.0 + curve)
    slope = half + 0.5 * x * (1.0 - curve * curve) * (ROOT * (1.0 + 3.0 * CUBE * square))
    return x * half, slope


def ffn_side(
    normed_ref, low_ref, bias, first, second, columns, act_ref, pre_ref, sum_ref, *sums
):
    hidden = act_ref.shape[1]
    one, two = columns
    pre = dot_nn(normed_ref[:, one], first[:, :hidden])
    pre = pre + dot_nn(normed_ref[:, two], second[:, :hidden]) + bias
    value, slope = gelu_parts(pre)
    grad = dot_nn(low_ref[:, one], first[:, hidden:])
    grad = (grad + dot_nn(low_ref[:, two], second[:, hidden:])) * slope
    sum_ref[...] = column_sum(grad)
    act_ref[...] = value.astype(BF16)
    pre_ref[...] = grad.astype(BF16)
    act, pre_low = act_ref[...], pre_ref[...]
    for at, weights in zip(columns, (first, second)):
        back = dot_nt(pre_low, weights[:, :hidden])
        down = dot_nt(act, weights[:, hidden:])
        if len(sums) == 2:
            back_ref, out_ref = sums
        else:
            back_near, out_near, back_ref, out_ref = sums
            back, down = back + back_near[:, at], down + out_near[:, at]
        back_ref[: act.shape[0], at] = back.astype(back_ref.dtype)
        out_ref[: act.shape[0], at] = down.astype(out_ref.dtype)
    clear_below(sums[-2], act.shape[0])
    clear_below(sums[-1], act.shape[0])


def ffn_near_kernel(
    spot_ref, stream_ref, mine_ref, got_ref, cotan_ref, lines_ref, pack_ref, first, second,
    back_ref, ffn_ref, out_ref, resid_ref, normed_ref, act_ref, pre_ref, low_ref, sum_ref, *, row,
):
    span = stream_ref.shape[0]
    terms = mine_ref[:span, :].astype(F32) + got_ref[:span, :].astype(F32)
    resid = stream_ref[...] + terms + lines_ref[4:5, :]
    resid_ref[...] = resid
    out_ref[...] = resid + lines_ref[5:6, :]
    hat, _ = norm_parts(resid)
    normed_ref[...] = (hat * lines_ref[2:3, :] + lines_ref[3:4, :]).astype(BF16)
    low_ref[...] = cotan_ref[...].astype(BF16)
    ffn_side(
        normed_ref, low_ref, bias_lines(pack_ref, row)[1], first, second,
        halves(spot_ref, first.shape[0]), act_ref, pre_ref, sum_ref, back_ref, ffn_ref,
    )


def ffn_far_kernel(spot_ref, normed_ref, low_ref, back_near, ffn_near, pack_ref, *refs, row):
    count = len(refs) - 7
    pieces, outs, (first, second) = refs[:count], refs[count:-2], refs[-2:]
    if count == 2:
        first, second = pieces
    else:
        rows = pieces[0].shape[0] // 2
        turn, other = turn_bits(spot_ref)
        for target, pairs, bits in (
            (first, pieces[:2], (0, turn, other, 3)),
            (second, pieces[2:], (0, other, turn, 3)),
        ):
            for i in range(4):
                block = pairs[i // 2][i % 2 * rows : (i % 2 + 1) * rows, :]
                target[window(spot_ref[1] ^ bits[i], rows), :] = block
    act_ref, pre_ref, sum_ref, back_ref, ffn_ref = outs
    ffn_side(
        normed_ref, low_ref, bias_lines(pack_ref, row)[1], first, second,
        halves(spot_ref, first.shape[0]), act_ref, pre_ref, sum_ref, back_near, ffn_near,
        back_ref, ffn_ref,
    )


def ffn_kernel(
    spot_ref, stream_ref, mine_ref, got_ref, cotan_ref, lines_ref, pack_ref, far_pack, first, second,
    *refs, row,
):
    pieces, outs, scratch = refs[:-16], refs[-16:-4], refs[-4:]
    back_ref, down_ref, out_ref, resid_ref, normed_ref, low_ref = outs[:6]
    act_n, pre_n, sum_n, act_f, pre_f, sum_f = outs[6:]
    back_near, down_near, one, two = scratch
    ffn_near_kernel(
        spot_ref, stream_ref, mine_ref, got_ref, cotan_ref, lines_ref, pack_ref, first, second,
        back_near, down_near, out_ref, resid_ref, normed_ref, act_n, pre_n, low_ref, sum_n, row=row,
    )
    ffn_far_kernel(
        spot_ref, normed_ref, low_ref, back_near, down_near, far_pack, *pieces,
        act_f, pre_f, sum_f, back_ref, down_ref, one, two, row=row,
    )


def ffn_grads_kernel(
    spot_ref, normed_ref, low_ref, act_n, pre_n, act_f, pre_f, kept_ref, *given
):
    hidden = act_n.shape[1]
    one, two = halves(spot_ref, normed_ref.shape[1] // 2)
    for columns in (two, one):
        normed, low = normed_ref[:, columns], low_ref[:, columns]
        for i, (left, right) in enumerate(((normed, pre_n), (low, act_n), (normed, pre_f), (low, act_f))):
            grads = dot_tn(left, right[...])
            if columns is one:
                kept_ref[:, i * hidden : (i + 1) * hidden] = grads
            else:
                given[i][...] = grads.astype(BF16)


def resid_part(
    spot_ref, mine_ref, got_ref, resid_ref, cotan_ref, lines_ref, grad_ref, low_ref, rows_ref,
    work_ref,
):
    half = resid_ref.shape[0] // 2
    mine = window(spot_ref[2] % 2, half)
    span = resid_ref.shape[0]
    grad = mine_ref[:span, :].astype(F32) + got_ref[:span, :].astype(F32)
    hat, inverse = norm_parts(resid_ref[...])
    resid_grad = cotan_ref[...] + norm_back(grad, hat, inverse, lines_ref[2:3, :])
    grad_ref[...] = resid_grad
    low_ref[...] = resid_grad.astype(BF16)
    work_ref[0] = grad * hat
    work_ref[1] = grad
    sums = [work_ref[0, mine, :], work_ref[1, mine, :], grad_ref[mine, :], cotan_ref[mine, :]]
    rows_ref[...] = jnp.concatenate([column_sum(v) for v in sums], axis=0)


def attend_backward(spot_ref, seg_ref, q_ref, grad, lse_ref, kvs, dq_ref, outs, side):
    span, width = q_ref.shape
    biases = mask_biases(spot_ref, seg_ref, span)
    query = q_ref[...]
    dq, dks, dvs = None, [None] * 4, [None] * 4
    for head in range(width // HEAD_DIM):
        mine = lane_mask((span, width), head)
        masked_q = jnp.where(mine, query * SCALE, jnp.zeros_like(query))
        masked_g = jnp.where(mine, grad, jnp.zeros_like(grad))
        lse = lse_ref[:, head * HEAD_DIM : head * HEAD_DIM + 1]
        probs = [
            jnp.exp(dot_nt(masked_q, kv[:span, :width]) + bias - lse)
            for kv, bias in zip(kvs, biases)
        ]
        grads = [dot_nt(masked_g, kv[:span, width:]) for kv in kvs]
        inner = total([jnp.sum(p * g, axis=-1, keepdims=True) for p, g in zip(probs, grads)])
        raws = [(p * (g - inner)).astype(BF16) for p, g in zip(probs, grads)]
        head_dq = total([dot_nn(raw, kv[:span, :width]) for raw, kv in zip(raws, kvs)])
        dq = head_dq if head == 0 else jnp.where(mine, head_dq, dq)
        for step in range(4):
            head_dk = dot_tn(raws[step], query)
            head_dv = dot_tn(probs[step].astype(BF16), grad)
            dks[step] = head_dk if head == 0 else jnp.where(mine, head_dk, dks[step])
            dvs[step] = head_dv if head == 0 else jnp.where(mine, head_dv, dvs[step])
    dq_ref[:, side * width : (side + 1) * width] = dq * SCALE
    at = 2 * side * width
    for step in range(4):
        outs[step][:span, at : at + width] = (dks[step] * SCALE).astype(outs[step].dtype)
        outs[step][:span, at + width : at + 2 * width] = dvs[step].astype(outs[step].dtype)


def pull_kernel(
    spot_ref, seg_ref, q_n, lse_n, n0, n1, n2, n3, q_f, lse_f, f0, f1, f2, f3,
    mine_ref, got_ref, resid_ref, cotan_ref, lines_ref, one_n, two_n, one_f, two_f,
    dq_ref, own_ref, out1, out2, out3, grad_ref, low_ref, rows_ref, work_ref,
):
    size = low_ref.shape[1] // 2
    resid_part(
        spot_ref, mine_ref, got_ref, resid_ref, cotan_ref, lines_ref, grad_ref, low_ref, rows_ref,
        work_ref,
    )
    one, two = halves(spot_ref, size)
    outs = (own_ref, out1, out2, out3)
    near = (q_n, lse_n, (n0, n1, n2, n3), one_n, two_n)
    far = (q_f, lse_f, (f0, f1, f2, f3), one_f, two_f)
    for side, (q_ref, lse_ref, kvs, first, second) in enumerate((near, far)):
        grad = dot_nn(low_ref[:, one], out_part(first, size))
        grad = grad + dot_nn(low_ref[:, two], out_part(second, size))
        attend_backward(
            spot_ref, seg_ref, q_ref, grad.astype(BF16), lse_ref, kvs, dq_ref, outs, side
        )
    for out_ref in (out1, out2, out3):
        clear_below(out_ref, q_n.shape[0])


def input_kernel(
    spot_ref, stream_ref, lines_ref, rows_ref, up_near, up_far, dq_ref, own_ref, g1, g2, g3,
    one_n, two_n, one_f, two_f, normed_ref, low_ref, near_ref, far_ref,
    given_ref, small_ref, w_kept_ref, w_near_ref, w_far_ref, w_out_ref, pulled_ref, terms_ref,
):
    span, width = stream_ref.shape
    cols = dq_ref.shape[1] // 2
    size = width // 2
    shard, slot = spot_ref[2], spot_ref[3]
    far = shard ^ 2
    one, two = halves(spot_ref, size)
    small_ref[...] = jnp.zeros_like(small_ref)
    parts = [ref[:span, :].astype(F32) for ref in (g1, g2, g3)]
    got = (own_ref[...] + parts[0]) + (parts[1] + parts[2])
    for side, (place, up_sum) in enumerate(((shard, up_near), (far, up_far))):
        dq = dq_ref[:, side * cols : (side + 1) * cols]
        dkv = got[:, 2 * side * cols : 2 * (side + 1) * cols]
        at = side * 3 * cols
        pulled_ref[:, at : at + cols] = dq.astype(BF16)
        pulled_ref[:, at + cols : at + 3 * cols] = dkv.astype(BF16)
        small_ref[6:7, window(place, cols)] = column_sum(dq)
        small_ref[7:8, window(place, cols)] = column_sum(dkv[:, cols:])
        small_ref[pl.ds(8 + place, 1), :] = up_sum[...]
    for columns, near_w, far_w in ((one, one_n, one_f), (two, two_n, two_f)):
        back = dot_nt(pulled_ref[:, : 3 * cols], near_w[:size, : 3 * cols])
        back = back + dot_nt(pulled_ref[:, 3 * cols :], far_w[:size, : 3 * cols])
        terms_ref[:, columns] = back
    back = terms_ref[...]
    hat, inverse = norm_parts(stream_ref[...])
    small_ref[0:1, :] = column_sum(back * hat)
    small_ref[1:2, :] = column_sum(back)
    small_ref[2:6, :] = rows_ref[...]
    grad = norm_back(back, hat, inverse, lines_ref[0:1, :])
    small_ref[pl.ds(12 + slot, 1), :] = column_sum(grad) + rows_ref[2:3, :]
    given_ref[...] = grad.astype(BF16)
    given = (w_near_ref, w_far_ref)
    for columns in (two, one):
        normed, low = normed_ref[:, columns], low_ref[:, columns]
        for side, mixed in enumerate((near_ref, far_ref)):
            at, start = side * 3 * cols, side * 4 * cols
            qkv = dot_tn(normed, pulled_ref[:, at : at + 3 * cols])
            out = dot_tn(low, mixed[...])
            if columns is one:
                w_kept_ref[:, start : start + 3 * cols] = qkv
                w_kept_ref[:, start + 3 * cols : start + 4 * cols] = out
            else:
                given[side][:size, :] = qkv.astype(BF16)
                w_out_ref[:size, side * cols : (side + 1) * cols] = out.astype(BF16)
    both_parts = jnp.concatenate(split_two(small_ref[...]), axis=1)
    w_near_ref[size:, :] = both_parts[:, : 3 * cols]
    w_far_ref[size:, :] = both_parts[:, 3 * cols : 6 * cols]
    w_out_ref[size:, :] = both_parts[:, 6 * cols :]


def turn_bits(spot_ref):
    return 1 + spot_ref[0], 2 - spot_ref[0]


def split_two(values):
    high = values.astype(BF16)
    return high, (values - high.astype(F32)).astype(BF16)


def both(high, low):
    return high.astype(F32) + low.astype(F32)


def cut_kernel(spot_ref, kept_ref, *refs):
    got, (own_ref, send_ref) = refs[:4], refs[4:]
    rows, width = own_ref.shape[0] // 2, got[0].shape[1]
    chunk = spot_ref[1]
    first, second = turn_bits(spot_ref)
    for spot, place in enumerate((chunk, chunk ^ second)):
        to = slice(spot * rows, (spot + 1) * rows)
        for i, piece in enumerate(got):
            columns = slice(i * width, (i + 1) * width)
            at = window(place, rows)
            own_ref[to, columns] = kept_ref[at, columns] + piece[at, :].astype(F32)
            at = window(place ^ first, rows)
            values = kept_ref[at, columns] + piece[at, :].astype(F32)
            send_ref[to, columns] = values.astype(BF16)


def middle_kernel(
    spot_ref, kept_ref, got_ref, base_ref, own_terms, got_terms, near_ref, send_ref, out_ref
):
    rows, width = near_ref.shape
    span = base_ref.shape[0]
    values = kept_ref[...] + got_ref[...].astype(F32)
    near_ref[...] = values[:, :width]
    terms = own_terms[:span, :].astype(F32) + got_terms[:span, :].astype(F32)
    out_ref[...] = (base_ref[...] + terms).astype(BF16)
    send_ref[: span // 2, :] = out_ref[window(spot_ref[2] % 2, span // 2), :]
    half = send_ref.shape[1]
    for i in range(width // half):
        at = span // 2 + i * rows
        columns = slice(width + i * half, width + (i + 1) * half)
        send_ref[at : at + rows, :] = values[:, columns].astype(BF16)
    clear_below(send_ref, span // 2 + width // half * rows)


def settle_kernel(spot_ref, near_ref, got_ref, out_ref, own_ref, *sends):
    rows, width = own_ref.shape
    span = out_ref.shape[0]
    out_ref[...] = got_ref[:span, :]
    half = got_ref.shape[1]
    for i in range(width // half):
        at, columns = span + 2 * i * rows, slice(i * half, (i + 1) * half)
        own_ref[:, columns] = near_ref[:rows, columns] + got_ref[at : at + rows, :].astype(F32)
        more = near_ref[rows:, columns] + got_ref[at + rows : at + 2 * rows, :].astype(F32)
        sends[i][...] = more.astype(BF16)


def fill_rows(spot_ref, own_ref, others, out_ref):
    pair, bit, span = spot_ref[2] // 2, spot_ref[2] % 2, own_ref.shape[0]
    out_ref[window(pair, span), :] = own_ref[...].astype(F32)
    if len(others) == 1:
        out_ref[window(1 - pair, span), :] = others[0][...].astype(F32)
    else:
        for i, other in enumerate(others):
            at = 2 * (1 - pair) + (bit ^ i)
            out_ref[window(at, span // 2), :] = other[: span // 2, :].astype(F32)


def rows_kernel(spot_ref, out_own, out_one, out_two, in_own, in_far, out_ref, in_ref):
    fill_rows(spot_ref, out_own, (out_one, out_two), out_ref)
    fill_rows(spot_ref, in_own, (in_far,), in_ref)


def cut_small_kernel(
    spot_ref, kept_ref, got_near, got_far, got_out, small_ref, own_ref, o1, o2, o3, sum_ref
):
    rows, width = own_ref.shape[0], small_ref.shape[1]
    whole = kept_ref.shape[0]
    for bits, out_ref in enumerate((own_ref, o1, o2, o3)):
        at = window(spot_ref[1] ^ bits, rows)
        for side, got_ref in enumerate((got_near, got_far)):
            cols = got_ref.shape[1] // 3
            got = (got_ref[at, :], got_out[at, side * cols : (side + 1) * cols])
            for part, start, stop in ((got[0], 0, 3 * cols), (got[1], 3 * cols, 4 * cols)):
                columns = slice(side * width + start, side * width + stop)
                values = kept_ref[at, columns] + part.astype(F32)
                out_ref[:rows, columns] = values.astype(out_ref.dtype)
    mine = both(*split_two(small_ref[...]))
    got = [piece[whole:, :].astype(F32) for piece in (got_near, got_far, got_out)]
    got = jnp.concatenate(got, axis=1)
    high, low = split_two(mine + (got[:, :width] + got[:, width:]))
    for out_ref in (o1, o2, o3):
        out_ref[rows:, :width] = high
        out_ref[rows:, width:] = low
    sum_ref[...] = both(high, low)


def shards_small_kernel(spot_ref, own_ref, g1, g2, g3, small_ref, kept_ref, send_ref):
    rows, width = kept_ref.shape
    got = [piece[:rows, :].astype(F32) for piece in (g1, g2, g3)]
    values = (own_ref[...] + got[0]) + (got[1] + got[2])
    kept_ref[...] = values[:, :width]
    send_ref[:rows, :] = values[:, width:].astype(BF16)
    count = small_ref.shape[0]
    got = [both(piece[rows:, :width], piece[rows:, width:]) for piece in (g1, g2, g3)]
    high, low = split_two((small_ref[...] + got[0]) + (got[1] + got[2]))
    send_ref[rows : rows + count, :] = high
    send_ref[rows + count :, :] = low


def owned_kernel(
    spot_ref, ffn_kept, ffn_one, ffn_two, kept_ref, sent_ref, got_ref, half_ref,
    out_ref, pass_ref,
):
    rows, width = kept_ref.shape
    half = half_ref.shape[0]
    pass_ref[:half, :] = half_ref[...]
    for i, piece in enumerate((ffn_one, ffn_two)):
        at = slice(i * width, (i + 1) * width)
        out_ref[:, at] = (ffn_kept[:, at] + piece[...].astype(F32)).astype(BF16)
    out_ref[:, 2 * width :] = (kept_ref[...] + got_ref[:rows, :].astype(F32)).astype(BF16)
    count = (sent_ref.shape[0] - rows) // 2
    top, end = slice(rows, rows + count), slice(rows + count, rows + 2 * count)
    mine = both(sent_ref[top, :], sent_ref[end, :])
    high, low = split_two(mine + both(got_ref[top, :], got_ref[end, :]))
    pass_ref[half : half + count, :] = high
    pass_ref[half + count :, :] = low


def sums_out(spot_ref, rows_ref, up_ref, qv_ref, lines):
    up_ref[...] = rows_ref[pl.ds(8 + spot_ref[2], 1), :]
    qv_ref[...] = rows_ref[6:8, window(spot_ref[2], qv_ref.shape[1])]
    for i, line_ref in enumerate(lines):
        line_ref[...] = rows_ref[i : i + 1, :]


def plain_sums_kernel(spot_ref, steps_ref, small_ref, table_ref, up_ref, qv_ref, *lines):
    table_ref[...] = jnp.zeros_like(table_ref)
    for place in range(steps_ref.shape[0]):
        at = pl.ds(steps_ref[place], 1)
        table_ref[at, :] = table_ref[at, :] + small_ref[12 + place : 13 + place, :]
    sums_out(spot_ref, small_ref, up_ref, qv_ref, lines)


def zero_kernel(spot_ref, table_hbm, block_ref, sems):
    block_ref[...] = jnp.zeros_like(block_ref)
    rows = block_ref.shape[0]
    fetch(
        [
            (block_ref, table_hbm.at[i * rows : (i + 1) * rows, :])
            for i in range(table_hbm.shape[0] // rows)
        ],
        sems,
    )


class Sends:
    def __init__(self, sems):
        self.sems, self.copies = sems, []

    def start(self, source, target, alone=None):
        copy = pltpu.make_async_copy(source, target, self.sems.at[len(self.copies)])
        self.copies.append((copy, alone))
        copy.start() if alone is None else pl.when(alone)(copy.start)

    def wait(self):
        for copy, alone in self.copies:
            copy.wait() if alone is None else pl.when(alone)(copy.wait)


def weights_kernel(
    spot_ref, p0, p1, p2, p3, up_hbm, down_hbm, qkv_hbm, proj_hbm,
    up_all, down_all, qkv_all, proj_all, sems,
):
    sends = Sends(sems)
    rows, hidden, cols = p0.shape[0], up_all.shape[1], proj_all.shape[1]
    pieces = (p0, p1, p2, p3)
    spots = [window(spot_ref[1] ^ bits, rows) for bits in range(4)]
    for i, (whole, target) in enumerate(((up_all, up_hbm), (down_all, down_hbm))):
        for spot, piece in zip(spots, pieces):
            whole[spot, :] = piece[:, i * hidden : (i + 1) * hidden].astype(F32)
        sends.start(whole, target)
    start = 2 * hidden
    for spot, piece in zip(spots, pieces):
        for i in range(3):
            qkv_all[i, spot, :] = piece[:, start + i * cols : start + (i + 1) * cols].astype(F32)
        proj_all[spot, :] = piece[:, start + 3 * cols :].astype(F32)
    sends.start(qkv_all, qkv_hbm)
    sends.start(proj_all, proj_hbm)
    sends.wait()


def close_kernel(
    spot_ref, steps_ref, out_own, out_one, out_two, in_own, in_far, zero_hbm,
    out_hbm, in_hbm, table_hbm, up_ref, qv_ref, *refs,
):
    lines, (out_all, in_all, rows_ref, blocks_ref, sems) = refs[:6], refs[6:]
    sends = Sends(sems)
    fill_rows(spot_ref, out_own, (out_one, out_two), out_all)
    sends.start(out_all, out_hbm)
    fill_rows(spot_ref, in_own, (in_far,), in_all)
    sends.start(in_all, in_hbm)
    start, count = out_one.shape[0] - 2 * rows_ref.shape[0], rows_ref.shape[0]
    parts = [
        both(ref[start : start + count, :], ref[start + count :, :]) for ref in (out_one, out_two)
    ]
    rows_ref[...] = parts[0] + parts[1]
    places = range(steps_ref.shape[0])
    at = lax.broadcasted_iota(jnp.int32, (8, 1), 0)
    for place in places:
        block = steps_ref[place] // 8
        total_rows = jnp.zeros(blocks_ref.shape[1:], F32)
        for other in places:
            step = steps_ref[other]
            row = jnp.where(step // 8 == block, step % 8, -1)
            total_rows = total_rows + jnp.where(at == row, rows_ref[12 + other : 13 + other, :], 0.0)
        blocks_ref[place] = total_rows
        seen = [steps_ref[other] // 8 == block for other in range(place)]
        alone = jnp.logical_not(functools.reduce(jnp.logical_or, seen)) if seen else None
        target = table_hbm.at[pl.ds(pl.multiple_of(block * 8, 8), 8), :]
        sends.start(blocks_ref.at[place], target, alone)
    sums_out(spot_ref, rows_ref, up_ref, qv_ref, lines)
    sends.wait()


class Reduction:
    def __init__(self, order, kept, small):
        self.order, self.kept, self.small = order, kept, small
        self.rows, self.width = kept.shape[0] // 4, kept.shape[1]

    def cut(self, got):
        rows, width, more = self.rows, self.width, self.small.shape[0]
        self.own, *cuts, self.small = self.order.call(
            cut_small_kernel,
            [((rows, width), F32)]
            + [((rows + more, width), BF16)] * 3
            + [(self.small.shape, F32)],
            [self.kept, *got, self.small],
        )
        self.got = [self.order.swap(cuts[bits - 1], "ctx", bits) for bits in (1, 2, 3)]

    def shards(self):
        rows, width, more = self.rows, self.width // 2, 2 * self.small.shape[0]
        self.own, self.sent = self.order.call(
            shards_small_kernel,
            [((rows, width), F32), ((rows + more, width), BF16)],
            [self.own, *self.got, self.small],
        )
        self.got = self.order.swap(self.sent, "tp", 2)


def reduce_plainly(kept, given, chunk):
    whole = jnp.concatenate([kept, given.astype(F32)])
    mine = lax.psum_scatter(whole, "fsdp", scatter_dimension=0, tiled=True)
    quarter = lax.psum_scatter(mine, "ctx", scatter_dimension=0, tiled=True)
    width = quarter.shape[1] // 2
    far = lax.ppermute(quarter[:, width:], "tp", [(i, i ^ 2) for i in range(4)])
    return lax.all_gather(quarter[:, :width] + far, "ctx", axis=0, tiled=True)


def pieces_of(order, part, parts, rows):
    if parts == 2:
        return part, order.swap(part, "fsdp", 1)
    whole = lax.all_gather(part[:rows], "fsdp", axis=0, tiled=True)
    size = whole.shape[0] // 2
    return whole[:size], whole[size:]


def per_device(
    layer_input,
    timesteps,
    segment_ids,
    time_table,
    ln1_gain,
    ln1_bias,
    w_qkv,
    b_qv,
    w_out_t,
    b_out,
    ln2_gain,
    ln2_bias,
    w_up,
    b_up,
    w_down_t,
    b_down,
    out_grad,
    *,
    parts,
):
    span, width = layer_input.shape[1:]
    rows, cols = w_qkv.shape[1:]
    hidden = w_up.shape[1]
    size = width // 2
    core = lax.axis_index("fsdp")
    chunk = lax.axis_index("ctx")
    shard = lax.axis_index("tp")
    place = core if parts == 2 else 0 * core
    spot = jnp.stack([place, chunk, shard, 2 * core + shard // 2]).astype(jnp.int32)
    order = Order(spot, parts)
    line = lambda values: values.reshape(1, -1)
    dma = lambda count: pltpu.SemaphoreType.DMA((count,))

    pack, qkv_part, out_part_own = order.call(
        pack_kernel,
        [
            ((rows + BIAS_ROWS, 4 * cols), BF16), ((rows + BIAS_ROWS, 3 * cols), BF16),
            ((rows, cols), BF16),
        ],
        [timesteps, w_qkv, w_out_t, b_qv, line(b_up)],
        far=range(5),
        scratch=[
            pltpu.VMEM(w_qkv.shape, F32),
            pltpu.VMEM(w_out_t.shape, F32),
            pltpu.VMEM(b_qv.shape, F32),
            pltpu.VMEM((1, hidden), F32),
            dma(4),
        ],
    )
    near = pieces_of(order, pack, parts, rows)
    pack_far = order.swap(qkv_part, "tp", 2)
    projected = [((span, cols), BF16), ((span, 2 * cols), BF16)]
    more = [((span, cols), BF16), ((span, 2 * cols), BF16)]
    q_near, kv_near, stream, normed, seg, lines = order.call(
        functools.partial(open_kernel, row=rows),
        projected
        + [
            ((span, width), F32), ((span, width), BF16), ((1, segment_ids.shape[1]), jnp.int32),
            ((8, width), F32),
        ],
        [timesteps, layer_input, time_table, segment_ids]
        + [line(v) for v in (ln1_gain, ln1_bias, ln2_gain, ln2_bias, b_out, b_down)]
        + [*near, pack],
        far=range(10),
        scratch=[
            pltpu.VMEM((span, width), F32),
            pltpu.VMEM((8, width), F32),
            pltpu.VMEM(segment_ids.shape, jnp.int32),
            pltpu.VMEM((6, 1, width), F32),
            dma(9),
        ],
    )
    kvs_near = [kv_near] + order.swap_three(kv_near, "ctx")
    project = functools.partial(project_kernel, row=rows)

    side_shape = (rows // 4 + rows // 8, 2 * hidden) if parts == 2 else (rows, cols)
    rest, side, cotan = order.call(
        pack_rest_kernel,
        [((rows, 2 * hidden), BF16), (side_shape, BF16), ((span, width), F32)],
        [out_part_own, w_up, w_down_t, out_grad],
        far=(1, 2, 3),
        scratch=[pltpu.VMEM(w_up.shape, F32), pltpu.VMEM(w_down_t.shape, F32), dma(3)],
        cost=QUICK,
    )
    side_far = order.swap(side, "tp", 2)
    if parts == 2:
        table = order.call(
            zero_kernel,
            [(time_table.shape, F32)],
            [],
            kept=(0,),
            scratch=[pltpu.VMEM((time_table.shape[0] // 5, width), F32), dma(5)],
            cost=QUICK,
        )[0]
    rest_near = pieces_of(order, rest, parts, rows)

    attended = [((span, cols), BF16), ((span, cols), F32)]
    pack_far, *kvs_near[1:] = hold(pack_far, *kvs_near[1:])
    far = pieces_of(order, pack_far, parts, rows)
    mixed_near, lse_near = order.call(
        attend_one_kernel, attended, [seg, q_near, *kvs_near], cost=COST
    )
    q_far, kv_far = order.call(project, more, [normed, *far, pack_far], cost=QUICK)
    kvs_far = [kv_far] + order.swap_three(kv_far, "ctx")
    if parts == 2:
        rest_far, out_far = order.call(
            unpack_kernel,
            [((rows // 4, 2 * hidden), BF16), ((rows, cols), BF16)],
            [side_far],
            cost=QUICK,
        )
        rest_turn = order.swap_turn(rest_far, 0)
    else:
        rest_far, out_far = order.swap(rest, "tp", 2), side_far
    out_far = pieces_of(order, out_far, parts, rows)
    mixed_far, lse_far, given = order.call(
        attend_two_kernel,
        attended + [((span, width), BF16)],
        [seg, q_far, *kvs_far, mixed_near, *near, *out_far],
    )
    got = order.swap(given, "tp", 1)
    if parts == 2:
        rest_one = order.call(
            stack_kernel, [((rows // 2, 2 * hidden), BF16)], [rest_far, rest_turn], cost=QUICK
        )[0]
        rest_two = order.swap_turn(rest_one, 1)
        rest_far = [
            rest_one, rest_two, order.swap(rest_one, "fsdp", 1), order.swap(rest_two, "fsdp", 1)
        ]
    else:
        rest_far = pieces_of(order, rest_far, parts, rows)

    acts = [((span, hidden), BF16), ((span, hidden), BF16), ((1, hidden), F32)]
    (
        back, ffn_terms, out_base, resid, normed_two, low, act_n, pre_n, up_near, act_f, pre_f, up_far,
    ) = order.call(
        functools.partial(ffn_kernel, row=rows),
        [
            ((span + PAD, width), BF16), ((span, width), BF16), ((span, width), F32),
            ((span, width), F32), ((span, width), BF16), ((span, width), BF16), *acts, *acts,
        ],
        [stream, given, got, cotan, lines, pack, pack_far, *rest_near, *rest_far],
        scratch=[pltpu.VMEM((span, width), F32)] * 2
        + [pltpu.VMEM((size, 2 * hidden), BF16)] * 2,
        limit=8,
    )
    back_got = order.swap(back, "tp", 1)
    ffn_kept, *ffn_sent = order.call(
        ffn_grads_kernel,
        [((size, 4 * hidden), F32)] + [((size, hidden), BF16)] * 4,
        [normed_two, low, act_n, pre_n, act_f, pre_f],
    )
    if parts == 2:
        ffn_got = [order.swap(piece, "fsdp", 1) for piece in ffn_sent]
        ffn_own, ffn_cut = order.call(
            cut_kernel,
            [((rows // 2, 4 * hidden), F32), ((rows // 2, 4 * hidden), BF16)],
            [ffn_kept, *ffn_got],
            cost=QUICK,
        )
        ffn_turn = order.swap_turn(ffn_cut, 0)
    dq, own, *shares, resid_grad, low_all, resid_rows = order.call(
        pull_kernel,
        [((span, 2 * cols), F32), ((span, 4 * cols), F32)]
        + [((span + PAD, 4 * cols), BF16)] * 3
        + [((span, width), F32), ((span, width), BF16), ((4, width), F32)],
        [
            seg, q_near, lse_near, *kvs_near, q_far, lse_far, *kvs_far, back, back_got, resid,
            cotan, lines, *near, *out_far,
        ],
        scratch=[pltpu.VMEM((2, span, width), F32)],
        limit=6,
    )
    shared = [order.swap(shares[bits - 1], "ctx", bits) for bits in (1, 2, 3)]

    terms_got = order.swap(ffn_terms, "tp", 1)
    if parts == 2:
        ffn_near, sent, out_low = order.call(
            middle_kernel,
            [
                ((rows // 2, 2 * hidden), F32), ((span // 2 + rows + 0 * PAD, width), BF16),
                ((span, width), BF16),
            ],
            [ffn_own, ffn_turn, out_base, ffn_terms, terms_got],
            cost=QUICK,
        )
        sent_got = order.swap(sent, "tp", 2)
    else:
        out_low = order.call(
            add_pair_kernel, [((span, width), BF16)], [out_base, ffn_terms, terms_got]
        )[0]
        half_rows = lax.dynamic_slice_in_dim(out_low, shard % 2 * (span // 2), span // 2, 0)
        out_half = order.swap(half_rows, "tp", 2)

    seqs = 2 * parts
    small_rows = -(-(12 + seqs) // 16) * 16
    in_terms, small, attention_kept, *attention_sent = order.call(
        input_kernel,
        [
            ((span, width), BF16), ((small_rows, width), F32),
            ((size, 8 * cols), F32), ((size + small_rows, 3 * cols), BF16),
            ((size + small_rows, 3 * cols), BF16), ((size + small_rows, 2 * cols), BF16),
        ],
        [
            stream, lines, resid_rows, up_near, up_far, dq, own, *shared, *near, *far,
            normed, low_all, mixed_near, mixed_far,
        ],
        scratch=[pltpu.VMEM((span, 6 * cols), BF16), pltpu.VMEM((span, width), F32)],
    )
    order.cost = QUICK
    if parts == 2:
        attention_far = [order.swap(piece, "fsdp", 1) for piece in attention_sent]
    in_got = order.swap(in_terms, "tp", 1)
    if parts == 2:
        sums = Reduction(order, attention_kept, small)
        sums.cut(attention_far)
        out_half, ffn_own, *ffn_cuts = order.call(
            settle_kernel,
            [((span // 2, width), BF16), ((rows // 4, 2 * hidden), F32)]
            + [((rows // 4, hidden), BF16)] * 2,
            [ffn_near, sent_got],
        )
        ffn_turns = [order.swap_turn(piece, 1) for piece in ffn_cuts]
        sums.shards()
    in_low = order.call(
        add_pair_kernel, [((span, width), BF16)], [resid_grad, in_terms, in_got]
    )[0]
    if parts == 2:
        in_low, sums.got = hold(in_low, sums.got)
    in_far = order.swap(in_low, "tp", 2)
    vectors = [((1, hidden), F32), ((2, cols), F32)] + [((1, width), F32)] * 6
    large = [((2 * span, width), F32)] * 2
    if parts == 2:
        owned, passed = order.call(
            owned_kernel,
            [
                ((rows // 4, 2 * hidden + 4 * cols), BF16),
                ((span // 2 + 2 * small_rows, width), BF16),
            ],
            [ffn_own, *ffn_turns, sums.own, sums.sent, sums.got, out_half],
        )
        passed_got = order.swap(passed, "tp", 1)
        pieces = [owned] + order.swap_three(owned, "ctx")
        bits = near[1][rows : rows + 9 : 3, 2 * cols : 2 * cols + 2].astype(F32)
        far_steps = jnp.sum(bits, axis=0).astype(jnp.int32)
        steps = jnp.where(
            core == 0,
            jnp.concatenate([timesteps, far_steps]),
            jnp.concatenate([far_steps, timesteps]),
        )
        whole = [
            ((rows, hidden), F32), ((rows, hidden), F32), ((3, rows, cols), F32),
            ((rows, cols), F32),
        ]
        grads_up, grads_down, grads_qkv, grads_out = order.call(
            weights_kernel,
            whole,
            pieces,
            kept=range(4),
            scratch=[pltpu.VMEM(shape, dtype) for shape, dtype in whole] + [dma(4)],
        )
        output, grad_input, table, *rest = order.call(
            close_kernel,
            large + [(time_table.shape, F32)] + vectors,
            [steps, out_low, passed, passed_got, in_low, in_far, table],
            far=(6,),
            kept=range(3),
            alias={6: 2},
            scratch=[pltpu.VMEM((2 * span, width), F32)] * 2
            + [
                pltpu.VMEM((small_rows, width), F32), pltpu.VMEM((seqs, 8, width), F32),
                dma(2 + seqs),
            ],
        )
    else:
        output, grad_input = order.call(
            rows_kernel, large, [out_low, out_half, order.swap(out_half, "tp", 1), in_low, in_far]
        )
        ffn_sent = jnp.concatenate(ffn_sent, axis=1)
        both_grads = reduce_plainly(ffn_kept, ffn_sent, chunk)
        grads_up, grads_down = both_grads[:, :hidden], both_grads[:, hidden:]
        near_part, far_part, out_columns = [piece[:size] for piece in attention_sent]
        attention_sent = jnp.concatenate(
            [near_part, out_columns[:, :cols], far_part, out_columns[:, cols:]], axis=1
        )
        every = reduce_plainly(attention_kept, attention_sent, chunk)
        grads_qkv = jnp.stack([every[:, i * cols : (i + 1) * cols] for i in range(3)])
        grads_out = every[:, 3 * cols :]
        small = lax.psum(small, ("fsdp", "ctx", "tp"))
        steps = lax.all_gather(timesteps, "fsdp", axis=0, tiled=True)
        table, *rest = order.call(
            plain_sums_kernel, [(time_table.shape, F32)] + vectors, [steps, small]
        )
    up_line, qv_lines, *sums = rest
    sums = [values.reshape(-1) for values in sums]

    shape = layer_input.shape
    return (
        output.reshape(shape),
        grad_input.reshape(shape),
        table,
        sums[0],
        sums[1],
        grads_qkv,
        qv_lines,
        grads_out,
        sums[4],
        sums[2],
        sums[3],
        grads_up,
        up_line.reshape(-1),
        grads_down,
        sums[5],
    )


def solution(mesh):
    placed = (
        P("fsdp", "ctx", None),
        P("fsdp"),
        P("fsdp", None),
        P(),
        P(),
        P(),
        P(None, "fsdp", "tp"),
        P(None, "tp"),
        P("fsdp", "tp"),
        P(),
        P(),
        P(),
        P("fsdp", "tp"),
        P("tp"),
        P("fsdp", "tp"),
        P(),
        P("fsdp", "ctx", None),
    )
    return jax.shard_map(
        functools.partial(per_device, parts=mesh.shape["fsdp"]),
        mesh=mesh,
        in_specs=placed,
        out_specs=(
            P("fsdp", "ctx", None),
            P("fsdp", "ctx", None),
            P(),
            P(),
            P(),
            P(None, "fsdp", "tp"),
            P(None, "tp"),
            P("fsdp", "tp"),
            P(),
            P(),
            P(),
            P("fsdp", "tp"),
            P("tp"),
            P("fsdp", "tp"),
            P(),
        ),
        check_vma=False,
    )
```

```python
import functools
import jax
import jax.numpy as jnp
from jax import lax
from jax.experimental import pallas as pl
from jax.experimental.pallas import tpu as pltpu
from jax.sharding import PartitionSpec as P

HEAD_DIM = 64
SCALE = HEAD_DIM ** (-0.5)
EPSILON = 1e-05
NEGATIVE = -1e30
F32 = jnp.float32
BF16 = jnp.bfloat16
BIAS_ROWS = 16
PAD = 16
CUBE = 0.044715
ROOT = 0.7978845608028654
COST, QUICK, LONG = 8_000_000_000, 1_000, 20_000_000_000
VMEM = pl.BlockSpec(memory_space=pltpu.VMEM)
SMEM = pl.BlockSpec(memory_space=pltpu.SMEM)


def dot_nn(left, right):
    return lax.dot_general(left, right, (((1,), (0,)), ((), ())), preferred_element_type=F32)


def dot_nt(left, right):
    return lax.dot_general(left, right, (((1,), (1,)), ((), ())), preferred_element_type=F32)


def dot_tn(left, right):
    return lax.dot_general(left, right, (((0,), (0,)), ((), ())), preferred_element_type=F32)


def total(values):
    return functools.reduce(jnp.add, values)


def norm_parts(values):
    centre = values - jnp.mean(values, axis=-1, keepdims=True)
    spread = jnp.mean(centre * centre, axis=-1, keepdims=True)
    inverse = lax.rsqrt(spread + EPSILON)
    return centre * inverse, inverse


def norm_back(grad, hat, inverse, gain):
    scaled = grad * gain
    mean_one = jnp.mean(scaled, axis=-1, keepdims=True)
    mean_two = jnp.mean(scaled * hat, axis=-1, keepdims=True)
    return inverse * (scaled - mean_one - hat * mean_two)


def column_sum(values):
    return jnp.sum(values, axis=0, keepdims=True)


def window(index, size):
    return pl.ds(pl.multiple_of(index * size, size), size)


def halves(spot_ref, size):
    return window(spot_ref[0], size), window(1 - spot_ref[0], size)


def hold(*values):
    return lax.optimization_barrier(values)


class Order:
    def __init__(self, spot, parts):
        self.spot, self.parts, self.cost = spot, parts, COST

    def call(self, kernel, outs, operands, *, far=(), kept=(), alias=None, scratch=(), limit=5, cost=None):
        specs = [
            SMEM if operand.ndim == 1
            else pl.BlockSpec(memory_space=pltpu.HBM if i in far else pltpu.VMEM)
            for i, operand in enumerate(operands)
        ]
        operands = [
            pltpu.with_memory_space_constraint(operand, pltpu.HBM) if i in far else operand
            for i, operand in enumerate(operands)
        ]
        count = len(operands)

        def body(*refs):
            kernel(refs[count], *refs[:count], *refs[count + 1 :])

        results = pl.pallas_call(
            body,
            out_shape=tuple(jax.ShapeDtypeStruct(shape, dtype) for shape, dtype in outs),
            in_specs=specs + [SMEM],
            out_specs=tuple(
                pl.BlockSpec(memory_space=pltpu.HBM) if i in kept else VMEM
                for i in range(len(outs))
            ),
            input_output_aliases=alias or {},
            scratch_shapes=list(scratch),
            compiler_params=pltpu.CompilerParams(vmem_limit_bytes=limit << 20),
            cost_estimate=pl.CostEstimate(
                flops=cost or self.cost, bytes_accessed=1 << 16, transcendentals=0
            ),
        )(*operands, self.spot)
        first, self.spot = hold(results[0], self.spot)
        return [first, *results[1:]]

    def swap(self, values, axis, bits):
        values, self.spot = hold(values, self.spot)
        size = 2 if axis == "fsdp" else 4
        with jax.named_scope("swap_%s_%d" % (axis, bits)):
            return lax.ppermute(values, axis, [(i, i ^ bits) for i in range(size)])

    def swap_three(self, values, axis):
        return [self.swap(values, axis, bits) for bits in (1, 2, 3)]

    def swap_turn(self, values, turn):
        if self.parts != 2:
            return self.swap(values, "ctx", 1 + turn)
        values, self.spot = hold(values, self.spot)
        pairs = [
            (4 * core + i, 4 * core + (i ^ (1 + (core + turn) % 2)))
            for core in range(2)
            for i in range(4)
        ]
        with jax.named_scope("swap_turn_%d" % turn):
            return lax.ppermute(values, ("fsdp", "ctx"), pairs)


def clear_below(ref, rows):
    if ref.shape[0] > rows:
        ref[rows:, :] = jnp.zeros((ref.shape[0] - rows, ref.shape[1]), ref.dtype)


def fetch(copies, sems):
    started = [
        pltpu.make_async_copy(source, target, sems.at[i])
        for i, (source, target) in enumerate(copies)
    ]
    for copy in started:
        copy.start()
    for copy in started:
        copy.wait()


def split_three(values):
    high = values.astype(BF16)
    rest = values - high.astype(F32)
    middle = rest.astype(BF16)
    return [high, middle, (rest - middle.astype(F32)).astype(BF16)]


def pack_kernel(
    spot_ref, steps_ref, w_hbm, out_hbm, qv_hbm, up_bias_hbm, pack_ref, qkv_ref, out_ref,
    w_ref, o_ref, qv_ref, up_bias_ref, sems,
):
    rows, cols = w_ref.shape[1:]
    fetch(
        [(w_hbm, w_ref), (out_hbm, o_ref), (qv_hbm, qv_ref), (up_bias_hbm, up_bias_ref)], sems
    )
    for i in range(3):
        pack_ref[:rows, i * cols : (i + 1) * cols] = w_ref[i].astype(BF16)
    pack_ref[:rows, 3 * cols :] = o_ref[...].astype(BF16)
    lanes = lax.broadcasted_iota(jnp.int32, (1, cols), 1)
    steps = jnp.zeros((1, cols), F32)
    for i in range(steps_ref.shape[0]):
        steps = jnp.where(lanes == i, steps_ref[i].astype(F32), steps)
    fill = jnp.zeros((1, cols), F32)
    up_bias = up_bias_ref[...]
    lines = [
        jnp.concatenate([qv_ref[0:1], qv_ref[1:2], steps, fill], axis=1),
        jnp.concatenate([up_bias[:, : 2 * cols], fill, fill], axis=1),
        jnp.concatenate([up_bias[:, 2 * cols :], fill, fill], axis=1),
    ]
    parts = split_three(jnp.concatenate(lines, axis=0))
    fill = jnp.zeros((BIAS_ROWS - 9, 4 * cols), F32)
    stack = jnp.concatenate([v.astype(F32) for v in parts] + [fill], axis=0)
    pack_ref[rows:, :] = stack.astype(BF16)
    qkv_ref[...] = pack_ref[:, : 3 * cols]
    out_ref[...] = pack_ref[:rows, 3 * cols :]


def pack_rest_kernel(
    spot_ref, own_out, up_hbm, down_hbm, cotan_hbm, rest_ref, side_ref, cotan_ref,
    up_ref, down_ref, sems,
):
    rows, hidden = up_ref.shape
    cols = own_out.shape[1]
    pair = spot_ref[2] // 2
    fetch([(up_hbm, up_ref), (down_hbm, down_ref), (cotan_hbm.at[pair], cotan_ref)], sems)
    rest_ref[:, :hidden] = up_ref[...].astype(BF16)
    rest_ref[:, hidden:] = down_ref[...].astype(BF16)
    if side_ref.shape[0] == rows:
        side_ref[...] = own_out[...]
        return
    quarter, fold = rows // 4, rows // 8
    mine = window(spot_ref[1], quarter)
    side_ref[:quarter, :hidden] = up_ref[mine, :].astype(BF16)
    side_ref[:quarter, hidden:] = down_ref[mine, :].astype(BF16)
    for i in range(8):
        block = own_out[i * fold : (i + 1) * fold, :]
        side_ref[quarter : quarter + fold, i * cols : (i + 1) * cols] = block
    clear_below(side_ref, quarter + fold)


def unpack_kernel(spot_ref, side_ref, quarter_ref, out_ref):
    rows, cols = out_ref.shape
    quarter, fold = rows // 4, rows // 8
    quarter_ref[...] = side_ref[:quarter, :]
    for i in range(8):
        block = side_ref[quarter : quarter + fold, i * cols : (i + 1) * cols]
        out_ref[i * fold : (i + 1) * fold, :] = block


def bias_lines(pack_ref, row):
    bits = pack_ref[row : row + BIAS_ROWS, :].astype(F32)
    lines = bits[0:3] + bits[3:6] + bits[6:9]
    half = 4 * HEAD_DIM
    return lines[0:1], jnp.concatenate([lines[1:2, :half], lines[2:3, :half]], axis=1)


def out_part(ref, size):
    cols = 2 * HEAD_DIM
    return ref[:size, ref.shape[1] - cols :]


def add_pair_kernel(spot_ref, base_ref, own_ref, got_ref, out_ref):
    span = base_ref.shape[0]
    terms = own_ref[:span, :].astype(F32) + got_ref[:span, :].astype(F32)
    out_ref[...] = (base_ref[...] + terms).astype(BF16)


def open_kernel(
    spot_ref, steps_ref, x_hbm, table_hbm, seg_hbm, g1, b1, g2, b2, bo, bd, one_ref, two_ref,
    bias_ref, q_ref, kv_ref, stream_ref, normed_ref, seg_ref, lines_ref,
    x_ref, table_ref, ids_ref, line_ref, sems, *, row,
):
    pair = spot_ref[2] // 2
    step = steps_ref[pair]
    block = pl.multiple_of(step // 8 * 8, 8)
    copies = [
        (x_hbm.at[pair], x_ref),
        (table_hbm.at[pl.ds(block, 8), :], table_ref),
        (seg_hbm, ids_ref),
    ]
    vectors = (g1, b1, g2, b2, bo, bd)
    fetch(copies + [(v, line_ref.at[i]) for i, v in enumerate(vectors)], sems)
    for i in range(len(vectors)):
        lines_ref[i : i + 1, :] = line_ref[i]
    seg_ref[...] = ids_ref[pl.ds(pair, 1), :]
    stream = x_ref[...] + table_ref[pl.ds(step % 8, 1), :]
    hat, _ = norm_parts(stream)
    stream_ref[...] = stream
    normed_ref[...] = (hat * line_ref[0] + line_ref[1]).astype(BF16)
    project_kernel(spot_ref, normed_ref, one_ref, two_ref, bias_ref, q_ref, kv_ref, row=row)


def project_kernel(spot_ref, normed_ref, one_ref, two_ref, bias_ref, q_ref, kv_ref, *, row):
    span, cols = q_ref.shape
    size = normed_ref.shape[1] // 2
    one, two = halves(spot_ref, size)
    raw = dot_nn(normed_ref[:, one], one_ref[:size, : 3 * cols])
    raw = raw + dot_nn(normed_ref[:, two], two_ref[:size, : 3 * cols])
    line, _ = bias_lines(bias_ref, row)
    q_bias, v_bias = line[:, :cols], line[:, cols : 2 * cols]
    q_ref[...] = (raw[:, :cols] + q_bias).astype(BF16)
    kv_ref[:span, :cols] = raw[:, cols : 2 * cols].astype(BF16)
    kv_ref[:span, cols:] = (raw[:, 2 * cols :] + v_bias).astype(BF16)
    clear_below(kv_ref, span)


def mask_biases(spot_ref, seg_ref, span):
    chunk = spot_ref[1]
    ids = [seg_ref[:, window(chunk ^ step, span)] for step in range(seg_ref.shape[1] // span)]
    own = jnp.broadcast_to(ids[0], (span, span)).T
    return [
        jnp.where(own == jnp.broadcast_to(step_ids, (span, span)), 0.0, NEGATIVE)
        for step_ids in ids
    ]


def lane_mask(shape, head):
    return (lax.broadcasted_iota(jnp.int32, shape, 1) // HEAD_DIM) == head


def attend_forward(spot_ref, seg_ref, q_ref, kvs, mixed_ref, lse_ref):
    span, width = q_ref.shape
    biases = mask_biases(spot_ref, seg_ref, span)
    query = q_ref[...]
    mixed, lse = None, None
    for head in range(width // HEAD_DIM):
        mine = lane_mask((span, width), head)
        masked = jnp.where(mine, query * SCALE, jnp.zeros_like(query))
        scores = [
            dot_nt(masked, kv[:span, :width]) + bias for kv, bias in zip(kvs, biases)
        ]
        top = functools.reduce(
            jnp.maximum, [jnp.max(block, axis=-1, keepdims=True) for block in scores]
        )
        grown = [jnp.exp(block - top) for block in scores]
        mass = total([jnp.sum(block, axis=-1, keepdims=True) for block in grown])
        share = 1.0 / mass
        out = total(
            [
                dot_nn((block * share).astype(BF16), kv[:span, width:])
                for block, kv in zip(grown, kvs)
            ]
        )
        log_mass = jnp.broadcast_to(top + jnp.log(mass), (span, width))
        mixed = out if head == 0 else jnp.where(mine, out, mixed)
        lse = log_mass if head == 0 else jnp.where(mine, log_mass, lse)
    mixed_ref[...] = mixed.astype(BF16)
    lse_ref[...] = lse


def attend_one_kernel(spot_ref, seg_ref, q_ref, kv0, kv1, kv2, kv3, mixed_ref, lse_ref):
    attend_forward(spot_ref, seg_ref, q_ref, (kv0, kv1, kv2, kv3), mixed_ref, lse_ref)


def attend_two_kernel(
    spot_ref, seg_ref, q_ref, kv0, kv1, kv2, kv3, near_ref, one_n, two_n, one_f, two_f,
    mixed_ref, lse_ref, given_ref,
):
    attend_forward(spot_ref, seg_ref, q_ref, (kv0, kv1, kv2, kv3), mixed_ref, lse_ref)
    size = given_ref.shape[1] // 2
    one, two = halves(spot_ref, size)
    near, far = near_ref[...], mixed_ref[...]
    for columns, near_w, far_w in ((one, one_n, one_f), (two, two_n, two_f)):
        terms = dot_nt(near, out_part(near_w, size)) + dot_nt(far, out_part(far_w, size))
        given_ref[: near.shape[0], columns] = terms.astype(BF16)
    clear_below(given_ref, near.shape[0])


def stack_kernel(spot_ref, one_ref, two_ref, out_ref):
    rows = out_ref.shape[0] // 2
    out_ref[:rows, :] = one_ref[:rows, :]
    out_ref[rows:, :] = two_ref[:rows, :]


def gelu_parts(x):
    square = x * x
    curve = jnp.tanh(ROOT * (x + CUBE * (x * square)))
    half = 0.5 * (1.0 + curve)
    slope = half + 0.5 * x * (1.0 - curve * curve) * (ROOT * (1.0 + 3.0 * CUBE * square))
    return x * half, slope


def ffn_side(
    normed_ref, low_ref, bias, first, second, columns, act_ref, pre_ref, sum_ref, *sums
):
    hidden = act_ref.shape[1]
    one, two = columns
    pre = dot_nn(normed_ref[:, one], first[:, :hidden])
    pre = pre + dot_nn(normed_ref[:, two], second[:, :hidden]) + bias
    value, slope = gelu_parts(pre)
    grad = dot_nn(low_ref[:, one], first[:, hidden:])
    grad = (grad + dot_nn(low_ref[:, two], second[:, hidden:])) * slope
    sum_ref[...] = column_sum(grad)
    act_ref[...] = value.astype(BF16)
    pre_ref[...] = grad.astype(BF16)
    act, pre_low = act_ref[...], pre_ref[...]
    for at, weights in zip(columns, (first, second)):
        back = dot_nt(pre_low, weights[:, :hidden])
        down = dot_nt(act, weights[:, hidden:])
        if len(sums) == 2:
            back_ref, out_ref = sums
        else:
            back_near, out_near, back_ref, out_ref = sums
            back, down = back + back_near[:, at], down + out_near[:, at]
        back_ref[: act.shape[0], at] = back.astype(back_ref.dtype)
        out_ref[: act.shape[0], at] = down.astype(out_ref.dtype)
    clear_below(sums[-2], act.shape[0])
    clear_below(sums[-1], act.shape[0])


def ffn_near_kernel(
    spot_ref, stream_ref, mine_ref, got_ref, cotan_ref, lines_ref, pack_ref, first, second,
    back_ref, ffn_ref, out_ref, resid_ref, normed_ref, act_ref, pre_ref, low_ref, sum_ref, *, row,
):
    span = stream_ref.shape[0]
    terms = mine_ref[:span, :].astype(F32) + got_ref[:span, :].astype(F32)
    resid = stream_ref[...] + terms + lines_ref[4:5, :]
    resid_ref[...] = resid
    out_ref[...] = resid + lines_ref[5:6, :]
    hat, _ = norm_parts(resid)
    normed_ref[...] = (hat * lines_ref[2:3, :] + lines_ref[3:4, :]).astype(BF16)
    low_ref[...] = cotan_ref[...].astype(BF16)
    ffn_side(
        normed_ref, low_ref, bias_lines(pack_ref, row)[1], first, second,
        halves(spot_ref, first.shape[0]), act_ref, pre_ref, sum_ref, back_ref, ffn_ref,
    )


def ffn_far_kernel(spot_ref, normed_ref, low_ref, back_near, ffn_near, pack_ref, *refs, row):
    count = len(refs) - 7
    pieces, outs, (first, second) = refs[:count], refs[count:-2], refs[-2:]
    if count == 2:
        first, second = pieces
    else:
        rows = pieces[0].shape[0] // 2
        turn, other = turn_bits(spot_ref)
        for target, pairs, bits in (
            (first, pieces[:2], (0, turn, other, 3)),
            (second, pieces[2:], (0, other, turn, 3)),
        ):
            for i in range(4):
                block = pairs[i // 2][i % 2 * rows : (i % 2 + 1) * rows, :]
                target[window(spot_ref[1] ^ bits[i], rows), :] = block
    act_ref, pre_ref, sum_ref, back_ref, ffn_ref = outs
    ffn_side(
        normed_ref, low_ref, bias_lines(pack_ref, row)[1], first, second,
        halves(spot_ref, first.shape[0]), act_ref, pre_ref, sum_ref, back_near, ffn_near,
        back_ref, ffn_ref,
    )


def ffn_kernel(
    spot_ref, stream_ref, mine_ref, got_ref, cotan_ref, lines_ref, pack_ref, far_pack, first, second,
    *refs, row,
):
    pieces, outs, scratch = refs[:-16], refs[-16:-4], refs[-4:]
    back_ref, down_ref, out_ref, resid_ref, normed_ref, low_ref = outs[:6]
    act_n, pre_n, sum_n, act_f, pre_f, sum_f = outs[6:]
    back_near, down_near, one, two = scratch
    ffn_near_kernel(
        spot_ref, stream_ref, mine_ref, got_ref, cotan_ref, lines_ref, pack_ref, first, second,
        back_near, down_near, out_ref, resid_ref, normed_ref, act_n, pre_n, low_ref, sum_n, row=row,
    )
    ffn_far_kernel(
        spot_ref, normed_ref, low_ref, back_near, down_near, far_pack, *pieces,
        act_f, pre_f, sum_f, back_ref, down_ref, one, two, row=row,
    )


def ffn_grads_kernel(
    spot_ref, normed_ref, low_ref, act_n, pre_n, act_f, pre_f, kept_ref, *given
):
    hidden = act_n.shape[1]
    one, two = halves(spot_ref, normed_ref.shape[1] // 2)
    for columns in (two, one):
        normed, low = normed_ref[:, columns], low_ref[:, columns]
        for i, (left, right) in enumerate(((normed, pre_n), (low, act_n), (normed, pre_f), (low, act_f))):
            grads = dot_tn(left, right[...])
            if columns is one:
                kept_ref[:, i * hidden : (i + 1) * hidden] = grads
            else:
                given[i][...] = grads.astype(BF16)


def resid_part(
    spot_ref, mine_ref, got_ref, resid_ref, cotan_ref, lines_ref, grad_ref, low_ref, rows_ref,
    work_ref,
):
    half = resid_ref.shape[0] // 2
    mine = window(spot_ref[2] % 2, half)
    span = resid_ref.shape[0]
    grad = mine_ref[:span, :].astype(F32) + got_ref[:span, :].astype(F32)
    hat, inverse = norm_parts(resid_ref[...])
    resid_grad = cotan_ref[...] + norm_back(grad, hat, inverse, lines_ref[2:3, :])
    grad_ref[...] = resid_grad
    low_ref[...] = resid_grad.astype(BF16)
    work_ref[0] = grad * hat
    work_ref[1] = grad
    sums = [work_ref[0, mine, :], work_ref[1, mine, :], grad_ref[mine, :], cotan_ref[mine, :]]
    rows_ref[...] = jnp.concatenate([column_sum(v) for v in sums], axis=0)


def attend_backward(biases, q_ref, grad, lse_ref, kvs, dq_ref, outs, side):
    span, width = q_ref.shape
    query = q_ref[...]
    dq, dks, dvs = None, [None] * 4, [None] * 4
    for head in range(width // HEAD_DIM):
        mine = lane_mask((span, width), head)
        masked_q = jnp.where(mine, query * SCALE, jnp.zeros_like(query))
        masked_g = jnp.where(mine, grad, jnp.zeros_like(grad))
        lse = lse_ref[:, head * HEAD_DIM : head * HEAD_DIM + 1]
        probs = [
            jnp.exp(dot_nt(masked_q, kv[:span, :width]) + bias - lse)
            for kv, bias in zip(kvs, biases)
        ]
        grads = [dot_nt(masked_g, kv[:span, width:]) for kv in kvs]
        inner = total([jnp.sum(p * g, axis=-1, keepdims=True) for p, g in zip(probs, grads)])
        raws = [(p * (g - inner)).astype(BF16) for p, g in zip(probs, grads)]
        head_dq = total([dot_nn(raw, kv[:span, :width]) for raw, kv in zip(raws, kvs)])
        dq = head_dq if head == 0 else jnp.where(mine, head_dq, dq)
        for step in range(4):
            head_dk = dot_tn(raws[step], query)
            head_dv = dot_tn(probs[step].astype(BF16), grad)
            dks[step] = head_dk if head == 0 else jnp.where(mine, head_dk, dks[step])
            dvs[step] = head_dv if head == 0 else jnp.where(mine, head_dv, dvs[step])
    dq_ref[:, side * width : (side + 1) * width] = dq * SCALE
    at = 2 * side * width
    for step in range(4):
        outs[step][:span, at : at + width] = (dks[step] * SCALE).astype(outs[step].dtype)
        outs[step][:span, at + width : at + 2 * width] = dvs[step].astype(outs[step].dtype)


def pull_kernel(
    spot_ref, seg_ref, q_n, lse_n, n0, n1, n2, n3, q_f, lse_f, f0, f1, f2, f3,
    mine_ref, got_ref, resid_ref, cotan_ref, lines_ref, one_n, two_n, one_f, two_f,
    dq_ref, own_ref, out1, out2, out3, grad_ref, low_ref, rows_ref, work_ref,
):
    size = low_ref.shape[1] // 2
    resid_part(
        spot_ref, mine_ref, got_ref, resid_ref, cotan_ref, lines_ref, grad_ref, low_ref, rows_ref,
        work_ref,
    )
    one, two = halves(spot_ref, size)
    outs = (own_ref, out1, out2, out3)
    biases = mask_biases(spot_ref, seg_ref, q_n.shape[0])
    near = (q_n, lse_n, (n0, n1, n2, n3), one_n, two_n)
    far = (q_f, lse_f, (f0, f1, f2, f3), one_f, two_f)
    for side, (q_ref, lse_ref, kvs, first, second) in enumerate((near, far)):
        grad = dot_nn(low_ref[:, one], out_part(first, size))
        grad = grad + dot_nn(low_ref[:, two], out_part(second, size))
        attend_backward(
            biases, q_ref, grad.astype(BF16), lse_ref, kvs, dq_ref, outs, side
        )
    for out_ref in (out1, out2, out3):
        clear_below(out_ref, q_n.shape[0])


def input_kernel(
    spot_ref, stream_ref, lines_ref, rows_ref, up_near, up_far, dq_ref, own_ref, g1, g2, g3,
    one_n, two_n, one_f, two_f, normed_ref, low_ref, near_ref, far_ref,
    given_ref, small_ref, w_kept_ref, w_near_ref, w_far_ref, w_out_ref, pulled_ref, terms_ref,
):
    span, width = stream_ref.shape
    cols = dq_ref.shape[1] // 2
    size = width // 2
    shard, slot = spot_ref[2], spot_ref[3]
    far = shard ^ 2
    one, two = halves(spot_ref, size)
    small_ref[...] = jnp.zeros_like(small_ref)
    parts = [ref[:span, :].astype(F32) for ref in (g1, g2, g3)]
    got = (own_ref[...] + parts[0]) + (parts[1] + parts[2])
    for side, (place, up_sum) in enumerate(((shard, up_near), (far, up_far))):
        dq = dq_ref[:, side * cols : (side + 1) * cols]
        dkv = got[:, 2 * side * cols : 2 * (side + 1) * cols]
        at = side * 3 * cols
        pulled_ref[:, at : at + cols] = dq.astype(BF16)
        pulled_ref[:, at + cols : at + 3 * cols] = dkv.astype(BF16)
        small_ref[6:7, window(place, cols)] = column_sum(dq)
        small_ref[7:8, window(place, cols)] = column_sum(dkv[:, cols:])
        small_ref[pl.ds(8 + place, 1), :] = up_sum[...]
    for columns, near_w, far_w in ((one, one_n, one_f), (two, two_n, two_f)):
        back = dot_nt(pulled_ref[:, : 3 * cols], near_w[:size, : 3 * cols])
        back = back + dot_nt(pulled_ref[:, 3 * cols :], far_w[:size, : 3 * cols])
        terms_ref[:, columns] = back
    back = terms_ref[...]
    hat, inverse = norm_parts(stream_ref[...])
    small_ref[0:1, :] = column_sum(back * hat)
    small_ref[1:2, :] = column_sum(back)
    small_ref[2:6, :] = rows_ref[...]
    grad = norm_back(back, hat, inverse, lines_ref[0:1, :])
    small_ref[pl.ds(12 + slot, 1), :] = column_sum(grad) + rows_ref[2:3, :]
    given_ref[...] = grad.astype(BF16)
    given = (w_near_ref, w_far_ref)
    for columns in (two, one):
        normed, low = normed_ref[:, columns], low_ref[:, columns]
        for side, mixed in enumerate((near_ref, far_ref)):
            at, start = side * 3 * cols, side * 4 * cols
            qkv = dot_tn(normed, pulled_ref[:, at : at + 3 * cols])
            out = dot_tn(low, mixed[...])
            if columns is one:
                w_kept_ref[:, start : start + 3 * cols] = qkv
                w_kept_ref[:, start + 3 * cols : start + 4 * cols] = out
            else:
                given[side][:size, :] = qkv.astype(BF16)
                w_out_ref[:size, side * cols : (side + 1) * cols] = out.astype(BF16)
    both_parts = jnp.concatenate(split_two(small_ref[...]), axis=1)
    w_near_ref[size:, :] = both_parts[:, : 3 * cols]
    w_far_ref[size:, :] = both_parts[:, 3 * cols : 6 * cols]
    w_out_ref[size:, :] = both_parts[:, 6 * cols :]


def turn_bits(spot_ref):
    return 1 + spot_ref[0], 2 - spot_ref[0]


def split_two(values):
    high = values.astype(BF16)
    return high, (values - high.astype(F32)).astype(BF16)


def both(high, low):
    return high.astype(F32) + low.astype(F32)


def cut_kernel(spot_ref, kept_ref, *refs):
    got, (own_ref, send_ref) = refs[:4], refs[4:]
    rows, width = own_ref.shape[0] // 2, got[0].shape[1]
    chunk = spot_ref[1]
    first, second = turn_bits(spot_ref)
    for spot, place in enumerate((chunk, chunk ^ second)):
        to = slice(spot * rows, (spot + 1) * rows)
        for i, piece in enumerate(got):
            columns = slice(i * width, (i + 1) * width)
            at = window(place, rows)
            own_ref[to, columns] = kept_ref[at, columns] + piece[at, :].astype(F32)
            at = window(place ^ first, rows)
            values = kept_ref[at, columns] + piece[at, :].astype(F32)
            send_ref[to, columns] = values.astype(BF16)


def middle_kernel(
    spot_ref, kept_ref, got_ref, base_ref, own_terms, got_terms, near_ref, send_ref, out_ref
):
    rows, width = near_ref.shape
    span = base_ref.shape[0]
    values = kept_ref[...] + got_ref[...].astype(F32)
    near_ref[...] = values[:, :width]
    terms = own_terms[:span, :].astype(F32) + got_terms[:span, :].astype(F32)
    out_ref[...] = (base_ref[...] + terms).astype(BF16)
    send_ref[: span // 2, :] = out_ref[window(spot_ref[2] % 2, span // 2), :]
    half = send_ref.shape[1]
    for i in range(width // half):
        at = span // 2 + i * rows
        columns = slice(width + i * half, width + (i + 1) * half)
        send_ref[at : at + rows, :] = values[:, columns].astype(BF16)
    clear_below(send_ref, span // 2 + width // half * rows)


def settle_kernel(spot_ref, near_ref, got_ref, out_ref, own_ref, *sends):
    rows, width = own_ref.shape
    span = out_ref.shape[0]
    out_ref[...] = got_ref[:span, :]
    half = got_ref.shape[1]
    for i in range(width // half):
        at, columns = span + 2 * i * rows, slice(i * half, (i + 1) * half)
        own_ref[:, columns] = near_ref[:rows, columns] + got_ref[at : at + rows, :].astype(F32)
        more = near_ref[rows:, columns] + got_ref[at + rows : at + 2 * rows, :].astype(F32)
        sends[i][...] = more.astype(BF16)


def fill_rows(spot_ref, own_ref, others, out_ref):
    pair, bit, span = spot_ref[2] // 2, spot_ref[2] % 2, own_ref.shape[0]
    out_ref[window(pair, span), :] = own_ref[...].astype(F32)
    if len(others) == 1:
        out_ref[window(1 - pair, span), :] = others[0][...].astype(F32)
    else:
        for i, other in enumerate(others):
            at = 2 * (1 - pair) + (bit ^ i)
            out_ref[window(at, span // 2), :] = other[: span // 2, :].astype(F32)


def rows_kernel(spot_ref, out_own, out_one, out_two, in_own, in_far, out_ref, in_ref):
    fill_rows(spot_ref, out_own, (out_one, out_two), out_ref)
    fill_rows(spot_ref, in_own, (in_far,), in_ref)


def cut_small_kernel(
    spot_ref, kept_ref, got_near, got_far, got_out, small_ref, own_ref, o1, o2, o3, sum_ref
):
    rows, width = own_ref.shape[0], small_ref.shape[1]
    whole = kept_ref.shape[0]
    for bits, out_ref in enumerate((own_ref, o1, o2, o3)):
        at = window(spot_ref[1] ^ bits, rows)
        for side, got_ref in enumerate((got_near, got_far)):
            cols = got_ref.shape[1] // 3
            got = (got_ref[at, :], got_out[at, side * cols : (side + 1) * cols])
            for part, start, stop in ((got[0], 0, 3 * cols), (got[1], 3 * cols, 4 * cols)):
                columns = slice(side * width + start, side * width + stop)
                values = kept_ref[at, columns] + part.astype(F32)
                out_ref[:rows, columns] = values.astype(out_ref.dtype)
    mine = both(*split_two(small_ref[...]))
    got = [piece[whole:, :].astype(F32) for piece in (got_near, got_far, got_out)]
    got = jnp.concatenate(got, axis=1)
    high, low = split_two(mine + (got[:, :width] + got[:, width:]))
    for out_ref in (o1, o2, o3):
        out_ref[rows:, :width] = high
        out_ref[rows:, width:] = low
    sum_ref[...] = both(high, low)


def shards_small_kernel(spot_ref, own_ref, g1, g2, g3, small_ref, kept_ref, send_ref):
    rows, width = kept_ref.shape
    got = [piece[:rows, :].astype(F32) for piece in (g1, g2, g3)]
    values = (own_ref[...] + got[0]) + (got[1] + got[2])
    kept_ref[...] = values[:, :width]
    send_ref[:rows, :] = values[:, width:].astype(BF16)
    count = small_ref.shape[0]
    got = [both(piece[rows:, :width], piece[rows:, width:]) for piece in (g1, g2, g3)]
    high, low = split_two((small_ref[...] + got[0]) + (got[1] + got[2]))
    send_ref[rows : rows + count, :] = high
    send_ref[rows + count :, :] = low


def owned_kernel(
    spot_ref, ffn_kept, ffn_one, ffn_two, kept_ref, sent_ref, got_ref, half_ref,
    out_ref, pass_ref,
):
    rows, width = kept_ref.shape
    half = half_ref.shape[0]
    pass_ref[:half, :] = half_ref[...]
    for i, piece in enumerate((ffn_one, ffn_two)):
        at = slice(i * width, (i + 1) * width)
        out_ref[:, at] = (ffn_kept[:, at] + piece[...].astype(F32)).astype(BF16)
    out_ref[:, 2 * width :] = (kept_ref[...] + got_ref[:rows, :].astype(F32)).astype(BF16)
    count = (sent_ref.shape[0] - rows) // 2
    top, end = slice(rows, rows + count), slice(rows + count, rows + 2 * count)
    mine = both(sent_ref[top, :], sent_ref[end, :])
    high, low = split_two(mine + both(got_ref[top, :], got_ref[end, :]))
    pass_ref[half : half + count, :] = high
    pass_ref[half + count :, :] = low


def sums_out(spot_ref, rows_ref, up_ref, qv_ref, lines):
    up_ref[...] = rows_ref[pl.ds(8 + spot_ref[2], 1), :]
    qv_ref[...] = rows_ref[6:8, window(spot_ref[2], qv_ref.shape[1])]
    for i, line_ref in enumerate(lines):
        line_ref[...] = rows_ref[i : i + 1, :]


def plain_sums_kernel(spot_ref, steps_ref, small_ref, table_ref, up_ref, qv_ref, *lines):
    table_ref[...] = jnp.zeros_like(table_ref)
    for place in range(steps_ref.shape[0]):
        at = pl.ds(steps_ref[place], 1)
        table_ref[at, :] = table_ref[at, :] + small_ref[12 + place : 13 + place, :]
    sums_out(spot_ref, small_ref, up_ref, qv_ref, lines)


def zero_kernel(spot_ref, table_hbm, block_ref, sems):
    block_ref[...] = jnp.zeros_like(block_ref)
    rows = block_ref.shape[0]
    fetch(
        [
            (block_ref, table_hbm.at[i * rows : (i + 1) * rows, :])
            for i in range(table_hbm.shape[0] // rows)
        ],
        sems,
    )


class Sends:
    def __init__(self, sems):
        self.sems, self.copies = sems, []

    def start(self, source, target, alone=None):
        copy = pltpu.make_async_copy(source, target, self.sems.at[len(self.copies)])
        self.copies.append((copy, alone))
        copy.start() if alone is None else pl.when(alone)(copy.start)

    def wait(self):
        for copy, alone in self.copies:
            copy.wait() if alone is None else pl.when(alone)(copy.wait)


def weights_kernel(
    spot_ref, p0, p1, p2, p3, up_hbm, down_hbm, qkv_hbm, proj_hbm,
    up_all, down_all, qkv_all, proj_all, sems,
):
    sends = Sends(sems)
    rows, hidden, cols = p0.shape[0], up_all.shape[1], proj_all.shape[1]
    pieces = (p0, p1, p2, p3)
    spots = [window(spot_ref[1] ^ bits, rows) for bits in range(4)]
    for i, (whole, target) in enumerate(((up_all, up_hbm), (down_all, down_hbm))):
        for spot, piece in zip(spots, pieces):
            whole[spot, :] = piece[:, i * hidden : (i + 1) * hidden].astype(F32)
        sends.start(whole, target)
    start = 2 * hidden
    for spot, piece in zip(spots, pieces):
        for i in range(3):
            qkv_all[i, spot, :] = piece[:, start + i * cols : start + (i + 1) * cols].astype(F32)
        proj_all[spot, :] = piece[:, start + 3 * cols :].astype(F32)
    sends.start(qkv_all, qkv_hbm)
    sends.start(proj_all, proj_hbm)
    sends.wait()


def close_kernel(
    spot_ref, steps_ref, out_own, out_one, out_two, in_own, in_far, zero_hbm,
    out_hbm, in_hbm, table_hbm, up_ref, qv_ref, *refs,
):
    lines, (out_all, in_all, rows_ref, blocks_ref, sems) = refs[:6], refs[6:]
    sends = Sends(sems)
    fill_rows(spot_ref, out_own, (out_one, out_two), out_all)
    sends.start(out_all, out_hbm)
    fill_rows(spot_ref, in_own, (in_far,), in_all)
    sends.start(in_all, in_hbm)
    start, count = out_one.shape[0] - 2 * rows_ref.shape[0], rows_ref.shape[0]
    parts = [
        both(ref[start : start + count, :], ref[start + count :, :]) for ref in (out_one, out_two)
    ]
    rows_ref[...] = parts[0] + parts[1]
    places = range(steps_ref.shape[0])
    at = lax.broadcasted_iota(jnp.int32, (8, 1), 0)
    for place in places:
        block = steps_ref[place] // 8
        total_rows = jnp.zeros(blocks_ref.shape[1:], F32)
        for other in places:
            step = steps_ref[other]
            row = jnp.where(step // 8 == block, step % 8, -1)
            total_rows = total_rows + jnp.where(at == row, rows_ref[12 + other : 13 + other, :], 0.0)
        blocks_ref[place] = total_rows
        seen = [steps_ref[other] // 8 == block for other in range(place)]
        alone = jnp.logical_not(functools.reduce(jnp.logical_or, seen)) if seen else None
        target = table_hbm.at[pl.ds(pl.multiple_of(block * 8, 8), 8), :]
        sends.start(blocks_ref.at[place], target, alone)
    sums_out(spot_ref, rows_ref, up_ref, qv_ref, lines)
    sends.wait()


class Reduction:
    def __init__(self, order, kept, small):
        self.order, self.kept, self.small = order, kept, small
        self.rows, self.width = kept.shape[0] // 4, kept.shape[1]

    def cut(self, got):
        rows, width, more = self.rows, self.width, self.small.shape[0]
        self.own, *cuts, self.small = self.order.call(
            cut_small_kernel,
            [((rows, width), F32)]
            + [((rows + more, width), BF16)] * 3
            + [(self.small.shape, F32)],
            [self.kept, *got, self.small],
        )
        self.got = [self.order.swap(cuts[bits - 1], "ctx", bits) for bits in (1, 2, 3)]

    def shards(self):
        rows, width, more = self.rows, self.width // 2, 2 * self.small.shape[0]
        self.own, self.sent = self.order.call(
            shards_small_kernel,
            [((rows, width), F32), ((rows + more, width), BF16)],
            [self.own, *self.got, self.small],
        )
        self.got = self.order.swap(self.sent, "tp", 2)


def reduce_plainly(kept, given, chunk):
    whole = jnp.concatenate([kept, given.astype(F32)])
    mine = lax.psum_scatter(whole, "fsdp", scatter_dimension=0, tiled=True)
    quarter = lax.psum_scatter(mine, "ctx", scatter_dimension=0, tiled=True)
    width = quarter.shape[1] // 2
    far = lax.ppermute(quarter[:, width:], "tp", [(i, i ^ 2) for i in range(4)])
    return lax.all_gather(quarter[:, :width] + far, "ctx", axis=0, tiled=True)


def pieces_of(order, part, parts, rows):
    if parts == 2:
        return part, order.swap(part, "fsdp", 1)
    whole = lax.all_gather(part[:rows], "fsdp", axis=0, tiled=True)
    size = whole.shape[0] // 2
    return whole[:size], whole[size:]


def per_device(
    layer_input,
    timesteps,
    segment_ids,
    time_table,
    ln1_gain,
    ln1_bias,
    w_qkv,
    b_qv,
    w_out_t,
    b_out,
    ln2_gain,
    ln2_bias,
    w_up,
    b_up,
    w_down_t,
    b_down,
    out_grad,
    *,
    parts,
):
    span, width = layer_input.shape[1:]
    rows, cols = w_qkv.shape[1:]
    hidden = w_up.shape[1]
    size = width // 2
    core = lax.axis_index("fsdp")
    chunk = lax.axis_index("ctx")
    shard = lax.axis_index("tp")
    place = core if parts == 2 else 0 * core
    spot = jnp.stack([place, chunk, shard, 2 * core + shard // 2]).astype(jnp.int32)
    order = Order(spot, parts)
    line = lambda values: values.reshape(1, -1)
    dma = lambda count: pltpu.SemaphoreType.DMA((count,))

    pack, qkv_part, out_part_own = order.call(
        pack_kernel,
        [
            ((rows + BIAS_ROWS, 4 * cols), BF16), ((rows + BIAS_ROWS, 3 * cols), BF16),
            ((rows, cols), BF16),
        ],
        [timesteps, w_qkv, w_out_t, b_qv, line(b_up)],
        far=range(5),
        scratch=[
            pltpu.VMEM(w_qkv.shape, F32),
            pltpu.VMEM(w_out_t.shape, F32),
            pltpu.VMEM(b_qv.shape, F32),
            pltpu.VMEM((1, hidden), F32),
            dma(4),
        ],
    )
    near = pieces_of(order, pack, parts, rows)
    pack_far = order.swap(qkv_part, "tp", 2)
    projected = [((span, cols), BF16), ((span, 2 * cols), BF16)]
    more = [((span, cols), BF16), ((span, 2 * cols), BF16)]
    q_near, kv_near, stream, normed, seg, lines = order.call(
        functools.partial(open_kernel, row=rows),
        projected
        + [
            ((span, width), F32), ((span, width), BF16), ((1, segment_ids.shape[1]), jnp.int32),
            ((8, width), F32),
        ],
        [timesteps, layer_input, time_table, segment_ids]
        + [line(v) for v in (ln1_gain, ln1_bias, ln2_gain, ln2_bias, b_out, b_down)]
        + [*near, pack],
        far=range(10),
        scratch=[
            pltpu.VMEM((span, width), F32),
            pltpu.VMEM((8, width), F32),
            pltpu.VMEM(segment_ids.shape, jnp.int32),
            pltpu.VMEM((6, 1, width), F32),
            dma(9),
        ],
    )
    kvs_near = [kv_near] + order.swap_three(kv_near, "ctx")
    project = functools.partial(project_kernel, row=rows)

    side_shape = (rows // 4 + rows // 8, 2 * hidden) if parts == 2 else (rows, cols)
    rest, side, cotan = order.call(
        pack_rest_kernel,
        [((rows, 2 * hidden), BF16), (side_shape, BF16), ((span, width), F32)],
        [out_part_own, w_up, w_down_t, out_grad],
        far=(1, 2, 3),
        scratch=[pltpu.VMEM(w_up.shape, F32), pltpu.VMEM(w_down_t.shape, F32), dma(3)],
        cost=QUICK,
    )
    side_far = order.swap(side, "tp", 2)
    if parts == 2:
        table = order.call(
            zero_kernel,
            [(time_table.shape, F32)],
            [],
            kept=(0,),
            scratch=[pltpu.VMEM((time_table.shape[0] // 5, width), F32), dma(5)],
            cost=QUICK,
        )[0]
    rest_near = pieces_of(order, rest, parts, rows)

    attended = [((span, cols), BF16), ((span, cols), F32)]
    pack_far, *kvs_near[1:] = hold(pack_far, *kvs_near[1:])
    far = pieces_of(order, pack_far, parts, rows)
    mixed_near, lse_near = order.call(
        attend_one_kernel, attended, [seg, q_near, *kvs_near], cost=COST
    )
    q_far, kv_far = order.call(project, more, [normed, *far, pack_far], cost=QUICK)
    kvs_far = [kv_far] + order.swap_three(kv_far, "ctx")
    if parts == 2:
        rest_far, out_far = order.call(
            unpack_kernel,
            [((rows // 4, 2 * hidden), BF16), ((rows, cols), BF16)],
            [side_far],
            cost=QUICK,
        )
        rest_turn = order.swap_turn(rest_far, 0)
    else:
        rest_far, out_far = order.swap(rest, "tp", 2), side_far
    out_far = pieces_of(order, out_far, parts, rows)
    mixed_far, lse_far, given = order.call(
        attend_two_kernel,
        attended + [((span, width), BF16)],
        [seg, q_far, *kvs_far, mixed_near, *near, *out_far],
    )
    got = order.swap(given, "tp", 1)
    if parts == 2:
        rest_one = order.call(
            stack_kernel, [((rows // 2, 2 * hidden), BF16)], [rest_far, rest_turn], cost=QUICK
        )[0]
        rest_two = order.swap_turn(rest_one, 1)
        rest_far = [
            rest_one, rest_two, order.swap(rest_one, "fsdp", 1), order.swap(rest_two, "fsdp", 1)
        ]
    else:
        rest_far = pieces_of(order, rest_far, parts, rows)

    acts = [((span, hidden), BF16), ((span, hidden), BF16), ((1, hidden), F32)]
    (
        back, ffn_terms, out_base, resid, normed_two, low, act_n, pre_n, up_near, act_f, pre_f, up_far,
    ) = order.call(
        functools.partial(ffn_kernel, row=rows),
        [
            ((span + PAD, width), BF16), ((span, width), BF16), ((span, width), F32),
            ((span, width), F32), ((span, width), BF16), ((span, width), BF16), *acts, *acts,
        ],
        [stream, given, got, cotan, lines, pack, pack_far, *rest_near, *rest_far],
        scratch=[pltpu.VMEM((span, width), F32)] * 2
        + [pltpu.VMEM((size, 2 * hidden), BF16)] * 2,
        limit=8,
    )
    back_got = order.swap(back, "tp", 1)
    ffn_kept, *ffn_sent = order.call(
        ffn_grads_kernel,
        [((size, 4 * hidden), F32)] + [((size, hidden), BF16)] * 4,
        [normed_two, low, act_n, pre_n, act_f, pre_f],
    )
    if parts == 2:
        ffn_got = [order.swap(piece, "fsdp", 1) for piece in ffn_sent]
        ffn_own, ffn_cut = order.call(
            cut_kernel,
            [((rows // 2, 4 * hidden), F32), ((rows // 2, 4 * hidden), BF16)],
            [ffn_kept, *ffn_got],
            cost=QUICK,
        )
        ffn_turn = order.swap_turn(ffn_cut, 0)
    dq, own, *shares, resid_grad, low_all, resid_rows = order.call(
        pull_kernel,
        [((span, 2 * cols), F32), ((span, 4 * cols), F32)]
        + [((span + PAD, 4 * cols), BF16)] * 3
        + [((span, width), F32), ((span, width), BF16), ((4, width), F32)],
        [
            seg, q_near, lse_near, *kvs_near, q_far, lse_far, *kvs_far, back, back_got, resid,
            cotan, lines, *near, *out_far,
        ],
        scratch=[pltpu.VMEM((2, span, width), F32)],
        limit=6,
    )
    shared = [order.swap(shares[bits - 1], "ctx", bits) for bits in (1, 2, 3)]

    terms_got = order.swap(ffn_terms, "tp", 1)
    if parts == 2:
        ffn_near, sent, out_low = order.call(
            middle_kernel,
            [
                ((rows // 2, 2 * hidden), F32), ((span // 2 + rows + 0 * PAD, width), BF16),
                ((span, width), BF16),
            ],
            [ffn_own, ffn_turn, out_base, ffn_terms, terms_got],
            cost=QUICK,
        )
        sent_got = order.swap(sent, "tp", 2)
    else:
        out_low = order.call(
            add_pair_kernel, [((span, width), BF16)], [out_base, ffn_terms, terms_got]
        )[0]
        half_rows = lax.dynamic_slice_in_dim(out_low, shard % 2 * (span // 2), span // 2, 0)
        out_half = order.swap(half_rows, "tp", 2)

    seqs = 2 * parts
    small_rows = -(-(12 + seqs) // 16) * 16
    in_terms, small, attention_kept, *attention_sent = order.call(
        input_kernel,
        [
            ((span, width), BF16), ((small_rows, width), F32),
            ((size, 8 * cols), F32), ((size + small_rows, 3 * cols), BF16),
            ((size + small_rows, 3 * cols), BF16), ((size + small_rows, 2 * cols), BF16),
        ],
        [
            stream, lines, resid_rows, up_near, up_far, dq, own, *shared, *near, *far,
            normed, low_all, mixed_near, mixed_far,
        ],
        scratch=[pltpu.VMEM((span, 6 * cols), BF16), pltpu.VMEM((span, width), F32)],
    )
    order.cost = QUICK
    if parts == 2:
        attention_far = [order.swap(piece, "fsdp", 1) for piece in attention_sent]
    in_got = order.swap(in_terms, "tp", 1)
    if parts == 2:
        sums = Reduction(order, attention_kept, small)
        sums.cut(attention_far)
        out_half, ffn_own, *ffn_cuts = order.call(
            settle_kernel,
            [((span // 2, width), BF16), ((rows // 4, 2 * hidden), F32)]
            + [((rows // 4, hidden), BF16)] * 2,
            [ffn_near, sent_got],
        )
        ffn_turns = [order.swap_turn(piece, 1) for piece in ffn_cuts]
        sums.shards()
    in_low = order.call(
        add_pair_kernel, [((span, width), BF16)], [resid_grad, in_terms, in_got]
    )[0]
    if parts == 2:
        in_low, sums.got = hold(in_low, sums.got)
    in_far = order.swap(in_low, "tp", 2)
    vectors = [((1, hidden), F32), ((2, cols), F32)] + [((1, width), F32)] * 6
    large = [((2 * span, width), F32)] * 2
    if parts == 2:
        owned, passed = order.call(
            owned_kernel,
            [
                ((rows // 4, 2 * hidden + 4 * cols), BF16),
                ((span // 2 + 2 * small_rows, width), BF16),
            ],
            [ffn_own, *ffn_turns, sums.own, sums.sent, sums.got, out_half],
        )
        passed_got = order.swap(passed, "tp", 1)
        pieces = [owned] + order.swap_three(owned, "ctx")
        bits = near[1][rows : rows + 9 : 3, 2 * cols : 2 * cols + 2].astype(F32)
        far_steps = jnp.sum(bits, axis=0).astype(jnp.int32)
        steps = jnp.where(
            core == 0,
            jnp.concatenate([timesteps, far_steps]),
            jnp.concatenate([far_steps, timesteps]),
        )
        whole = [
            ((rows, hidden), F32), ((rows, hidden), F32), ((3, rows, cols), F32),
            ((rows, cols), F32),
        ]
        grads_up, grads_down, grads_qkv, grads_out = order.call(
            weights_kernel,
            whole,
            pieces,
            kept=range(4),
            scratch=[pltpu.VMEM(shape, dtype) for shape, dtype in whole] + [dma(4)],
        )
        output, grad_input, table, *rest = order.call(
            close_kernel,
            large + [(time_table.shape, F32)] + vectors,
            [steps, out_low, passed, passed_got, in_low, in_far, table],
            far=(6,),
            kept=range(3),
            alias={6: 2},
            scratch=[pltpu.VMEM((2 * span, width), F32)] * 2
            + [
                pltpu.VMEM((small_rows, width), F32), pltpu.VMEM((seqs, 8, width), F32),
                dma(2 + seqs),
            ],
        )
    else:
        output, grad_input = order.call(
            rows_kernel, large, [out_low, out_half, order.swap(out_half, "tp", 1), in_low, in_far]
        )
        ffn_sent = jnp.concatenate(ffn_sent, axis=1)
        both_grads = reduce_plainly(ffn_kept, ffn_sent, chunk)
        grads_up, grads_down = both_grads[:, :hidden], both_grads[:, hidden:]
        near_part, far_part, out_columns = [piece[:size] for piece in attention_sent]
        attention_sent = jnp.concatenate(
            [near_part, out_columns[:, :cols], far_part, out_columns[:, cols:]], axis=1
        )
        every = reduce_plainly(attention_kept, attention_sent, chunk)
        grads_qkv = jnp.stack([every[:, i * cols : (i + 1) * cols] for i in range(3)])
        grads_out = every[:, 3 * cols :]
        small = lax.psum(small, ("fsdp", "ctx", "tp"))
        steps = lax.all_gather(timesteps, "fsdp", axis=0, tiled=True)
        table, *rest = order.call(
            plain_sums_kernel, [(time_table.shape, F32)] + vectors, [steps, small]
        )
    up_line, qv_lines, *sums = rest
    sums = [values.reshape(-1) for values in sums]

    shape = layer_input.shape
    return (
        output.reshape(shape),
        grad_input.reshape(shape),
        table,
        sums[0],
        sums[1],
        grads_qkv,
        qv_lines,
        grads_out,
        sums[4],
        sums[2],
        sums[3],
        grads_up,
        up_line.reshape(-1),
        grads_down,
        sums[5],
    )


def solution(mesh):
    placed = (
        P("fsdp", "ctx", None),
        P("fsdp"),
        P("fsdp", None),
        P(),
        P(),
        P(),
        P(None, "fsdp", "tp"),
        P(None, "tp"),
        P("fsdp", "tp"),
        P(),
        P(),
        P(),
        P("fsdp", "tp"),
        P("tp"),
        P("fsdp", "tp"),
        P(),
        P("fsdp", "ctx", None),
    )
    return jax.shard_map(
        functools.partial(per_device, parts=mesh.shape["fsdp"]),
        mesh=mesh,
        in_specs=placed,
        out_specs=(
            P("fsdp", "ctx", None),
            P("fsdp", "ctx", None),
            P(),
            P(),
            P(),
            P(None, "fsdp", "tp"),
            P(None, "tp"),
            P("fsdp", "tp"),
            P(),
            P(),
            P(),
            P("fsdp", "tp"),
            P("tp"),
            P("fsdp", "tp"),
            P(),
        ),
        check_vma=False,
    )
```
